32 devices in a mesh: dp: 8 (over z, y), tensor: 4 (over x, core).
Axes of the slice: x: 2, y: 2, z: 4, core: 2. Of those that a mesh axis runs over, the one named last changes fastest.
Arguments:
- inputs: float32 [4096, 2048], P(('dp', 'tensor')), may hold values from -12 to 12
- grad_output: float32 [4096, 2048], P(('dp', 'tensor')), may hold values from -12 to 12
- seg_ids: int32 [4096], P('dp'), may hold values from 0 to 4, as said below
- positions: int32 [4096], P('dp'), may hold values from 0 to 319, as said below
- norm1_gain: float32 [2048], replicated, may hold values from 0.5 to 1.5
- norm1_bias: float32 [2048], replicated, may hold values from -1.75 to 1.75
- query_weight: float32 [2048, 2048], P('dp', 'tensor'), may hold values from -0.125 to 0.125
- query_bias: float32 [2048], P('tensor'), may hold values from -1.75 to 1.75
- key_weight: float32 [2048, 2048], P('dp', 'tensor'), may hold values from -0.125 to 0.125
- value_weight: float32 [2048, 2048], P('dp', 'tensor'), may hold values from -0.125 to 0.125
- value_bias: float32 [2048], P('tensor'), may hold values from -1.75 to 1.75
- out_weight: float32 [2048, 2048], P('tensor', 'dp'), may hold values from -0.5 to 0.5
- out_bias: float32 [2048], replicated, may hold values from -1.75 to 1.75
- norm2_gain: float32 [2048], replicated, may hold values from 0.5 to 1.5
- norm2_bias: float32 [2048], replicated, may hold values from -1.75 to 1.75
- up_weight: float32 [2048, 8192], P('dp', 'tensor'), may hold values from -0.125 to 0.125
- up_bias: float32 [8192], P('tensor'), may hold values from -1.75 to 1.75
- down_weight: float32 [8192, 2048], P('tensor', 'dp'), may hold values from -0.0625 to 0.0625
- down_bias: float32 [2048], replicated, may hold values from -1.75 to 1.75
Outputs:
- layer_output: float32 [4096, 2048], P(('dp', 'tensor'))
- grad_inputs: float32 [4096, 2048], P(('dp', 'tensor'))
- grad_norm1_gain: float32 [2048], replicated
- grad_norm1_bias: float32 [2048], replicated
- grad_query_weight: float32 [2048, 2048], P('dp', 'tensor')
- grad_query_bias: float32 [2048], P('tensor')
- grad_key_weight: float32 [2048, 2048], P('dp', 'tensor')
- grad_value_weight: float32 [2048, 2048], P('dp', 'tensor')
- grad_value_bias: float32 [2048], P('tensor')
- grad_out_weight: float32 [2048, 2048], P('tensor', 'dp')
- grad_out_bias: float32 [2048], replicated
- grad_norm2_gain: float32 [2048], replicated
- grad_norm2_bias: float32 [2048], replicated
- grad_up_weight: float32 [2048, 8192], P('dp', 'tensor')
- grad_up_bias: float32 [8192], P('tensor')
- grad_down_weight: float32 [8192, 2048], P('tensor', 'dp')
- grad_down_bias: float32 [2048], replicated
The draws below stay inside these ranges and needn't reach their ends.
Inputs may be any that keep to these rules, and one draw needn't show every extreme that they name: `seg_ids`: each group of 512 consecutive tokens holds one prompt (segment 0, positions 0 to 255) and 4 continuations (segments 1 to 4, positions 256 to 319 each); the tokens stand in blocks of 64 consecutive positions of one segment, the blocks of a group in an order drawn from the seed. `positions`: positions as stated for seg_ids; within a block they rise by one from token to token.
All inputs are finite; a program needn't handle non-finite values.
Results may differ from the reference program's by a relative error of at most 0.012.
Values may be sent and summed in bfloat16 or wider, within the bound.
A program may use at most 192 MiB of HBM per device.

```python
import jax
import jax.numpy as jnp
from jax import lax

D = 2048
HEADS = 16
FF = 8192
HEAD_DIM = 128
PROMPT = 256
CONT_LEN = 64
CONTS = 4
GROUP = 512
TOKENS = 4096


def group_layout(key):
    prompt_blocks = PROMPT // CONT_LEN
    block_total = prompt_blocks + CONTS
    group_total = TOKENS // GROUP
    group_keys = jax.random.split(jax.random.fold_in(key, 7), group_total)
    orders = jax.vmap(lambda one_key: jax.random.permutation(one_key, block_total))(group_keys)
    orders = orders.astype(jnp.int32)
    block_segment = jnp.where(orders < prompt_blocks, 0, orders - prompt_blocks + 1)
    block_first = jnp.where(orders < prompt_blocks, orders * CONT_LEN, PROMPT)
    offsets = jnp.arange(CONT_LEN, dtype=jnp.int32)
    segment = (block_segment[:, :, None] + 0 * offsets[None, None, :]).reshape(-1)
    places = (block_first[:, :, None] + offsets[None, None, :]).reshape(-1)
    return (segment.astype(jnp.int32), places.astype(jnp.int32))


def draw_seg_ids(key, part):
    segment, places = group_layout(key)
    return segment


def draw_positions(key, part):
    segment, places = group_layout(key)
    return places


def with_spikes(entries, rng, source, target, blocks, factor):
    def block_of(axis_at):
        return (jnp.arange(entries.shape[axis_at]) // (entries.shape[axis_at] // blocks)).reshape((-1,) + (1,) * (entries.ndim - 1 - axis_at))

    one_side = jax.random.permutation(rng, blocks)[block_of(target)]
    far = (block_of(target) + blocks // 2) % blocks
    return jnp.where((block_of(source) == one_side) | (block_of(source) == far), factor * entries, entries)


def shard_levels(stream_key, extent, cuts, least, high):
    def one(position, parts):
        heights = jax.random.uniform(jax.random.fold_in(jax.random.fold_in(stream_key, 6), position), (parts,), jnp.float32, least / len(cuts), high / len(cuts))
        return jnp.repeat(jnp.exp(heights), extent[position] // parts).reshape((-1,) + (1,) * (len(extent) - position - 1))

    loudness = one(*cuts[0])
    for cut in cuts[1:]:
        loudness = loudness * one(*cut)
    return loudness


def gaussian(key, dims, width, most, shards=(), kind=jnp.bfloat16):
    level = shard_levels(key, dims, shards, -0.22, 0.18) if shards else 1.0
    array = jax.random.normal(key, dims, jnp.float32) * width * level
    return jnp.minimum(jnp.maximum(array, -most), most).astype(kind)


def bell_draw_with(stream_key, dims, width, most, cuts, heavy, kind=jnp.bfloat16):
    values = width * jax.random.normal(stream_key, dims, jnp.float32)
    if cuts:
        values = values * shard_levels(stream_key, dims, cuts, -0.22, 0.18)
    return jnp.clip(with_spikes(values, jax.random.fold_in(stream_key, 3), *heavy), -most, most).astype(kind)


def setup_inputs(seed: int = 0) -> dict:
    key_of = jax.random.split(jax.random.key(seed), 20)
    inputs = bell_draw_with(key_of[0], (TOKENS, D), 1.0, 12.0, ((0, 32),), (0, 1, 32, 2.75), jnp.float32)
    grad_output = bell_draw_with(key_of[1], (TOKENS, D), 1.0, 12.0, ((0, 32),), (0, 1, 32, 2.75), jnp.float32)
    seg_ids = draw_seg_ids(jax.random.fold_in(key_of[19], 71), 0)
    positions = draw_positions(jax.random.fold_in(key_of[19], 71), 0)
    norm1_gain = jnp.clip(1.0 + 0.1 * jax.random.normal(key_of[4], (D,), jnp.float32), 0.5, 1.5)
    norm1_bias = gaussian(key_of[5], (D,), 0.3, 1.75, (), jnp.float32)
    query_weight = gaussian(key_of[6], (D, D), D ** -0.5, 0.125, ((0, 8), (1, 4)), jnp.float32)
    query_bias = gaussian(key_of[7], (D,), 0.3, 1.75, ((0, 4),), jnp.float32)
    key_weight = gaussian(key_of[8], (D, D), D ** -0.5, 0.125, ((0, 8), (1, 4)), jnp.float32)
    value_weight = gaussian(key_of[9], (D, D), D ** -0.5, 0.125, ((0, 8), (1, 4)), jnp.float32)
    value_bias = gaussian(key_of[10], (D,), 0.3, 1.75, ((0, 4),), jnp.float32)
    out_weight = gaussian(key_of[11], (D, D), (D // 16) ** -0.5, 0.5, ((0, 4), (1, 8)), jnp.float32)
    out_bias = gaussian(key_of[12], (D,), 0.3, 1.75, (), jnp.float32)
    norm2_gain = jnp.clip(1.0 + 0.1 * jax.random.normal(key_of[13], (D,), jnp.float32), 0.5, 1.5)
    norm2_bias = gaussian(key_of[14], (D,), 0.3, 1.75, (), jnp.float32)
    up_weight = gaussian(key_of[15], (D, FF), D ** -0.5, 0.125, ((0, 8), (1, 4)), jnp.float32)
    up_bias = gaussian(key_of[16], (FF,), 0.3, 1.75, ((0, 4),), jnp.float32)
    down_weight = gaussian(key_of[17], (FF, D), FF ** -0.5, 0.0625, ((0, 4), (1, 8)), jnp.float32)
    down_bias = gaussian(key_of[18], (D,), 0.3, 1.75, (), jnp.float32)
    return dict(inputs=inputs, grad_output=grad_output, seg_ids=seg_ids, positions=positions, norm1_gain=norm1_gain, norm1_bias=norm1_bias, query_weight=query_weight, query_bias=query_bias, key_weight=key_weight, value_weight=value_weight, value_bias=value_bias, out_weight=out_weight, out_bias=out_bias, norm2_gain=norm2_gain, norm2_bias=norm2_bias, up_weight=up_weight, up_bias=up_bias, down_weight=down_weight, down_bias=down_bias)


EPSILON = 1e-05
HIGHEST = lax.Precision.HIGHEST
NEGATIVE = -1e+30

@jax.custom_vjp
def low(v):
    return lax.optimization_barrier(v.astype(jnp.bfloat16)).astype(jnp.float32)

@jax.custom_vjp
def low_back(v):
    return v

def low_keep(v):
    return (low(v), None)

def low_pass(kept, grad):
    return (grad,)

def back_keep(v):
    return (v, None)

def back_low(kept, grad):
    return (low(grad),)
low.defvjp(low_keep, low_pass)
low_back.defvjp(back_keep, back_low)

def layer_norm(values, gain, shift):
    mean_row = lax.optimization_barrier(jnp.mean(values, axis=1, keepdims=True))
    centred = values - mean_row
    variance = lax.optimization_barrier(jnp.mean(centred * centred, axis=1, keepdims=True))
    return centred * lax.rsqrt(variance + EPSILON) * gain + shift

def matmul(left, right):
    return jnp.dot(left, right, precision=HIGHEST)

def group_attention(queries, keys, values, segment, places):
    scale_factor = HEAD_DIM ** (-0.5)
    scores = low_back(jnp.einsum('qhd,khd->hqk', queries, keys, precision=HIGHEST) * scale_factor)
    allowed = (places[None, :] <= places[:, None]) & ((segment[None, :] == segment[:, None]) | (segment[None, :] == 0))
    scores = jnp.where(allowed[None], scores, NEGATIVE)
    attn_probs = jax.nn.softmax(scores, axis=-1)
    return jnp.einsum('hqk,khd->qhd', low(attn_probs), values, precision=HIGHEST)

def forward(rows, norm1_gain, norm1_bias, query_weight, query_bias, key_weight, value_weight, value_bias, out_weight, out_bias, norm2_gain, norm2_bias, up_weight, up_bias, down_weight, down_bias, segment, places):
    row_count = rows.shape[0]
    normed1 = low(layer_norm(rows, norm1_gain, norm1_bias))
    queries = low(low_back(matmul(normed1, low(query_weight)) + query_bias))
    keys = low(low_back(matmul(normed1, low(key_weight))))
    values = low(low_back(matmul(normed1, low(value_weight)) + value_bias))
    attended = group_attention(queries.reshape(row_count, HEADS, HEAD_DIM), keys.reshape(row_count, HEADS, HEAD_DIM), values.reshape(row_count, HEADS, HEAD_DIM), segment, places)
    attended = low(low_back(attended.reshape(row_count, -1)))
    resid = rows + low_back(matmul(attended, low(out_weight))) + out_bias
    normed2 = low(layer_norm(resid, norm2_gain, norm2_bias))
    pre_act = low_back(matmul(normed2, low(up_weight)) + up_bias)
    activated = low(jax.nn.gelu(pre_act, approximate=False))
    return resid + low_back(matmul(activated, low(down_weight))) + down_bias

def reference(inputs, grad_output, seg_ids, positions, norm1_gain, norm1_bias, query_weight, query_bias, key_weight, value_weight, value_bias, out_weight, out_bias, norm2_gain, norm2_bias, up_weight, up_bias, down_weight, down_bias):
    group_total = inputs.shape[0] // GROUP
    params = (norm1_gain, norm1_bias, query_weight, query_bias, key_weight, value_weight, value_bias, out_weight, out_bias, norm2_gain, norm2_bias, up_weight, up_bias, down_weight, down_bias)

    def one_group(totals, pieces):
        rows, row_grads, segment, places = pieces

        def closed(rows_in, *weights):
            return forward(rows_in, *weights, segment, places)
        result_rows, pullback = jax.vjp(closed, rows, *params)
        grads = pullback(row_grads)
        new_totals = tuple((old + new for old, new in zip(totals, grads[1:])))
        return (new_totals, (result_rows, grads[0]))
    zero_totals = tuple((jnp.zeros_like(value) for value in params))
    totals, (result_rows, grad_rows) = lax.scan(one_group, zero_totals, (inputs.reshape(group_total, GROUP, -1), grad_output.reshape(group_total, GROUP, -1), seg_ids.reshape(group_total, GROUP), positions.reshape(group_total, GROUP)))
    g_n1g, g_n1b, g_qw, g_qb, g_kw, g_vw, g_vb, g_ow, g_ob, g_n2g, g_n2b, g_uw, g_ub, g_dw, g_db = totals
    return (result_rows.reshape(inputs.shape), grad_rows.reshape(inputs.shape), g_n1g, g_n1b, g_qw, g_qb, g_kw, g_vw, g_vb, g_ow, g_ob, g_n2g, g_n2b, g_uw, g_ub, g_dw, g_db)
```

```python
import jax
import jax.numpy as jnp
from jax import lax
from jax.sharding import PartitionSpec as P

HEAD_DIM = 128
GROUP = 512
EPSILON = 1e-05
NEGATIVE = -1e30
LOW = jnp.bfloat16
F32 = jnp.float32


def normalize(values, gain, shift):
    mean_row = jnp.mean(values, axis=1, keepdims=True)
    centred = values - mean_row
    inverse = lax.rsqrt(jnp.mean(centred * centred, axis=1, keepdims=True) + EPSILON)
    unit_rows = centred * inverse
    return (unit_rows * gain + shift, unit_rows, inverse)


def normalize_back(grad_rows, unit_rows, inverse, gain):
    scaled = grad_rows * gain
    grad_in = inverse * (
        scaled
        - jnp.mean(scaled, axis=1, keepdims=True)
        - unit_rows * jnp.mean(scaled * unit_rows, axis=1, keepdims=True)
    )
    return (grad_in, jnp.sum(grad_rows * unit_rows, axis=0), jnp.sum(grad_rows, axis=0))


def gelu_parts(pre_act):
    cumulative = 0.5 * (1.0 + lax.erf(pre_act * 0.7071067811865476))
    density = jnp.exp(-0.5 * pre_act * pre_act) * 0.3989422804014327
    return cumulative, cumulative + pre_act * density


def heads_of(rows):
    return rows.reshape(-1, GROUP, rows.shape[1] // HEAD_DIM, HEAD_DIM)


def scores_of(query_heads, key_heads, segment, places):
    scores = jnp.einsum(
        "gqhd,gkhd->ghqk", query_heads, key_heads, preferred_element_type=F32
    ) * (HEAD_DIM**-0.5)
    allowed = (places[:, None, :] <= places[:, :, None]) & (
        (segment[:, None, :] == segment[:, :, None]) | (segment[:, None, :] == 0)
    )
    return jnp.where(allowed[:, None], scores, NEGATIVE)


def attend(queries, keys, values, segment, places):
    scores = scores_of(heads_of(queries), heads_of(keys), segment, places)
    row_max = jnp.max(scores, axis=3, keepdims=True)
    exp_terms = jnp.exp(scores - row_max)
    exp_total = jnp.sum(exp_terms, axis=3, keepdims=True)
    probs = (exp_terms / exp_total).astype(LOW)
    mixed = jnp.einsum("ghqk,gkhd->gqhd", probs, heads_of(values), preferred_element_type=F32)
    return mixed.astype(LOW).reshape(queries.shape), row_max + jnp.log(exp_total)


def attend_back(queries, keys, values, grad_att, segment, places, log_totals):
    scale_factor = HEAD_DIM**-0.5
    query_heads, key_heads, value_heads, grad_heads = map(heads_of, (queries, keys, values, grad_att))
    probs = jnp.exp(scores_of(query_heads, key_heads, segment, places) - log_totals)
    grad_probs = jnp.einsum("gqhd,gkhd->ghqk", grad_heads, value_heads, preferred_element_type=F32)
    row_delta = jnp.sum(probs * grad_probs, axis=3, keepdims=True)
    grad_scores = (probs * (grad_probs - row_delta)).astype(LOW)
    grad_query = jnp.einsum("ghqk,gkhd->gqhd", grad_scores, key_heads, preferred_element_type=F32)
    grad_key = jnp.einsum("ghqk,gqhd->gkhd", grad_scores, query_heads, preferred_element_type=F32)
    grad_value = jnp.einsum(
        "ghqk,gqhd->gkhd", probs.astype(LOW), grad_heads, preferred_element_type=F32
    )
    return (
        (grad_query * scale_factor).astype(LOW).reshape(queries.shape),
        (grad_key * scale_factor).astype(LOW).reshape(queries.shape),
        grad_value.astype(LOW).reshape(queries.shape),
    )


def local(
    inputs,
    grad_output,
    seg_ids,
    positions,
    norm1_gain,
    norm1_bias,
    query_weight,
    query_bias,
    key_weight,
    value_weight,
    value_bias,
    out_weight,
    out_bias,
    norm2_gain,
    norm2_bias,
    up_weight,
    up_bias,
    down_weight,
    down_bias,
):
    dp_total = lax.axis_size("dp")
    half_total = dp_total // 2
    tensor_total = lax.axis_size("tensor")
    place = lax.axis_index("dp")
    lane, line = place & 1, place >> 1
    side = line & 1

    def hop(rows, mask):
        return lax.ppermute(rows, "dp", [(i, i ^ mask) for i in range(dp_total)])

    def hop_tensor(rows, mask):
        return lax.ppermute(rows, "tensor", [(i, i ^ mask) for i in range(tensor_total)])

    def own_half(array, axis):
        size = array.shape[axis] // 2
        return lax.dynamic_slice_in_dim(array, side * size, size, axis)

    def gather_weight(weight, axis):
        size = weight.shape[1 - axis] // 2
        low = weight.astype(LOW)
        mine = lax.dynamic_slice_in_dim(low, side * size, size, 1 - axis)
        other = lax.dynamic_slice_in_dim(low, (1 - side) * size, size, 1 - axis)
        along = [mine] + [hop(other if k & 1 else mine, 2 * k) for k in range(1, half_total)]
        across = [hop(mine, 1)] + [hop(block, 1) for block in along[1:]]
        shape = list(mine.shape)
        width = shape[axis]
        shape[axis] *= dp_total
        whole = jnp.zeros(tuple(shape), LOW)
        for k in range(half_total):
            for step, block in ((0, along[k]), (1, across[k])):
                start = [0, 0]
                start[axis] = (place ^ (2 * k + step)) * width
                whole = lax.dynamic_update_slice(whole, block, tuple(start))
        return whole

    def block_at(array, axis, index, width):
        return lax.dynamic_slice_in_dim(array, index * width, width, axis)

    def scatter_grad(partial, axis):
        width = partial.shape[axis] // dp_total
        send = jnp.concatenate(
            [block_at(partial, axis, 2 * k + 1 - lane, width) for k in range(half_total)], axis
        )
        got = hop(send, 1)

        def summed(index):
            return block_at(partial, axis, 2 * index + lane, width).astype(F32) + block_at(
                got, axis, index, width
            ).astype(F32)

        sums = [summed(line), None]
        for k in range(1, half_total):
            came = hop(summed(line ^ k).astype(LOW), 2 * k).astype(F32)
            sums[k & 1] = came if sums[k & 1] is None else sums[k & 1] + came
        first = jnp.where(side == 0, sums[0], sums[1])
        second = jnp.where(side == 0, sums[1], sums[0])
        return jnp.concatenate([first, second], 1 - axis)

    def gather_tokens(rows):
        pair = jnp.stack([rows, hop(rows, 2)])
        whole = lax.all_gather(pair, "tensor", axis=1, tiled=True)
        return whole.reshape(-1, rows.shape[1])

    def scatter_tokens(partial):
        pair = partial.astype(LOW).reshape(2, -1, partial.shape[1])
        mine = lax.psum_scatter(pair, "tensor", scatter_dimension=1, tiled=True)
        return mine[0].astype(F32) + hop(mine[1], 2).astype(F32)

    def mm(left, right):
        return jnp.dot(left, right, preferred_element_type=F32)

    def mm_nt(left, right):
        return jnp.einsum("td,fd->tf", left, right, preferred_element_type=F32)

    def mm_tn(left, right):
        return jnp.einsum("ta,tb->ab", left, right, preferred_element_type=F32)

    segment = jnp.stack([seg_ids, hop(seg_ids, 2)]).reshape(-1, GROUP)
    places = jnp.stack([positions, hop(positions, 2)]).reshape(-1, GROUP)

    normed1, unit1, inverse1 = normalize(inputs, norm1_gain, norm1_bias)
    whole1 = gather_tokens(normed1.astype(LOW))
    q_full = gather_weight(query_weight, 0)
    k_full = gather_weight(key_weight, 0)
    v_full = gather_weight(value_weight, 0)
    queries = (mm(whole1, q_full) + own_half(query_bias, 0)).astype(LOW)
    keys = mm(whole1, k_full).astype(LOW)
    values = (mm(whole1, v_full) + own_half(value_bias, 0)).astype(LOW)
    attended, log_totals = attend(queries, keys, values, segment, places)
    o_full = gather_weight(out_weight, 1)
    resid = inputs + scatter_tokens(mm(attended, o_full)) + out_bias
    normed2, unit2, inverse2 = normalize(resid, norm2_gain, norm2_bias)
    whole2 = gather_tokens(normed2.astype(LOW))
    up_full = gather_weight(up_weight, 0)
    pre_act = mm(whole2, up_full) + own_half(up_bias, 0)
    cumulative, slope = gelu_parts(pre_act)
    activated = (pre_act * cumulative).astype(LOW)
    grad_whole = gather_tokens(grad_output.astype(LOW))
    down_full = gather_weight(down_weight, 1)
    grad_down = scatter_grad(mm_tn(activated, grad_whole).astype(LOW), 1)
    layer_output = resid + scatter_tokens(mm(activated, down_full)) + down_bias
    grad_pre = (mm_nt(grad_whole, down_full) * slope).astype(LOW)
    grad_up_part = jnp.sum(grad_pre.astype(F32), axis=0)
    grad_up = scatter_grad(mm_tn(whole2, grad_pre).astype(LOW), 0)
    grad_normed2 = scatter_tokens(mm_nt(grad_pre, up_full))
    back2, gain2_part, bias2_part = normalize_back(grad_normed2, unit2, inverse2, norm2_gain)
    grad_resid = grad_output + back2
    grad_mixed = gather_tokens(grad_resid.astype(LOW))
    grad_out_w = scatter_grad(mm_tn(attended, grad_mixed).astype(LOW), 1)
    grad_att = mm_nt(grad_mixed, o_full).astype(LOW)
    grad_queries, grad_keys, grad_values = attend_back(
        queries, keys, values, grad_att, segment, places, log_totals
    )
    grad_value_w = scatter_grad(mm_tn(whole1, grad_values).astype(LOW), 0)
    grad_key_w = scatter_grad(mm_tn(whole1, grad_keys).astype(LOW), 0)
    grad_query_w = scatter_grad(mm_tn(whole1, grad_queries).astype(LOW), 0)
    grad_normed1 = scatter_tokens(
        mm_nt(grad_queries, q_full) + mm_nt(grad_keys, k_full) + mm_nt(grad_values, v_full)
    )
    back1, gain1_part, bias1_part = normalize_back(grad_normed1, unit1, inverse1, norm1_gain)
    grad_inputs = grad_resid + back1

    def sum_dp(vector):
        mask = 1
        while mask < dp_total:
            vector = vector + hop(vector, mask)
            mask *= 2
        return vector

    def sum_all(vector):
        vector = sum_dp(vector)
        mask = 1
        while mask < tensor_total:
            vector = vector + hop_tensor(vector, mask)
            mask *= 2
        return vector

    def spread(half):
        empty = jnp.zeros_like(half)
        return jnp.where(
            side == 0, jnp.concatenate([half, empty]), jnp.concatenate([empty, half])
        )

    width = inputs.shape[1]
    early = sum_all(
        jnp.stack(
            [
                jnp.sum(grad_output, axis=0),
                gain2_part,
                bias2_part,
                jnp.sum(grad_resid, axis=0),
            ]
        )
    )
    late = sum_all(jnp.stack([gain1_part, bias1_part]))
    up_sum = sum_dp(spread(grad_up_part))
    query_sum = sum_dp(spread(jnp.sum(grad_queries.astype(F32), axis=0)))
    value_sum = sum_dp(spread(jnp.sum(grad_values.astype(F32), axis=0)))
    return (
        layer_output,
        grad_inputs,
        late[0],
        late[1],
        grad_query_w,
        query_sum,
        grad_key_w,
        grad_value_w,
        value_sum,
        grad_out_w,
        early[3],
        early[1],
        early[2],
        grad_up,
        up_sum,
        grad_down,
        early[0],
    )


def solution(mesh):
    tokens, weight, weight_t = P(("dp", "tensor"), None), P("dp", "tensor"), P("tensor", "dp")
    whole, part = P(), P("tensor")
    return jax.shard_map(
        local,
        mesh=mesh,
        in_specs=(
            tokens, tokens, P("dp"), P("dp"), whole, whole, weight, part, weight, weight, part,
            weight_t, whole, whole, whole, weight, part, weight_t, whole,
        ),
        out_specs=(
            tokens, tokens, whole, whole, weight, part, weight, weight, part, weight_t, whole,
            whole, whole, weight, part, weight_t, whole,
        ),
        check_vma=False,
    )
```

```python
import jax
import jax.numpy as jnp
from jax import lax
from jax.experimental import pallas as pl
from jax.experimental.pallas import tpu as pltpu
from jax.sharding import PartitionSpec as P

HEAD_DIM = 128
GROUP = 512
EPSILON = 1e-05
NEGATIVE = -1e30
LOW = jnp.bfloat16
F32 = jnp.float32


def gelu_parts(pre_act):
    cumulative = 0.5 * (1.0 + lax.erf(pre_act * 0.7071067811865476))
    density = jnp.exp(-0.5 * pre_act * pre_act) * 0.3989422804014327
    return cumulative, cumulative + pre_act * density


def heads_of(rows):
    return rows.reshape(-1, GROUP, rows.shape[1] // HEAD_DIM, HEAD_DIM)


def scores_of(query_heads, key_heads, segment, places):
    scores = jnp.einsum(
        "gqhd,gkhd->ghqk", query_heads, key_heads, preferred_element_type=F32
    ) * (HEAD_DIM**-0.5)
    allowed = (places[:, None, :] <= places[:, :, None]) & (
        (segment[:, None, :] == segment[:, :, None]) | (segment[:, None, :] == 0)
    )
    return jnp.where(allowed[:, None], scores, NEGATIVE)


def attend(queries, keys, values, segment, places):
    scores = scores_of(heads_of(queries), heads_of(keys), segment, places)
    row_max = jnp.max(scores, axis=3, keepdims=True)
    exp_terms = jnp.exp(scores - row_max)
    exp_total = jnp.sum(exp_terms, axis=3, keepdims=True)
    probs = (exp_terms / exp_total).astype(LOW)
    mixed = jnp.einsum("ghqk,gkhd->gqhd", probs, heads_of(values), preferred_element_type=F32)
    return mixed.astype(LOW).reshape(queries.shape), row_max + jnp.log(exp_total)


def attend_back(queries, keys, values, grad_att, segment, places, log_totals):
    scale_factor = HEAD_DIM**-0.5
    query_heads, key_heads, value_heads, grad_heads = map(heads_of, (queries, keys, values, grad_att))
    probs = jnp.exp(scores_of(query_heads, key_heads, segment, places) - log_totals)
    grad_probs = jnp.einsum("gqhd,gkhd->ghqk", grad_heads, value_heads, preferred_element_type=F32)
    row_delta = jnp.sum(probs * grad_probs, axis=3, keepdims=True)
    grad_scores = (probs * (grad_probs - row_delta)).astype(LOW)
    grad_query = jnp.einsum("ghqk,gkhd->gqhd", grad_scores, key_heads, preferred_element_type=F32)
    grad_key = jnp.einsum("ghqk,gqhd->gkhd", grad_scores, query_heads, preferred_element_type=F32)
    grad_value = jnp.einsum(
        "ghqk,gqhd->gkhd", probs.astype(LOW), grad_heads, preferred_element_type=F32
    )
    return (
        (grad_query * scale_factor).astype(LOW).reshape(queries.shape),
        (grad_key * scale_factor).astype(LOW).reshape(queries.shape),
        grad_value.astype(LOW).reshape(queries.shape),
    )


NC = 4
MESH = pl.DeviceIdType.MESH


class Place:
    def __init__(self):
        self.d = lax.axis_index("dp")
        self.t = lax.axis_index("tensor")
        self.c = lax.rem(self.t, 2)
        self.t_core = self.t + 1 - 2 * self.c
        self.t_x = lax.rem(self.t + 2, 4)
        self.t_far = lax.rem(self.t_core + 2, 4)
        self.d_y = self.d + 1 - 2 * lax.rem(self.d, 2)
        self.d_z = self.d + 2 - 4 * lax.rem(lax.div(self.d, 2), 2)
        c = self.c
        self.first = (self.d + c * (self.d_z - self.d), self.t_x + c * (self.t - self.t_x))
        self.second = (self.d_z + c * (self.d - self.d_z), self.t + c * (self.t_x - self.t))
        self.core = (self.d, self.t_core)
        self.x = (self.d, self.t_x)
        self.z = (self.d_z, self.t)


def greet(peers):
    barrier = pltpu.get_barrier_semaphore()
    for peer in peers:
        pl.semaphore_signal(barrier, inc=1, device_id=peer, device_id_type=MESH)
    pl.semaphore_wait(barrier, len(peers))


def remote(src, dst, send, recv, peer):
    return pltpu.make_async_remote_copy(
        src_ref=src, dst_ref=dst, send_sem=send, recv_sem=recv, device_id=peer, device_id_type=MESH
    )


class Gather:
    SEMS = [pltpu.SemaphoreType.DMA((7, NC)), pltpu.SemaphoreType.DMA((7, NC)), pltpu.SemaphoreType.DMA((NC,))]

    def __init__(self, me, own, whole, send, recv, keep):
        self.me, self.own, self.whole = me, own, whole
        self.send, self.recv, self.keep = send, recv, keep
        self.rows = own.shape[0] // NC

    def at(self, side, t, j):
        return self.whole.at[side, t, pl.ds(j * self.rows, self.rows)]

    def piece(self, j):
        return self.own.at[pl.ds(j * self.rows, self.rows)]

    def copy(self, kind, j, src, dst, peer):
        return remote(src, dst, self.send.at[kind, j], self.recv.at[kind, j], peer)

    def own_copies(self, j):
        me = self.me
        return [
            self.copy(2, j, self.piece(j), self.at(1, me.t, j), me.z),
            self.copy(1, j, self.piece(j), self.at(0, me.t, j), me.x),
            self.copy(0, j, self.piece(j), self.at(0, me.t, j), me.core),
            pltpu.make_async_copy(self.piece(j), self.at(0, me.t, j), self.keep.at[j]),
        ]

    def start(self, j):
        for copy in self.own_copies(j):
            copy.start()

    def wait_recv(self, kind, j, side, t):
        slot = self.at(side, t, j)
        self.copy(kind, j, slot, slot, self.me.core).wait_recv()

    def relay(self, kind, j, side, t):
        slot = self.at(side, t, j)
        self.copy(kind + 3, j, slot, slot, self.me.core).start()

    def finish(self):
        me, c = self.me, self.me.c

        @pl.loop(0, NC)
        def _(j):
            side, t = 1 - c, me.t + c * (me.t_x - me.t)
            self.wait_recv(2 - c, j, side, t)
            slot = self.at(side, t, j)
            self.copy(3, j, slot, self.at(1, t, j), me.first).start()
            self.relay(2 - c, j, side, t)
            side, t = c, me.t_x + c * (me.t - me.t_x)
            self.wait_recv(1 + c, j, side, t)
            self.relay(1 + c, j, side, t)

        @pl.loop(0, NC)
        def _(j):
            self.wait_recv(3, j, 1, me.t_x)
            self.relay(3, j, 1, me.t_x)

        @pl.loop(0, NC)
        def _(j):
            self.wait_recv(0, j, 0, me.t_core)
            self.wait_recv(4, j, 0, me.t_far)
            self.wait_recv(5, j, 1, me.t_core)
            self.wait_recv(6, j, 1, me.t_far)
            for copy in self.own_copies(j)[:3]:
                copy.wait_send()
            self.own_copies(j)[3].wait()
            for kind in (3, 4, 5, 6):
                slot = self.at(0, me.t, j)
                self.copy(kind, j, slot, slot, me.core).wait_send()


class Scatter:
    SEMS = [
        pltpu.SemaphoreType.DMA((4, NC)),
        pltpu.SemaphoreType.DMA((4, NC)),
        pltpu.SemaphoreType.DMA((4, NC)),
        pltpu.SemaphoreType.DMA((3, NC)),
        pltpu.SemaphoreType.DMA((3, NC)),
    ]

    @staticmethod
    def buffers(rows, width):
        return [
            pltpu.VMEM((4, rows, width), LOW),
            pltpu.VMEM((4, rows, width), LOW),
            pltpu.VMEM((3, rows, width), LOW),
        ]

    def __init__(self, me, parts, held, came, hops, load, send, recv, hop_send, hop_recv):
        self.me, self.parts = me, parts
        self.held, self.came, self.hops = held, came, hops
        self.load, self.send, self.recv = load, send, recv
        self.hop_send, self.hop_recv = hop_send, hop_recv
        self.rows = held.shape[1] // NC

    def span(self, j):
        return pl.ds(j * self.rows, self.rows)

    def pairs(self):
        me = self.me
        return [(0, me.t, me.t_core), (0, me.t_x, me.t_far), (1, me.t, me.t_core), (1, me.t_x, me.t_far)]

    def core_copy(self, i, j):
        side, _, theirs = self.pairs()[i]
        return remote(
            self.parts.at[side, theirs, self.span(j)],
            self.came.at[i, self.span(j)],
            self.send.at[i, j],
            self.recv.at[i, j],
            self.me.core,
        )

    def load_copy(self, i, j):
        side, mine, _ = self.pairs()[i]
        return pltpu.make_async_copy(
            self.parts.at[side, mine, self.span(j)], self.held.at[i, self.span(j)], self.load.at[i, j]
        )

    def hop(self, kind, j, src, peer):
        return remote(
            src, self.hops.at[kind, self.span(j)], self.hop_send.at[kind, j], self.hop_recv.at[kind, j], peer
        )

    def start(self):
        for i in (3, 1, 2, 0):

            @pl.loop(0, NC)
            def _(j):
                self.core_copy(i, j).start()
                self.load_copy(i, j).start()

    def joined(self, i, j):
        held, came = self.held.at[i, self.span(j)], self.came.at[i, self.span(j)]
        pltpu.make_async_copy(held, held, self.load.at[i, j]).wait()
        remote(came, came, self.send.at[i, j], self.recv.at[i, j], self.me.core).wait_recv()
        return held[...].astype(F32) + came[...].astype(F32)

    def spread(self):
        me, c = self.me, self.me.c
        straight, turn = 1 + c, 2 - c

        @pl.loop(0, NC)
        def _(j):
            self.held[3, self.span(j)] = self.joined(3, j).astype(LOW)
            self.hop(0, j, self.held.at[3, self.span(j)], me.first).start()

        @pl.loop(0, NC)
        def _(j):
            self.held[straight, self.span(j)] = self.joined(straight, j).astype(LOW)
            self.hop(1, j, self.held.at[straight, self.span(j)], me.first).start()

        @pl.loop(0, NC)
        def _(j):
            total = self.joined(turn, j)
            arrived = self.hops.at[0, self.span(j)]
            self.hop(0, j, arrived, me.first).wait_recv()
            self.held[turn, self.span(j)] = (total + arrived[...].astype(F32)).astype(LOW)
            self.hop(2, j, self.held.at[turn, self.span(j)], me.second).start()

    def result(self, j):
        total = self.joined(0, j)
        for kind in (1, 2):
            arrived = self.hops.at[kind, self.span(j)]
            self.hop(kind, j, arrived, self.me.first).wait_recv()
            total = total + arrived[...].astype(F32)
        return total

    def finish(self):
        @pl.loop(0, NC)
        def _(j):
            for i in range(4):
                self.core_copy(i, j).wait_send()
            for kind in range(3):
                self.hop(kind, j, self.hops.at[kind, self.span(j)], self.me.first).wait_send()


def unit_of(rows):
    centred = rows - jnp.mean(rows, axis=1, keepdims=True)
    inverse = lax.rsqrt(jnp.mean(centred * centred, axis=1, keepdims=True) + EPSILON)
    return centred * inverse, inverse


def back_of(grad_rows, unit_rows, inverse, gain):
    scaled = grad_rows * gain
    return inverse * (
        scaled
        - jnp.mean(scaled, axis=1, keepdims=True)
        - unit_rows * jnp.mean(scaled * unit_rows, axis=1, keepdims=True)
    )


def pieces(rows):
    size = rows // NC
    return lambda j: pl.ds(j * size, size)


def head_kernel(x, gain, shift, grad, whole, whole_grad, own, own_grad, *sems):
    me = Place()
    at = pieces(x.shape[0])
    gather = Gather(me, own, whole, *sems[:3])
    gather_grad = Gather(me, own_grad, whole_grad, *sems[3:])
    greet([me.core, me.x, me.z])

    @pl.loop(0, NC)
    def _(j):
        unit_rows, _ = unit_of(x[at(j)])
        own[at(j)] = (unit_rows * gain[...] + shift[...]).astype(LOW)
        gather.start(j)

    gather.finish()

    @pl.loop(0, NC)
    def _(j):
        own_grad[at(j)] = grad[at(j)].astype(LOW)
        gather_grad.start(j)

    gather_grad.finish()


def middle_kernel(parts, base, gain, shift, resid, whole, own, *scratch):
    me = Place()
    at = pieces(base.shape[0])
    scatter = Scatter(me, parts, *scratch[:8])
    gather = Gather(me, own, whole, *scratch[8:])
    greet([me.core, me.x, me.z])
    scatter.start()
    scatter.spread()

    @pl.loop(0, NC)
    def _(j):
        rows = base[at(j)] + scatter.result(j)
        resid[at(j)] = rows
        unit_rows, _ = unit_of(rows)
        own[at(j)] = (unit_rows * gain[...] + shift[...]).astype(LOW)
        gather.start(j)

    gather.finish()
    scatter.finish()


def turn_kernel(parts, resid, grad, gain, grad_resid, whole, sums, own, *scratch):
    me = Place()
    at = pieces(resid.shape[0])
    scatter = Scatter(me, parts, *scratch[:8])
    gather = Gather(me, own, whole, *scratch[8:])
    greet([me.core, me.x, me.z])
    scatter.start()
    scatter.spread()
    sums[...] = jnp.zeros_like(sums)

    @pl.loop(0, NC)
    def _(j):
        unit_rows, inverse = unit_of(resid[at(j)])
        e = scatter.result(j)
        rows = grad[at(j)] + back_of(e, unit_rows, inverse, gain[...])
        grad_resid[at(j)] = rows
        own[at(j)] = rows.astype(LOW)
        gather.start(j)
        sums[0:1] += jnp.sum(e * unit_rows, axis=0, keepdims=True)
        sums[1:2] += jnp.sum(e, axis=0, keepdims=True)
        sums[2:3] += jnp.sum(rows, axis=0, keepdims=True)

    gather.finish()
    scatter.finish()


def tail_kernel(parts, lowered, x, gain, grad_resid, base, grad_inputs, output, sums, *scratch):
    me = Place()
    at = pieces(x.shape[0])
    scatter = Scatter(me, parts, *scratch[:8])
    other = Scatter(me, lowered, *scratch[8:])
    greet([me.core, me.x, me.z])
    scatter.start()
    scatter.spread()
    other.start()
    sums[...] = jnp.zeros_like(sums)

    @pl.loop(0, NC)
    def _(j):
        unit_rows, inverse = unit_of(x[at(j)])
        e = scatter.result(j)
        grad_inputs[at(j)] = grad_resid[at(j)] + back_of(e, unit_rows, inverse, gain[...])
        sums[0:1] += jnp.sum(e * unit_rows, axis=0, keepdims=True)
        sums[1:2] += jnp.sum(e, axis=0, keepdims=True)

    scatter.finish()
    other.spread()

    @pl.loop(0, NC)
    def _(j):
        output[at(j)] = base[at(j)] + other.result(j)

    other.finish()


VMEM = pl.BlockSpec(memory_space=pltpu.VMEM)
ANY = pl.BlockSpec(memory_space=pl.ANY)


def call(kernel, number, ins, in_specs, outs, out_specs, scratch):
    return pl.pallas_call(
        kernel,
        out_shape=outs,
        in_specs=in_specs,
        out_specs=out_specs,
        scratch_shapes=scratch,
        compiler_params=pltpu.CompilerParams(
            collective_id=number, has_side_effects=True, vmem_limit_bytes=40 << 20
        ),
        cost_estimate=pl.CostEstimate(flops=0, bytes_accessed=100_000_000, transcendentals=0),
    )(*ins)


def like(*shape, dtype=F32):
    return jax.ShapeDtypeStruct(shape, dtype)


def local(
    inputs,
    grad_output,
    seg_ids,
    positions,
    norm1_gain,
    norm1_bias,
    query_weight,
    query_bias,
    key_weight,
    value_weight,
    value_bias,
    out_weight,
    out_bias,
    norm2_gain,
    norm2_bias,
    up_weight,
    up_bias,
    down_weight,
    down_bias,
):
    dp_total = lax.axis_size("dp")
    half_total = dp_total // 2
    tensor_total = lax.axis_size("tensor")
    place = lax.axis_index("dp")
    lane, line = place & 1, place >> 1
    side = line & 1

    def hop(rows, mask):
        return lax.ppermute(rows, "dp", [(i, i ^ mask) for i in range(dp_total)])

    def hop_tensor(rows, mask):
        return lax.ppermute(rows, "tensor", [(i, i ^ mask) for i in range(tensor_total)])

    def own_half(array, axis):
        size = array.shape[axis] // 2
        return lax.dynamic_slice_in_dim(array, side * size, size, axis)

    def gather_weight(weight, axis):
        size = weight.shape[1 - axis] // 2
        low = weight.astype(LOW)
        mine = lax.dynamic_slice_in_dim(low, side * size, size, 1 - axis)
        other = lax.dynamic_slice_in_dim(low, (1 - side) * size, size, 1 - axis)
        along = [mine] + [hop(other if k & 1 else mine, 2 * k) for k in range(1, half_total)]
        across = [hop(mine, 1)] + [hop(block, 1) for block in along[1:]]
        shape = list(mine.shape)
        width = shape[axis]
        shape[axis] *= dp_total
        whole = jnp.zeros(tuple(shape), LOW)
        for k in range(half_total):
            for step, block in ((0, along[k]), (1, across[k])):
                start = [0, 0]
                start[axis] = (place ^ (2 * k + step)) * width
                whole = lax.dynamic_update_slice(whole, block, tuple(start))
        return whole

    def block_at(array, axis, index, width):
        return lax.dynamic_slice_in_dim(array, index * width, width, axis)

    def scatter_grad(partial, axis):
        width = partial.shape[axis] // dp_total
        send = jnp.concatenate(
            [block_at(partial, axis, 2 * k + 1 - lane, width) for k in range(half_total)], axis
        )
        got = hop(send, 1)

        def summed(index):
            return block_at(partial, axis, 2 * index + lane, width).astype(F32) + block_at(
                got, axis, index, width
            ).astype(F32)

        sums = [summed(line), None]
        for k in range(1, half_total):
            came = hop(summed(line ^ k).astype(LOW), 2 * k).astype(F32)
            sums[k & 1] = came if sums[k & 1] is None else sums[k & 1] + came
        first = jnp.where(side == 0, sums[0], sums[1])
        second = jnp.where(side == 0, sums[1], sums[0])
        return jnp.concatenate([first, second], 1 - axis)

    def mm(left, right):
        return jnp.dot(left, right, preferred_element_type=F32)

    def mm_nt(left, right):
        return jnp.einsum("td,fd->tf", left, right, preferred_element_type=F32)

    def mm_tn(left, right):
        return jnp.einsum("ta,tb->ab", left, right, preferred_element_type=F32)

    rows, width = inputs.shape
    row = lambda vector: vector.reshape(1, -1)
    group = like(2, tensor_total, rows, width, dtype=LOW)
    own = pltpu.VMEM((rows, width), LOW)
    spread_scratch = Scatter.buffers(rows, width) + Scatter.SEMS

    segment = jnp.stack([seg_ids, hop(seg_ids, 2)]).reshape(-1, GROUP)
    places = jnp.stack([positions, hop(positions, 2)]).reshape(-1, GROUP)

    whole1, grad_whole = call(
        head_kernel, 1,
        (inputs, row(norm1_gain), row(norm1_bias), grad_output), [VMEM] * 4,
        (group, group), (ANY, ANY),
        [own, own] + Gather.SEMS * 2,
    )
    whole1, grad_whole = whole1.reshape(-1, width), grad_whole.reshape(-1, width)
    halves = query_bias.shape[0] // 2
    qkv_weight = jnp.stack([query_weight, key_weight, value_weight], 1).astype(LOW)
    qkv_full = gather_weight(
        jnp.concatenate([qkv_weight[..., :halves].reshape(-1, 3 * halves), qkv_weight[..., halves:].reshape(-1, 3 * halves)], 1), 0
    )
    qkv = mm(whole1, qkv_full)
    queries = (qkv[:, :halves] + own_half(query_bias, 0)).astype(LOW)
    keys = qkv[:, halves : 2 * halves].astype(LOW)
    values = (qkv[:, 2 * halves :] + own_half(value_bias, 0)).astype(LOW)
    attended, log_totals = attend(queries, keys, values, segment, places)
    o_full = gather_weight(out_weight, 1)

    def as_group(partial):
        return partial.astype(LOW).reshape(group.shape)

    resid, whole2 = call(
        middle_kernel, 2,
        (as_group(mm(attended, o_full)), inputs + out_bias, row(norm2_gain), row(norm2_bias)), [ANY] + [VMEM] * 3,
        (like(rows, width), group), (VMEM, ANY),
        [own] + spread_scratch + Gather.SEMS,
    )
    whole2 = whole2.reshape(-1, width)
    up_full = gather_weight(up_weight, 0)
    pre_act = mm(whole2, up_full) + own_half(up_bias, 0)
    cumulative, slope = gelu_parts(pre_act)
    activated = (pre_act * cumulative).astype(LOW)
    down_full = gather_weight(down_weight, 1)
    grad_down = scatter_grad(mm_tn(activated, grad_whole).astype(LOW), 1)
    lowered = as_group(mm(activated, down_full))
    grad_pre = (mm_nt(grad_whole, down_full) * slope).astype(LOW)
    grad_up_part = jnp.sum(grad_pre.astype(F32), axis=0)
    grad_up = scatter_grad(mm_tn(whole2, grad_pre).astype(LOW), 0)
    grad_resid, grad_mixed, sums2 = call(
        turn_kernel, 3,
        (as_group(mm_nt(grad_pre, up_full)), resid, grad_output, row(norm2_gain)), [ANY] + [VMEM] * 3,
        (like(rows, width), group, like(8, width)), (VMEM, ANY, VMEM),
        [own] + spread_scratch + Gather.SEMS,
    )
    grad_mixed = grad_mixed.reshape(-1, width)
    grad_out_w = scatter_grad(mm_tn(attended, grad_mixed).astype(LOW), 1)
    grad_att = mm_nt(grad_mixed, o_full).astype(LOW)
    grad_queries, grad_keys, grad_values = attend_back(
        queries, keys, values, grad_att, segment, places, log_totals
    )
    grad_qkv = jnp.concatenate([grad_queries, grad_keys, grad_values], 1)
    grad_qkv_w = scatter_grad(mm_tn(whole1, grad_qkv).astype(LOW), 0)
    grad_qkv_w = grad_qkv_w.reshape(-1, 2, 3, halves).transpose(2, 0, 1, 3).reshape(3, -1, 2 * halves)
    grad_inputs, layer_output, sums1 = call(
        tail_kernel, 4,
        (as_group(mm_nt(grad_qkv, qkv_full)), lowered, inputs, row(norm1_gain), grad_resid, resid + down_bias), [ANY] * 2 + [VMEM] * 4,
        (like(rows, width), like(rows, width), like(8, width)), (VMEM,) * 3,
        spread_scratch * 2,
    )

    def sum_dp(vector):
        mask = 1
        while mask < dp_total:
            vector = vector + hop(vector, mask)
            mask *= 2
        return vector

    def sum_all(vector):
        vector = sum_dp(vector)
        mask = 1
        while mask < tensor_total:
            vector = vector + hop_tensor(vector, mask)
            mask *= 2
        return vector

    def spread(half):
        empty = jnp.zeros_like(half)
        return jnp.where(
            side == 0, jnp.concatenate([half, empty]), jnp.concatenate([empty, half])
        )

    early = sum_all(
        jnp.stack(
            [
                jnp.sum(grad_output, axis=0),
                sums2[0],
                sums2[1],
                sums2[2],
            ]
        )
    )
    late = sum_all(sums1[:2])
    up_sum = sum_dp(spread(grad_up_part))
    query_sum = sum_dp(spread(jnp.sum(grad_queries.astype(F32), axis=0)))
    value_sum = sum_dp(spread(jnp.sum(grad_values.astype(F32), axis=0)))
    return (
        layer_output,
        grad_inputs,
        late[0],
        late[1],
        grad_qkv_w[0],
        query_sum,
        grad_qkv_w[1],
        grad_qkv_w[2],
        value_sum,
        grad_out_w,
        early[3],
        early[1],
        early[2],
        grad_up,
        up_sum,
        grad_down,
        early[0],
    )


def solution(mesh):
    tokens, weight, weight_t = P(("dp", "tensor"), None), P("dp", "tensor"), P("tensor", "dp")
    whole, part = P(), P("tensor")
    return jax.shard_map(
        local,
        mesh=mesh,
        in_specs=(
            tokens, tokens, P("dp"), P("dp"), whole, whole, weight, part, weight, weight, part,
            weight_t, whole, whole, whole, weight, part, weight_t, whole,
        ),
        out_specs=(
            tokens, tokens, whole, whole, weight, part, weight, weight, part, weight_t, whole,
            whole, whole, weight, part, weight_t, whole,
        ),
        check_vma=False,
    )
```

```python
import functools

import jax
import jax.numpy as jnp
from jax import lax
from jax.experimental import pallas as pl
from jax.experimental.pallas import tpu as pltpu
from jax.sharding import PartitionSpec as P

HEAD_DIM = 128
GROUP = 512
EPSILON = 1e-05
NEGATIVE = -1e30
LOW = jnp.bfloat16
F32 = jnp.float32


def gelu_parts(pre_act):
    cumulative = 0.5 * (1.0 + lax.erf(pre_act * 0.7071067811865476))
    density = jnp.exp(-0.5 * pre_act * pre_act) * 0.3989422804014327
    return cumulative, cumulative + pre_act * density


def heads_of(rows):
    return rows.reshape(-1, GROUP, rows.shape[1] // HEAD_DIM, HEAD_DIM)


def scores_of(query_heads, key_heads, segment, places):
    scores = jnp.einsum(
        "gqhd,gkhd->ghqk", query_heads, key_heads, preferred_element_type=F32
    ) * (HEAD_DIM**-0.5)
    allowed = (places[:, None, :] <= places[:, :, None]) & (
        (segment[:, None, :] == segment[:, :, None]) | (segment[:, None, :] == 0)
    )
    return jnp.where(allowed[:, None], scores, NEGATIVE)


def attend(queries, keys, values, segment, places):
    scores = scores_of(heads_of(queries), heads_of(keys), segment, places)
    row_max = jnp.max(scores, axis=3, keepdims=True)
    exp_terms = jnp.exp(scores - row_max)
    exp_total = jnp.sum(exp_terms, axis=3, keepdims=True)
    probs = (exp_terms / exp_total).astype(LOW)
    mixed = jnp.einsum("ghqk,gkhd->gqhd", probs, heads_of(values), preferred_element_type=F32)
    return mixed.astype(LOW).reshape(queries.shape), row_max + jnp.log(exp_total)


def attend_back(queries, keys, values, grad_att, segment, places, log_totals):
    scale_factor = HEAD_DIM**-0.5
    query_heads, key_heads, value_heads, grad_heads = map(heads_of, (queries, keys, values, grad_att))
    probs = jnp.exp(scores_of(query_heads, key_heads, segment, places) - log_totals)
    grad_probs = jnp.einsum("gqhd,gkhd->ghqk", grad_heads, value_heads, preferred_element_type=F32)
    row_delta = jnp.sum(probs * grad_probs, axis=3, keepdims=True)
    grad_scores = (probs * (grad_probs - row_delta)).astype(LOW)
    grad_query = jnp.einsum("ghqk,gkhd->gqhd", grad_scores, key_heads, preferred_element_type=F32)
    grad_key = jnp.einsum("ghqk,gqhd->gkhd", grad_scores, query_heads, preferred_element_type=F32)
    grad_value = jnp.einsum(
        "ghqk,gqhd->gkhd", probs.astype(LOW), grad_heads, preferred_element_type=F32
    )
    return (
        (grad_query * scale_factor).astype(LOW).reshape(queries.shape),
        (grad_key * scale_factor).astype(LOW).reshape(queries.shape),
        grad_value.astype(LOW).reshape(queries.shape),
    )


NC = 4
NW = 2
MESH = pl.DeviceIdType.MESH


def remote(src, dst, send, recv, peer):
    return pltpu.make_async_remote_copy(
        src_ref=src, dst_ref=dst, send_sem=send, recv_sem=recv, device_id=peer, device_id_type=MESH
    )


def grid_of(*shape):
    return pltpu.SemaphoreType.DMA(shape)


class Place:
    def __init__(self, dp_total):
        self.lines = dp_total // 2
        self.d = lax.axis_index("dp")
        self.t = lax.axis_index("tensor")
        self.lane, self.line = lax.rem(self.d, 2), lax.div(self.d, 2)
        self.side = lax.rem(self.line, 2)
        self.t_core = self.t + 1 - 2 * lax.rem(self.t, 2)
        self.t_x = lax.rem(self.t + 2, 4)
        self.t_far = lax.rem(self.t_core + 2, 4)
        self.core = (self.d, self.t_core)
        self.x = (self.d, self.t_x)
        self.y = (self.d + 1 - 2 * self.lane, self.t)
        self.z = (self.d + 2 - 4 * self.side, self.t)

    def ahead(self, k):
        return lax.rem(self.line + k, self.lines)

    def behind(self, k):
        return lax.rem(self.line + self.lines - k, self.lines)

    def mate(self, line):
        return (2 * line + self.lane, self.t)

    def greet(self):
        barrier = pltpu.get_barrier_semaphore()
        for peer in (self.core, self.x, self.y):
            pl.semaphore_signal(barrier, inc=1, device_id=peer, device_id_type=MESH)

        @pl.loop(1, self.lines)
        def _(k):
            pl.semaphore_signal(barrier, inc=1, device_id=self.mate(self.ahead(k)), device_id_type=MESH)

        pl.semaphore_wait(barrier, 2 + self.lines)


class Gather:
    SEMS = [grid_of(7, NC), grid_of(7, NC), grid_of(NC)]

    def __init__(self, me, own, whole, send, recv, keep):
        self.me, self.own, self.whole = me, own, whole
        self.send, self.recv, self.keep = send, recv, keep
        self.rows = own.shape[0] // NC

    def at(self, side, t, j):
        return self.whole.at[side, t, pl.ds(j * self.rows, self.rows)]

    def piece(self, j):
        return self.own.at[pl.ds(j * self.rows, self.rows)]

    def copy(self, kind, j, src, dst, peer):
        return remote(src, dst, self.send.at[kind, j], self.recv.at[kind, j], peer)

    def local(self, j):
        return pltpu.make_async_copy(self.piece(j), self.at(0, self.me.t, j), self.keep.at[j])

    def start(self, j):
        me = self.me
        self.copy(2, j, self.piece(j), self.at(1, me.t, j), me.z).start()
        self.copy(1, j, self.piece(j), self.at(0, me.t, j), me.x).start()
        self.copy(0, j, self.piece(j), self.at(0, me.t, j), me.core).start()
        self.local(j).start()

    def wait_recv(self, kind, j, side, t):
        slot = self.at(side, t, j)
        self.copy(kind, j, slot, slot, self.me.core).wait_recv()

    def share(self, kind, j, side, t):
        self.wait_recv(kind, j, side, t)
        slot = self.at(side, t, j)
        self.copy(kind + 3, j, slot, slot, self.me.core).start()

    def relay(self):
        me = self.me

        @pl.loop(0, NC)
        def _(j):
            self.share(2, j, 1, me.t)
            slot = self.at(1, me.t, j)
            self.copy(3, j, slot, slot, me.x).start()
            self.share(1, j, 0, me.t_x)

    def finish(self):
        me = self.me

        @pl.loop(0, NC)
        def _(j):
            self.share(3, j, 1, me.t_x)

        @pl.loop(0, NC)
        def _(j):
            self.wait_recv(0, j, 0, me.t_core)
            self.wait_recv(4, j, 0, me.t_far)
            self.wait_recv(5, j, 1, me.t_core)
            self.wait_recv(6, j, 1, me.t_far)
            self.local(j).wait()
            for kind in range(7):
                self.copy(kind, j, self.piece(j), self.piece(j), me.core).wait_send()


class Scatter:
    SEMS = [grid_of(4, NC), grid_of(4, NC), grid_of(4, NC), grid_of(3, NC), grid_of(3, NC)]

    @staticmethod
    def scratch(rows, width):
        return [pltpu.VMEM((n, rows, width), LOW) for n in (4, 4, 3)] + Scatter.SEMS

    def __init__(self, me, parts, held, came, hops, load, send, recv, hop_send, hop_recv):
        self.me, self.parts = me, parts
        self.held, self.came, self.hops = held, came, hops
        self.load, self.send, self.recv = load, send, recv
        self.hop_send, self.hop_recv = hop_send, hop_recv
        self.rows = held.shape[1] // NC
        self.pairs = [
            (0, me.t, me.t_core),
            (0, me.t_x, me.t_far),
            (1, me.t, me.t_core),
            (1, me.t_x, me.t_far),
        ]

    def span(self, j):
        return pl.ds(j * self.rows, self.rows)

    def core_copy(self, i, j):
        side, _, theirs = self.pairs[i]
        return remote(
            self.parts.at[side, theirs, self.span(j)],
            self.came.at[i, self.span(j)],
            self.send.at[i, j],
            self.recv.at[i, j],
            self.me.core,
        )

    def load_copy(self, i, j):
        side, mine, _ = self.pairs[i]
        return pltpu.make_async_copy(
            self.parts.at[side, mine, self.span(j)], self.held.at[i, self.span(j)], self.load.at[i, j]
        )

    def hop(self, kind, j, src, peer):
        return remote(
            src, self.hops.at[kind, self.span(j)], self.hop_send.at[kind, j], self.hop_recv.at[kind, j], peer
        )

    def start(self):
        for i in (3, 1, 2, 0):

            @pl.loop(0, NC)
            def _(j):
                self.core_copy(i, j).start()
                self.load_copy(i, j).start()

    def joined(self, i, j):
        self.load_copy(i, j).wait()
        self.core_copy(i, j).wait_recv()
        return self.held[i, self.span(j)].astype(F32) + self.came[i, self.span(j)].astype(F32)

    def arrived(self, kind, j):
        self.hop(kind, j, self.hops.at[kind, self.span(j)], self.me.x).wait_recv()
        return self.hops[kind, self.span(j)].astype(F32)

    def spread(self):
        for kind, i in ((0, 3), (1, 1)):

            @pl.loop(0, NC)
            def _(j):
                self.held[i, self.span(j)] = self.joined(i, j).astype(LOW)
                self.hop(kind, j, self.held.at[i, self.span(j)], self.me.x).start()

    def turn(self):
        @pl.loop(0, NC)
        def _(j):
            total = self.joined(2, j) + self.arrived(0, j)
            self.held[2, self.span(j)] = total.astype(LOW)
            self.hop(2, j, self.held.at[2, self.span(j)], self.me.z).start()

    def result(self, j):
        return self.joined(0, j) + self.arrived(1, j) + self.arrived(2, j)

    def finish(self):
        @pl.loop(0, NC)
        def _(j):
            for i in range(4):
                self.core_copy(i, j).wait_send()
            for kind in range(3):
                self.hop(kind, j, self.hops.at[kind, self.span(j)], self.me.x).wait_send()


def block_at(ref, owner, rows, width, first=0, count=None):
    count = rows if count is None else count
    if len(ref.shape) == 3:
        return ref.at[owner, pl.ds(first, count)]
    if ref.shape[0] == rows:
        return ref.at[pl.ds(first, count), pl.ds(pl.multiple_of(owner * width, width), width)]
    return ref.at[pl.ds(pl.multiple_of(owner * rows + first, count), count)]


class WeightGather:
    @staticmethod
    def sems(lines):
        return [grid_of(lines, NW), grid_of(lines, NW), grid_of(lines, NW), grid_of(lines, NW), grid_of(NW)]

    def __init__(self, me, halves, whole, z_send, z_recv, y_send, y_recv, keep):
        self.me, self.halves, self.whole = me, halves, whole
        self.z_send, self.z_recv, self.y_send, self.y_recv, self.keep = z_send, z_recv, y_send, y_recv, keep
        _, self.rows, self.width = halves.shape
        self.count = self.rows // NW

    def at(self, owner, p):
        return block_at(self.whole, owner, self.rows, self.width, p * self.count, self.count)

    def piece(self, half, p):
        return self.halves.at[half, pl.ds(p * self.count, self.count)]

    def z_copy(self, k, p, src, dst, peer):
        return remote(src, dst, self.z_send.at[k, p], self.z_recv.at[k, p], peer)

    def y_copy(self, k, p, src, dst):
        return remote(src, dst, self.y_send.at[k, p], self.y_recv.at[k, p], self.me.y)

    def local(self, p):
        return pltpu.make_async_copy(self.piece(self.me.side, p), self.at(self.me.d, p), self.keep.at[p])

    def start(self, p):
        me = self.me

        @pl.loop(1, me.lines)
        def _(k):
            line = me.ahead(k)
            self.z_copy(k, p, self.piece(lax.rem(line, 2), p), self.at(me.d, p), me.mate(line)).start()

        self.y_copy(0, p, self.piece(me.side, p), self.at(me.d, p)).start()
        self.local(p).start()

    def forward(self, p):
        me = self.me

        @pl.loop(1, me.lines)
        def _(k):
            slot = self.at(2 * me.behind(k) + me.lane, p)
            self.z_copy(k, p, slot, slot, me.y).wait_recv()
            self.y_copy(k, p, slot, slot).start()

    def finish(self):
        me = self.me
        for p in range(NW):

            @pl.loop(0, me.lines)
            def _(k):
                slot = self.at(2 * me.behind(k) + 1 - me.lane, p)
                self.y_copy(k, p, slot, slot).wait()

            @pl.loop(1, me.lines)
            def _(k):
                slot = self.at(me.d, p)
                self.z_copy(k, p, slot, slot, me.y).wait_send()

            self.local(p).wait()


class WeightScatter:
    @staticmethod
    def scratch(lines, rows, width):
        return [pltpu.VMEM((lines, rows, width), LOW)] * 3 + [grid_of(lines)] * 5

    def __init__(self, me, parts, held, came, hops, load, y_send, y_recv, z_send, z_recv):
        self.me, self.parts, self.held, self.came, self.hops = me, parts, held, came, hops
        self.load, self.y_send, self.y_recv, self.z_send, self.z_recv = load, y_send, y_recv, z_send, z_recv
        _, self.rows, self.width = held.shape
        self.step = 32

    def y_copy(self, k):
        src = block_at(self.parts, 2 * self.me.ahead(k) + 1 - self.me.lane, self.rows, self.width)
        return remote(src, self.came.at[k], self.y_send.at[k], self.y_recv.at[k], self.me.y)

    def load_copy(self, k):
        src = block_at(self.parts, 2 * self.me.ahead(k) + self.me.lane, self.rows, self.width)
        return pltpu.make_async_copy(src, self.held.at[k], self.load.at[k])

    def z_copy(self, k, peer):
        return remote(self.held.at[k], self.hops.at[k], self.z_send.at[k], self.z_recv.at[k], peer)

    def start(self):
        @pl.loop(1, self.me.lines + 1)
        def _(n):
            k = lax.rem(n, self.me.lines)
            self.y_copy(k).start()
            self.load_copy(k).start()

    def joined(self, k, at):
        return self.held[k, at].astype(F32) + self.came[k, at].astype(F32)

    def spread(self, first, last):
        @pl.loop(first, last)
        def _(k):
            self.load_copy(k).wait()
            self.y_copy(k).wait_recv()

            @pl.loop(0, self.rows, step=self.step)
            def _(row):
                at = pl.ds(row, self.step)
                self.held[k, at] = self.joined(k, at).astype(LOW)

            self.z_copy(k, self.me.mate(self.me.ahead(k))).start()

    def finish(self, store):
        me = self.me
        self.load_copy(0).wait()
        self.y_copy(0).wait_recv()

        @pl.loop(1, me.lines)
        def _(k):
            self.z_copy(k, me.y).wait_recv()

        @pl.loop(0, self.rows, step=self.step)
        def _(row):
            at = pl.ds(row, self.step)
            same, other = self.joined(0, at), self.hops[1, at].astype(F32)
            for k in range(2, me.lines):
                if k % 2:
                    other = other + self.hops[k, at].astype(F32)
                else:
                    same = same + self.hops[k, at].astype(F32)
            store(me.side, at, same)
            store(1 - me.side, at, other)

        @pl.loop(0, me.lines)
        def _(k):
            self.y_copy(k).wait_send()

        @pl.loop(1, me.lines)
        def _(k):
            self.z_copy(k, me.y).wait_send()


def store_columns(*outs):
    def store(half, at, value):
        width = outs[0].shape[1] // 2
        for n, out in enumerate(outs):
            out[at, pl.ds(pl.multiple_of(half * width, width), width)] = value[:, n * width : (n + 1) * width]

    return store


def store_rows(out):
    def store(half, at, value):
        out[pl.ds(pl.multiple_of(half * (out.shape[0] // 2) + at.start, at.size), at.size)] = value

    return store


class SumAll:
    @staticmethod
    def scratch(dp_total, width):
        steps = dp_total.bit_length() + 1
        return [pltpu.VMEM((steps + 1, 8, width), F32), pltpu.VMEM((steps, 8, width), F32), grid_of(steps), grid_of(steps)]

    def __init__(self, me, held, came, send, recv):
        self.me, self.held, self.came, self.send, self.recv = me, held, came, send, recv

    def run(self, shared):
        me, peers, mask = self.me, [], 1
        while mask < 2 * me.lines:
            peers.append((me.d + mask - 2 * mask * lax.rem(lax.div(me.d, mask), 2), me.t))
            mask *= 2
        dp_steps = len(peers)
        for n, peer in enumerate(peers + [me.core, me.x]):
            copy = remote(self.held.at[n], self.came.at[n], self.send.at[n], self.recv.at[n], peer)
            copy.start()
            copy.wait()
            total = self.held[n] + self.came[n]
            if n >= dp_steps:
                row = lax.broadcasted_iota(jnp.int32, total.shape, 0)
                total = jnp.where(row < shared, total, self.held[n])
            self.held[n + 1] = total
        return self.held[dp_steps + 2]


def unit_of(rows):
    centred = rows - jnp.mean(rows, axis=1, keepdims=True)
    inverse = lax.rsqrt(jnp.mean(centred * centred, axis=1, keepdims=True) + EPSILON)
    return centred * inverse, inverse


def back_of(grad_rows, unit_rows, inverse, gain):
    scaled = grad_rows * gain
    return inverse * (
        scaled
        - jnp.mean(scaled, axis=1, keepdims=True)
        - unit_rows * jnp.mean(scaled * unit_rows, axis=1, keepdims=True)
    )


def pieces(rows):
    size = rows // NC
    return lambda j: pl.ds(j * size, size)


class Cut:
    def __init__(self, refs):
        self.refs = list(refs)

    def take(self, count):
        taken, self.refs = self.refs[:count], self.refs[count:]
        return taken


def head_kernel(dp_total, x, gain, shift, grad, qkv, out, whole, whole_grad, qkv_whole, out_whole, own, own_grad, *scratch):
    me = Place(dp_total)
    at, cut = pieces(x.shape[0]), Cut(scratch)
    gather, gather_grad = Gather(me, own, whole, *cut.take(3)), Gather(me, own_grad, whole_grad, *cut.take(3))
    first, second = WeightGather(me, qkv, qkv_whole, *cut.take(5)), WeightGather(me, out, out_whole, *cut.take(5))
    me.greet()

    @pl.loop(0, NC)
    def _(j):
        unit_rows, _ = unit_of(x[at(j)])
        own[at(j)] = (unit_rows * gain[...] + shift[...]).astype(LOW)
        gather.start(j)

    for p in range(NW):
        first.start(p)

    @pl.loop(0, NC)
    def _(j):
        own_grad[at(j)] = grad[at(j)].astype(LOW)

    gather.relay()
    for p in range(NW):
        second.start(p)
    first.forward(0)
    gather.finish()

    @pl.loop(0, NC)
    def _(j):
        gather_grad.start(j)

    for p in range(1, NW):
        first.forward(p)
    for p in range(NW):
        second.forward(p)
    gather_grad.relay()
    gather_grad.finish()
    first.finish()
    second.finish()


def middle_kernel(dp_total, parts, base, gain, shift, up, down, resid, whole, up_whole, down_whole, own, *scratch):
    me = Place(dp_total)
    at, cut = pieces(base.shape[0]), Cut(scratch)
    scatter, gather = Scatter(me, parts, *cut.take(8)), Gather(me, own, whole, *cut.take(3))
    first, second = WeightGather(me, up, up_whole, *cut.take(5)), WeightGather(me, down, down_whole, *cut.take(5))
    me.greet()
    scatter.start()
    first.start(0)
    scatter.spread()
    scatter.turn()
    first.forward(0)

    @pl.loop(0, NC)
    def _(j):
        rows = base[at(j)] + scatter.result(j)
        resid[at(j)] = rows
        unit_rows, _ = unit_of(rows)
        own[at(j)] = (unit_rows * gain[...] + shift[...]).astype(LOW)
        gather.start(j)

    for p in range(1, NW):
        first.start(p)
    for p in range(NW):
        second.start(p)
    gather.relay()
    for p in range(1, NW):
        first.forward(p)
    gather.finish()
    for p in range(NW):
        second.forward(p)
    scatter.finish()
    first.finish()
    second.finish()


def turn_kernel(
    dp_total, parts, resid, grad, gain, down, up, grad_resid, whole, sums, down_done, up_done, own, *scratch
):
    me = Place(dp_total)
    at, cut = pieces(resid.shape[0]), Cut(scratch)
    scatter, gather = Scatter(me, parts, *cut.take(8)), Gather(me, own, whole, *cut.take(3))
    first, second = WeightScatter(me, down, *cut.take(8)), WeightScatter(me, up, *cut.take(8))
    lines = me.lines
    me.greet()
    scatter.start()
    first.start()
    second.start()
    scatter.spread()
    scatter.turn()
    first.spread(1, lines // 2)
    sums[...] = jnp.zeros_like(sums)

    @pl.loop(0, NC)
    def _(j):
        unit_rows, inverse = unit_of(resid[at(j)])
        e = scatter.result(j)
        rows = grad[at(j)] + back_of(e, unit_rows, inverse, gain[...])
        grad_resid[at(j)] = rows
        own[at(j)] = rows.astype(LOW)
        gather.start(j)
        sums[0:1] += jnp.sum(e * unit_rows, axis=0, keepdims=True)
        sums[1:2] += jnp.sum(e, axis=0, keepdims=True)
        sums[2:3] += jnp.sum(rows, axis=0, keepdims=True)
        sums[3:4] += jnp.sum(grad[at(j)], axis=0, keepdims=True)

    first.spread(lines // 2, lines)
    gather.relay()
    gather.finish()
    scatter.finish()
    second.spread(1, lines)
    first.finish(store_rows(down_done))
    second.finish(store_columns(up_done))


def tail_kernel(
    dp_total, parts, lowered, x, gain, grad_resid, base, early, out, qkv,
    grad_inputs, output, sums, out_done, query_done, key_done, value_done, *scratch,
):
    me = Place(dp_total)
    at, cut = pieces(x.shape[0]), Cut(scratch)
    scatter, other = Scatter(me, parts, *cut.take(8)), Scatter(me, lowered, *cut.take(8))
    first, second = WeightScatter(me, out, *cut.take(8)), WeightScatter(me, qkv, *cut.take(8))
    vectors = SumAll(me, *cut.take(4))
    me.greet()
    scatter.start()
    second.start()
    first.start()
    scatter.spread()
    scatter.turn()
    vectors.held[0] = early[...]
    other.start()
    second.spread(1, me.lines)

    @pl.loop(0, NC)
    def _(j):
        unit_rows, inverse = unit_of(x[at(j)])
        e = scatter.result(j)
        grad_inputs[at(j)] = grad_resid[at(j)] + back_of(e, unit_rows, inverse, gain[...])
        vectors.held[0, 0:1] += jnp.sum(e * unit_rows, axis=0, keepdims=True)
        vectors.held[0, 1:2] += jnp.sum(e, axis=0, keepdims=True)

    sums[...] = vectors.run(6)
    scatter.finish()
    other.spread()
    other.turn()
    first.spread(1, me.lines)

    @pl.loop(0, NC)
    def _(j):
        output[at(j)] = base[at(j)] + other.result(j)

    other.finish()
    second.finish(store_columns(query_done, key_done, value_done))
    first.finish(store_rows(out_done))


VMEM = pl.BlockSpec(memory_space=pltpu.VMEM)
ANY = pl.BlockSpec(memory_space=pl.ANY)


def call(kernel, number, ins, in_specs, outs, out_specs, scratch):
    return pl.pallas_call(
        functools.partial(kernel, lax.axis_size("dp")),
        out_shape=outs,
        in_specs=in_specs,
        out_specs=out_specs,
        scratch_shapes=scratch,
        compiler_params=pltpu.CompilerParams(
            collective_id=number, has_side_effects=True, vmem_limit_bytes=48 << 20
        ),
        cost_estimate=pl.CostEstimate(flops=0, bytes_accessed=100_000_000, transcendentals=0),
    )(*ins)


def like(*shape, dtype=F32):
    return jax.ShapeDtypeStruct(shape, dtype)


def local(
    inputs,
    grad_output,
    seg_ids,
    positions,
    norm1_gain,
    norm1_bias,
    query_weight,
    query_bias,
    key_weight,
    value_weight,
    value_bias,
    out_weight,
    out_bias,
    norm2_gain,
    norm2_bias,
    up_weight,
    up_bias,
    down_weight,
    down_bias,
):
    dp_total = lax.axis_size("dp")
    tensor_total = lax.axis_size("tensor")
    lines = dp_total // 2
    place = lax.axis_index("dp")
    side = (place >> 1) & 1

    def hop(rows, mask):
        return lax.ppermute(rows, "dp", [(i, i ^ mask) for i in range(dp_total)])

    def own_half(vector):
        return lax.dynamic_slice_in_dim(vector, side * (vector.shape[0] // 2), vector.shape[0] // 2, 0)

    def column_halves(*weights):
        cut = [w.astype(LOW).reshape(w.shape[0], 2, -1) for w in weights]
        return jnp.concatenate(cut, 2).transpose(1, 0, 2)

    def row_halves(weight):
        return weight.astype(LOW).reshape(2, -1, weight.shape[1])

    def mm(left, right):
        return jnp.dot(left, right, preferred_element_type=F32)

    def mm_nt(left, right):
        return jnp.einsum("td,fd->tf", left, right, preferred_element_type=F32)

    def mm_tn(left, right):
        return jnp.einsum("ta,tb->ab", left, right, preferred_element_type=F32)

    rows, width = inputs.shape
    row = lambda vector: vector.reshape(1, -1)
    group = like(2, tensor_total, rows, width, dtype=LOW)
    own = pltpu.VMEM((rows, width), LOW)
    token_scratch = Scatter.scratch(rows, width)

    def whole_rows(halves):
        return like(dp_total * halves.shape[1], halves.shape[2], dtype=LOW)

    def whole_columns(halves):
        _, high, wide = halves.shape
        return like(*((dp_total, high, wide) if wide % 128 else (high, dp_total * wide)), dtype=LOW)

    def side_by_side(whole):
        return whole if whole.ndim == 2 else whole.transpose(1, 0, 2).reshape(whole.shape[1], -1)

    def column_blocks(partial):
        wide = partial.shape[1] // dp_total
        return partial.reshape(-1, dp_total, wide).transpose(1, 0, 2) if wide % 128 else partial

    segment = jnp.stack([seg_ids, hop(seg_ids, 2)]).reshape(-1, GROUP)
    places = jnp.stack([positions, hop(positions, 2)]).reshape(-1, GROUP)
    qkv_halves = column_halves(query_weight, key_weight, value_weight)
    out_halves, up_halves, down_halves = row_halves(out_weight), column_halves(up_weight), row_halves(down_weight)

    whole1, grad_whole, qkv_full, o_full = call(
        head_kernel, 1,
        (inputs, row(norm1_gain), row(norm1_bias), grad_output, qkv_halves, out_halves), [VMEM] * 6,
        (group, group, whole_rows(qkv_halves), whole_columns(out_halves)), (ANY,) * 4,
        [own, own] + Gather.SEMS * 2 + WeightGather.sems(lines) * 2,
    )
    whole1, grad_whole, o_full = whole1.reshape(-1, width), grad_whole.reshape(-1, width), side_by_side(o_full)
    halves = query_bias.shape[0] // 2
    qkv = mm(whole1, qkv_full)
    queries = (qkv[:, :halves] + own_half(query_bias)).astype(LOW)
    keys = qkv[:, halves : 2 * halves].astype(LOW)
    values = (qkv[:, 2 * halves :] + own_half(value_bias)).astype(LOW)
    attended, log_totals = attend(queries, keys, values, segment, places)

    def as_group(partial):
        return partial.astype(LOW).reshape(group.shape)

    resid, whole2, up_full, down_full = call(
        middle_kernel, 2,
        (as_group(mm(attended, o_full)), inputs + out_bias, row(norm2_gain), row(norm2_bias), up_halves, down_halves),
        [ANY] + [VMEM] * 5,
        (like(rows, width), group, whole_rows(up_halves), whole_columns(down_halves)), (VMEM, ANY, ANY, ANY),
        [own] + token_scratch + Gather.SEMS + WeightGather.sems(lines) * 2,
    )
    whole2, down_full = whole2.reshape(-1, width), side_by_side(down_full)
    pre_act = mm(whole2, up_full) + own_half(up_bias)
    cumulative, slope = gelu_parts(pre_act)
    activated = (pre_act * cumulative).astype(LOW)
    grad_down = column_blocks(mm_tn(activated, grad_whole).astype(LOW))
    lowered = as_group(mm(activated, down_full))
    grad_pre = (mm_nt(grad_whole, down_full) * slope).astype(LOW)
    grad_up = mm_tn(whole2, grad_pre).astype(LOW)

    grad_resid, grad_mixed, sums2, down_done, up_done = call(
        turn_kernel, 3,
        (as_group(mm_nt(grad_pre, up_full)), resid, grad_output, row(norm2_gain), grad_down, grad_up),
        [ANY] + [VMEM] * 3 + [ANY] * 2,
        (like(rows, width), group, like(8, width), like(*down_weight.shape), like(*up_weight.shape)),
        (VMEM, ANY, VMEM, VMEM, VMEM),
        [own] + token_scratch + Gather.SEMS
        + WeightScatter.scratch(lines, *down_halves.shape[1:]) + WeightScatter.scratch(lines, *up_halves.shape[1:]),
    )
    grad_mixed = grad_mixed.reshape(-1, width)
    grad_out = column_blocks(mm_tn(attended, grad_mixed).astype(LOW))
    grad_att = mm_nt(grad_mixed, o_full).astype(LOW)
    grad_queries, grad_keys, grad_values = attend_back(
        queries, keys, values, grad_att, segment, places, log_totals
    )
    grad_qkv = jnp.concatenate([grad_queries, grad_keys, grad_values], 1)
    grad_qkv_w = mm_tn(whole1, grad_qkv).astype(LOW)

    def column_sums(values):
        half = jnp.sum(values.astype(F32), axis=0)
        return jnp.where(side == jnp.arange(2)[:, None], half, 0.0).reshape(-1)

    heads = jnp.concatenate([column_sums(grad_queries), column_sums(grad_values)])
    early = jnp.concatenate(
        [
            jnp.zeros((2, width), F32),
            sums2[:4],
            row(jnp.pad(column_sums(grad_pre), (0, width - 2 * grad_pre.shape[1]))),
            row(jnp.pad(heads, (0, width - heads.shape[0]))),
        ]
    )
    grad_inputs, layer_output, sums, out_done, query_done, key_done, value_done = call(
        tail_kernel, 4,
        (
            as_group(mm_nt(grad_qkv, qkv_full)), lowered, inputs, row(norm1_gain), grad_resid, resid + down_bias, early,
            grad_out, grad_qkv_w,
        ),
        [ANY] * 2 + [VMEM] * 5 + [ANY] * 2,
        (
            like(rows, width), like(rows, width), like(8, width), like(*out_weight.shape),
            *[like(*query_weight.shape)] * 3,
        ),
        (VMEM,) * 7,
        token_scratch * 2
        + WeightScatter.scratch(lines, *out_halves.shape[1:]) + WeightScatter.scratch(lines, *qkv_halves.shape[1:])
        + SumAll.scratch(dp_total, width),
    )
    return (
        layer_output,
        grad_inputs,
        sums[0],
        sums[1],
        query_done,
        sums[7, : 2 * halves],
        key_done,
        value_done,
        sums[7, 2 * halves : 4 * halves],
        out_done,
        sums[4],
        sums[2],
        sums[3],
        up_done,
        sums[6, : up_bias.shape[0]],
        down_done,
        sums[5],
    )


def solution(mesh):
    tokens, weight, weight_t = P(("dp", "tensor"), None), P("dp", "tensor"), P("tensor", "dp")
    whole, part = P(), P("tensor")
    return jax.shard_map(
        local,
        mesh=mesh,
        in_specs=(
            tokens, tokens, P("dp"), P("dp"), whole, whole, weight, part, weight, weight, part,
            weight_t, whole, whole, whole, weight, part, weight_t, whole,
        ),
        out_specs=(
            tokens, tokens, whole, whole, weight, part, weight, weight, part, weight_t, whole,
            whole, whole, weight, part, weight_t, whole,
        ),
        check_vma=False,
    )
```

```python
import functools

import jax
import jax.numpy as jnp
from jax import lax
from jax.experimental import pallas as pl
from jax.experimental.pallas import tpu as pltpu
from jax.sharding import PartitionSpec as P

HEAD_DIM = 128
GROUP = 512
EPSILON = 1e-05
NEGATIVE = -1e30
LOW = jnp.bfloat16
F32 = jnp.float32


def gelu_parts(pre_act):
    cumulative = 0.5 * (1.0 + lax.erf(pre_act * 0.7071067811865476))
    density = jnp.exp(-0.5 * pre_act * pre_act) * 0.3989422804014327
    return cumulative, cumulative + pre_act * density


NC = 4
NW = 2
MESH = pl.DeviceIdType.MESH


def remote(src, dst, send, recv, peer):
    return pltpu.make_async_remote_copy(
        src_ref=src, dst_ref=dst, send_sem=send, recv_sem=recv, device_id=peer, device_id_type=MESH
    )


def grid_of(*shape):
    return pltpu.SemaphoreType.DMA(shape)


class Place:
    def __init__(self, dp_total):
        self.lines = dp_total // 2
        self.d = lax.axis_index("dp")
        self.t = lax.axis_index("tensor")
        self.lane, self.line = lax.rem(self.d, 2), lax.div(self.d, 2)
        self.side = lax.rem(self.line, 2)
        self.t_core = self.t + 1 - 2 * lax.rem(self.t, 2)
        self.t_x = lax.rem(self.t + 2, 4)
        self.t_far = lax.rem(self.t_core + 2, 4)
        self.core = (self.d, self.t_core)
        self.x = (self.d, self.t_x)
        self.y = (self.d + 1 - 2 * self.lane, self.t)
        self.z = (self.d + 2 - 4 * self.side, self.t)

    def ahead(self, k):
        return lax.rem(self.line + k, self.lines)

    def behind(self, k):
        return lax.rem(self.line + self.lines - k, self.lines)

    def mate(self, line):
        return (2 * line + self.lane, self.t)

    def greet(self):
        barrier = pltpu.get_barrier_semaphore()
        for peer in (self.core, self.x, self.y):
            pl.semaphore_signal(barrier, inc=1, device_id=peer, device_id_type=MESH)

        @pl.loop(1, self.lines)
        def _(k):
            pl.semaphore_signal(barrier, inc=1, device_id=self.mate(self.ahead(k)), device_id_type=MESH)

        pl.semaphore_wait(barrier, 2 + self.lines)


class Gather:
    SEMS = [grid_of(7, NC), grid_of(7, NC), grid_of(NC)]

    def __init__(self, me, own, whole, send, recv, keep):
        self.me, self.own, self.whole = me, own, whole
        self.send, self.recv, self.keep = send, recv, keep
        self.rows = own.shape[0] // NC

    def at(self, side, t, j):
        return self.whole.at[side, t, pl.ds(j * self.rows, self.rows)]

    def piece(self, j):
        return self.own.at[pl.ds(j * self.rows, self.rows)]

    def copy(self, kind, j, src, dst, peer):
        return remote(src, dst, self.send.at[kind, j], self.recv.at[kind, j], peer)

    def local(self, j):
        return pltpu.make_async_copy(self.piece(j), self.at(0, self.me.t, j), self.keep.at[j])

    def start(self, j):
        me = self.me
        self.copy(2, j, self.piece(j), self.at(1, me.t, j), me.z).start()
        self.copy(1, j, self.piece(j), self.at(0, me.t, j), me.x).start()
        self.copy(0, j, self.piece(j), self.at(0, me.t, j), me.core).start()
        self.local(j).start()

    def wait_recv(self, kind, j, side, t):
        slot = self.at(side, t, j)
        self.copy(kind, j, slot, slot, self.me.core).wait_recv()

    def share(self, kind, j, side, t):
        self.wait_recv(kind, j, side, t)
        slot = self.at(side, t, j)
        self.copy(kind + 3, j, slot, slot, self.me.core).start()

    def relay(self):
        me = self.me

        @pl.loop(0, NC)
        def _(j):
            self.share(2, j, 1, me.t)
            slot = self.at(1, me.t, j)
            self.copy(3, j, slot, slot, me.x).start()
            self.share(1, j, 0, me.t_x)

    def finish(self):
        me = self.me

        @pl.loop(0, NC)
        def _(j):
            self.share(3, j, 1, me.t_x)

        @pl.loop(0, NC)
        def _(j):
            self.wait_recv(0, j, 0, me.t_core)
            self.wait_recv(4, j, 0, me.t_far)
            self.wait_recv(5, j, 1, me.t_core)
            self.wait_recv(6, j, 1, me.t_far)
            self.local(j).wait()
            for kind in range(7):
                self.copy(kind, j, self.piece(j), self.piece(j), me.core).wait_send()


class Scatter:
    SEMS = [grid_of(4, NC), grid_of(4, NC), grid_of(4, NC), grid_of(3, NC), grid_of(3, NC)]

    @staticmethod
    def scratch(rows, width):
        return [pltpu.VMEM((n, rows, width), LOW) for n in (4, 4, 3)] + Scatter.SEMS

    def __init__(self, me, parts, held, came, hops, load, send, recv, hop_send, hop_recv):
        self.me, self.parts = me, parts
        self.held, self.came, self.hops = held, came, hops
        self.load, self.send, self.recv = load, send, recv
        self.hop_send, self.hop_recv = hop_send, hop_recv
        self.rows = held.shape[1] // NC
        self.pairs = [
            (0, me.t, me.t_core),
            (0, me.t_x, me.t_far),
            (1, me.t, me.t_core),
            (1, me.t_x, me.t_far),
        ]

    def span(self, j):
        return pl.ds(j * self.rows, self.rows)

    def core_copy(self, i, j):
        side, _, theirs = self.pairs[i]
        return remote(
            self.parts.at[side, theirs, self.span(j)],
            self.came.at[i, self.span(j)],
            self.send.at[i, j],
            self.recv.at[i, j],
            self.me.core,
        )

    def load_copy(self, i, j):
        side, mine, _ = self.pairs[i]
        return pltpu.make_async_copy(
            self.parts.at[side, mine, self.span(j)], self.held.at[i, self.span(j)], self.load.at[i, j]
        )

    def hop(self, kind, j, src, peer):
        return remote(
            src, self.hops.at[kind, self.span(j)], self.hop_send.at[kind, j], self.hop_recv.at[kind, j], peer
        )

    def start(self):
        for i in (3, 1, 2, 0):

            @pl.loop(0, NC)
            def _(j):
                self.core_copy(i, j).start()
                self.load_copy(i, j).start()

    def joined(self, i, j):
        self.load_copy(i, j).wait()
        self.core_copy(i, j).wait_recv()
        return self.held[i, self.span(j)].astype(F32) + self.came[i, self.span(j)].astype(F32)

    def arrived(self, kind, j):
        self.hop(kind, j, self.hops.at[kind, self.span(j)], self.me.x).wait_recv()
        return self.hops[kind, self.span(j)].astype(F32)

    def spread(self):
        for kind, i in ((0, 3), (1, 1)):

            @pl.loop(0, NC)
            def _(j):
                self.held[i, self.span(j)] = self.joined(i, j).astype(LOW)
                self.hop(kind, j, self.held.at[i, self.span(j)], self.me.x).start()

    def turn(self):
        @pl.loop(0, NC)
        def _(j):
            total = self.joined(2, j) + self.arrived(0, j)
            self.held[2, self.span(j)] = total.astype(LOW)
            self.hop(2, j, self.held.at[2, self.span(j)], self.me.z).start()

    def result(self, j):
        return self.joined(0, j) + self.arrived(1, j) + self.arrived(2, j)

    def finish(self):
        @pl.loop(0, NC)
        def _(j):
            for i in range(4):
                self.core_copy(i, j).wait_send()
            for kind in range(3):
                self.hop(kind, j, self.hops.at[kind, self.span(j)], self.me.x).wait_send()


def block_at(ref, owner, rows, width, first=0, count=None):
    count = rows if count is None else count
    if len(ref.shape) == 3:
        return ref.at[owner, pl.ds(first, count)]
    if ref.shape[0] == rows:
        return ref.at[pl.ds(first, count), pl.ds(pl.multiple_of(owner * width, width), width)]
    return ref.at[pl.ds(pl.multiple_of(owner * rows + first, count), count)]


class WeightGather:
    @staticmethod
    def sems(lines):
        return [grid_of(lines, NW), grid_of(lines, NW), grid_of(lines, NW), grid_of(lines, NW), grid_of(NW)]

    def __init__(self, me, halves, whole, z_send, z_recv, y_send, y_recv, keep):
        self.me, self.halves, self.whole = me, halves, whole
        self.z_send, self.z_recv, self.y_send, self.y_recv, self.keep = z_send, z_recv, y_send, y_recv, keep
        _, self.rows, self.width = halves.shape
        self.count = self.rows // NW

    def at(self, owner, p):
        return block_at(self.whole, owner, self.rows, self.width, p * self.count, self.count)

    def piece(self, half, p):
        return self.halves.at[half, pl.ds(p * self.count, self.count)]

    def z_copy(self, k, p, src, dst, peer):
        return remote(src, dst, self.z_send.at[k, p], self.z_recv.at[k, p], peer)

    def y_copy(self, k, p, src, dst):
        return remote(src, dst, self.y_send.at[k, p], self.y_recv.at[k, p], self.me.y)

    def local(self, p):
        return pltpu.make_async_copy(self.piece(self.me.side, p), self.at(self.me.d, p), self.keep.at[p])

    def start(self, p):
        me = self.me

        @pl.loop(1, me.lines)
        def _(k):
            line = me.ahead(k)
            self.z_copy(k, p, self.piece(lax.rem(line, 2), p), self.at(me.d, p), me.mate(line)).start()

        self.y_copy(0, p, self.piece(me.side, p), self.at(me.d, p)).start()
        self.local(p).start()

    def forward(self, p, first=1, last=None):
        me = self.me

        @pl.loop(first, me.lines if last is None else last)
        def _(k):
            slot = self.at(2 * me.behind(k) + me.lane, p)
            self.z_copy(k, p, slot, slot, me.y).wait_recv()
            self.y_copy(k, p, slot, slot).start()

    def finish(self, *which):
        me = self.me
        for p in which:

            @pl.loop(0, me.lines)
            def _(k):
                slot = self.at(2 * me.behind(k) + 1 - me.lane, p)
                self.y_copy(k, p, slot, slot).wait()

            @pl.loop(1, me.lines)
            def _(k):
                slot = self.at(me.d, p)
                self.z_copy(k, p, slot, slot, me.y).wait_send()

            self.local(p).wait()


class WeightScatter:
    @staticmethod
    def scratch(lines, rows, width):
        return [pltpu.VMEM((lines, rows, width), LOW)] * 3 + [grid_of(lines)] * 5

    def __init__(self, me, parts, held, came, hops, load, y_send, y_recv, z_send, z_recv):
        self.me, self.parts, self.held, self.came, self.hops = me, parts, held, came, hops
        self.load, self.y_send, self.y_recv, self.z_send, self.z_recv = load, y_send, y_recv, z_send, z_recv
        _, self.rows, self.width = held.shape
        self.step = 32

    def y_copy(self, k):
        src = block_at(self.parts, 2 * self.me.ahead(k) + 1 - self.me.lane, self.rows, self.width)
        return remote(src, self.came.at[k], self.y_send.at[k], self.y_recv.at[k], self.me.y)

    def load_copy(self, k):
        src = block_at(self.parts, 2 * self.me.ahead(k) + self.me.lane, self.rows, self.width)
        return pltpu.make_async_copy(src, self.held.at[k], self.load.at[k])

    def z_copy(self, k, peer):
        return remote(self.held.at[k], self.hops.at[k], self.z_send.at[k], self.z_recv.at[k], peer)

    def start(self):
        @pl.loop(1, self.me.lines + 1)
        def _(n):
            k = lax.rem(n, self.me.lines)
            self.y_copy(k).start()
            self.load_copy(k).start()

    def joined(self, k, at):
        return self.held[k, at].astype(F32) + self.came[k, at].astype(F32)

    def spread(self, first, last):
        @pl.loop(first, last)
        def _(k):
            self.load_copy(k).wait()
            self.y_copy(k).wait_recv()

            @pl.loop(0, self.rows, step=self.step)
            def _(row):
                at = pl.ds(row, self.step)
                self.held[k, at] = self.joined(k, at).astype(LOW)

            self.z_copy(k, self.me.mate(self.me.ahead(k))).start()

    def finish(self, store):
        me = self.me
        self.load_copy(0).wait()
        self.y_copy(0).wait_recv()

        @pl.loop(1, me.lines)
        def _(k):
            self.z_copy(k, me.y).wait_recv()

        @pl.loop(0, self.rows, step=self.step)
        def _(row):
            at = pl.ds(row, self.step)
            same, other = self.joined(0, at), self.hops[1, at].astype(F32)
            for k in range(2, me.lines):
                if k % 2:
                    other = other + self.hops[k, at].astype(F32)
                else:
                    same = same + self.hops[k, at].astype(F32)
            store(me.side, at, same)
            store(1 - me.side, at, other)

        @pl.loop(0, me.lines)
        def _(k):
            self.y_copy(k).wait_send()

        @pl.loop(1, me.lines)
        def _(k):
            self.z_copy(k, me.y).wait_send()


def store_columns(*outs):
    def store(half, at, value):
        width = outs[0].shape[1] // 2
        for n, out in enumerate(outs):
            out[at, pl.ds(pl.multiple_of(half * width, width), width)] = value[:, n * width : (n + 1) * width]

    return store


def store_rows(out):
    def store(half, at, value):
        out[pl.ds(pl.multiple_of(half * (out.shape[0] // 2) + at.start, at.size), at.size)] = value

    return store


class SumAll:
    @staticmethod
    def scratch(dp_total, width):
        steps = dp_total.bit_length() + 1
        return [pltpu.VMEM((steps + 1, 8, width), F32), pltpu.VMEM((steps, 8, width), F32), grid_of(steps), grid_of(steps)]

    def __init__(self, me, held, came, send, recv):
        self.me, self.held, self.came, self.send, self.recv = me, held, came, send, recv

    def run(self, shared):
        me, peers, mask = self.me, [], 1
        while mask < 2 * me.lines:
            peers.append((me.d + mask - 2 * mask * lax.rem(lax.div(me.d, mask), 2), me.t))
            mask *= 2
        dp_steps = len(peers)
        for n, peer in enumerate(peers + [me.core, me.x]):
            copy = remote(self.held.at[n], self.came.at[n], self.send.at[n], self.recv.at[n], peer)
            copy.start()
            copy.wait()
            total = self.held[n] + self.came[n]
            if n >= dp_steps:
                row = lax.broadcasted_iota(jnp.int32, total.shape, 0)
                total = jnp.where(row < shared, total, self.held[n])
            self.held[n + 1] = total
        return self.held[dp_steps + 2]


def unit_of(rows):
    centred = rows - jnp.mean(rows, axis=1, keepdims=True)
    inverse = lax.rsqrt(jnp.mean(centred * centred, axis=1, keepdims=True) + EPSILON)
    return centred * inverse, inverse


def back_of(grad_rows, unit_rows, inverse, gain):
    scaled = grad_rows * gain
    return inverse * (
        scaled
        - jnp.mean(scaled, axis=1, keepdims=True)
        - unit_rows * jnp.mean(scaled * unit_rows, axis=1, keepdims=True)
    )


def pieces(rows):
    size = rows // NC
    return lambda j: pl.ds(j * size, size)


class Cut:
    def __init__(self, refs):
        self.refs = list(refs)

    def take(self, count):
        taken, self.refs = self.refs[:count], self.refs[count:]
        return taken


NN, NT, TN = ((1,), (0,)), ((1,), (1,)), ((0,), (0,))


def dot(left, right, dims):
    return lax.dot_general(left, right, (dims, ((), ())), preferred_element_type=F32)


def column_halves(halves, *weights):
    width = weights[0].shape[1] // 2
    for n, weight in enumerate(weights):
        for half in range(2):
            halves[half, :, n * width : (n + 1) * width] = weight[:, half * width : (half + 1) * width].astype(LOW)


def row_halves(halves, weight):
    rows = weight.shape[0] // 2
    for half in range(2):
        halves[half] = weight[half * rows : (half + 1) * rows].astype(LOW)


def turned_halves(halves, weight):
    rows = weight.shape[0] // 2
    for half in range(2):
        halves[half] = weight[half * rows : (half + 1) * rows].T.astype(LOW)


def fill_mask(mask, infos, turned):
    @pl.loop(0, 2)
    def _(side):
        across = infos[side].astype(F32)
        down = across.T
        seg_row, pos_row, seg_col, pos_col = down[:, 0:1], down[:, 1:2], across[0:1], across[1:2]
        if turned:
            seg_q, pos_q, seg_k, pos_k = seg_col, pos_col, seg_row, pos_row
        else:
            seg_q, pos_q, seg_k, pos_k = seg_row, pos_row, seg_col, pos_col
        allowed = (pos_k <= pos_q) & ((seg_k == seg_q) | (seg_k == 0.0))
        mask[side] = jnp.where(allowed, 0.0, NEGATIVE).astype(LOW)


def heads_of(width):
    return [slice(n * HEAD_DIM, (n + 1) * HEAD_DIM) for n in range(width // HEAD_DIM)]


def attend(queries, keys, values, mask, attended, between):
    group = mask.shape[1]
    part = group // 2
    for side in range(2):
        for head in heads_of(queries.shape[1]):
            all_rows = pl.ds(side * group, group)

            @pl.loop(0, 2)
            def _(r):
                at = pl.ds(side * group + r * part, part)
                scores = dot(queries[at, head], keys[all_rows, head], NT) * (HEAD_DIM**-0.5)
                scores = scores + mask[side, pl.ds(r * part, part)].astype(F32)
                terms = jnp.exp(scores - jnp.max(scores, axis=1, keepdims=True))
                probs = (terms / jnp.sum(terms, axis=1, keepdims=True)).astype(LOW)
                attended[at, head] = dot(probs, values[all_rows, head], NN).astype(LOW)

            between()


def attend_back(queries, keys, values, grads, mask, grad_qkv, between):
    group, width = mask.shape[1], queries.shape[1]
    part = group // 2
    scale = HEAD_DIM**-0.5
    for side in range(2):
        for n, head in enumerate(heads_of(width)):
            rows = pl.ds(side * group, group)
            grad_key, grad_value = 0.0, 0.0
            for r in range(2):
                at = pl.ds(side * group + r * part, part)
                scores = dot(keys[rows, head], queries[at, head], NT) * scale
                scores = scores + mask[side, :, r * part : (r + 1) * part].astype(F32)
                terms = jnp.exp(scores - jnp.max(scores, axis=0, keepdims=True))
                probs = terms / jnp.sum(terms, axis=0, keepdims=True)
                grad_probs = dot(values[rows, head], grads[at, head], NT)
                delta = jnp.sum(probs * grad_probs, axis=0, keepdims=True)
                grad_scores = (probs * (grad_probs - delta)).astype(LOW)
                grad_value = grad_value + dot(probs.astype(LOW), grads[at, head], NN)
                grad_key = grad_key + dot(grad_scores, queries[at, head], NN)
                grad_query = dot(grad_scores, keys[rows, head], TN)
                grad_qkv[at, n * HEAD_DIM : (n + 1) * HEAD_DIM] = (grad_query * scale).astype(LOW)
            for m, value in ((1, grad_key * scale), (2, grad_value)):
                grad_qkv[rows, m * width + n * HEAD_DIM : m * width + (n + 1) * HEAD_DIM] = value.astype(LOW)
            between()


def column_blocks_of(width, size=256):
    return lambda n: pl.ds(pl.multiple_of(n * size, size), size)


def head_kernel(
    dp_total, x, gain, shift, grad, query, key, value, out, up, query_bias, value_bias, info,
    whole_out, whole_grad, qkv_out, o_out, up_out, parts, queries, keys, values, attended, infos,
    own, own_grad, whole, qkv_half, out_half, up_half, qkv_whole, o_whole, mask, *scratch,
):
    me = Place(dp_total)
    at, cut = pieces(x.shape[0]), Cut(scratch)
    gather, gather_grad = Gather(me, own, whole, *cut.take(3)), Gather(me, own_grad, whole_grad, *cut.take(3))
    first, second = WeightGather(me, qkv_half, qkv_whole, *cut.take(5)), WeightGather(me, out_half, o_whole, *cut.take(5))
    third = WeightGather(me, up_half, up_out, *cut.take(5))
    (save,) = cut.take(1)
    me.greet()
    info_copy = remote(info, infos.at[1], save.at[0], save.at[1], me.z)
    info_copy.start()

    @pl.loop(0, NC)
    def _(j):
        unit_rows, _ = unit_of(x[at(j)])
        own[at(j)] = (unit_rows * gain[...] + shift[...]).astype(LOW)
        gather.start(j)

    column_halves(qkv_half, query, key, value)
    for p in range(NW):
        first.start(p)
    turned_halves(out_half, out)
    for p in range(NW):
        second.start(p)
    column_halves(up_half, up)

    @pl.loop(0, NC)
    def _(j):
        own_grad[at(j)] = grad[at(j)].astype(LOW)

    info_copy.wait()
    infos[0] = info[...]
    fill_mask(mask, infos, False)
    gather.relay()
    first.forward(0)
    gather.finish()
    third.start(0)
    first.forward(1)

    @pl.loop(0, NC)
    def _(j):
        gather_grad.start(j)

    save_whole = pltpu.make_async_copy(whole, whole_out, save.at[2])
    save_whole.start()
    second.forward(0)
    second.forward(1)
    first.finish(0, 1)
    save_qkv = pltpu.make_async_copy(qkv_whole, qkv_out, save.at[3])
    save_qkv.start()
    group = mask.shape[1]
    width = queries.shape[1]

    @pl.loop(0, 2)
    def _(side):
        rows = pl.ds(pl.multiple_of(side * group, group), group)
        tokens = whole[side].reshape(group, -1)
        for n, (result, bias) in enumerate(((queries, query_bias), (keys, None), (values, value_bias))):
            total = dot(tokens, qkv_whole[:, n * width : (n + 1) * width], NN)
            result[rows] = (total if bias is None else total + bias[...]).astype(LOW)

    gather_grad.relay()
    steps = iter(((1, 2), (2, 3), (3, None)) if me.lines == 4 else ((1, None),))

    def between():
        span = next(steps, None)
        if span:
            third.forward(0, *span)

    attend(queries, keys, values, mask, attended, between)
    second.finish(0, 1)
    save_o = pltpu.make_async_copy(o_whole, o_out, save.at[4])
    save_o.start()
    block = column_blocks_of(x.shape[1])

    @pl.loop(0, x.shape[1] // 256)
    def _(n):
        total = dot(attended[...], o_whole[pl.ds(pl.multiple_of(n * 256, 256), 256)], NT)
        parts[:, :, :, block(n)] = total.astype(LOW).reshape(*parts.shape[:3], 256)

    gather_grad.finish()
    third.finish(0)
    for copy in (save_whole, save_qkv, save_o):
        copy.wait()


def middle_kernel(
    dp_total, parts, x, out_bias, gain, shift, up, down, up_part,
    resid, whole, up_whole, down_whole, own, up_half, down_half, *scratch,
):
    me = Place(dp_total)
    at, cut = pieces(x.shape[0]), Cut(scratch)
    scatter, gather = Scatter(me, parts, *cut.take(8)), Gather(me, own, whole, *cut.take(3))
    first, second = WeightGather(me, up_half, up_whole, *cut.take(5)), WeightGather(me, down_half, down_whole, *cut.take(5))
    me.greet()
    scatter.start()
    column_halves(up_half, up)
    first.start(1)
    scatter.spread()
    scatter.turn()
    row_halves(down_half, down)
    first.forward(1)

    @pl.loop(0, NC)
    def _(j):
        rows = x[at(j)] + scatter.result(j) + out_bias[...]
        resid[at(j)] = rows
        unit_rows, _ = unit_of(rows)
        own[at(j)] = (unit_rows * gain[...] + shift[...]).astype(LOW)
        gather.start(j)

    for p in range(NW):
        second.start(p)
    gather.relay()
    gather.finish()
    for p in range(NW):
        second.forward(p)
    scatter.finish()
    first.finish(1)
    second.finish(0, 1)


def turn_kernel(
    dp_total, parts, lowered, resid, grad, gain, down_bias, down, whole2, grad_pre, o_whole,
    queries, keys, values, attended, infos,
    grad_resid, output, sums, down_done, up_done, grad_qkv, grad_out,
    own, whole, mask, grad_att, grad_up, *scratch,
):
    me = Place(dp_total)
    at, cut = pieces(resid.shape[0]), Cut(scratch)
    scatter, other = Scatter(me, parts, *cut.take(8)), Scatter(me, lowered, *cut.take(8))
    gather = Gather(me, own, whole, *cut.take(3))
    first, second = WeightScatter(me, down, *cut.take(8)), WeightScatter(me, grad_up, *cut.take(8))
    lines = me.lines
    block = column_blocks_of(resid.shape[1])
    me.greet()
    scatter.start()
    first.start()
    scatter.spread()
    scatter.turn()

    @pl.loop(0, grad_up.shape[0] // 256)
    def _(n):
        grad_up[pl.ds(pl.multiple_of(n * 256, 256), 256)] = dot(whole2[:, block(n)], grad_pre[...], TN).astype(LOW)

    second.start()
    first.spread(1, lines // 2)
    sums[...] = jnp.zeros_like(sums)

    @pl.loop(0, NC)
    def _(j):
        unit_rows, inverse = unit_of(resid[at(j)])
        e = scatter.result(j)
        rows = grad[at(j)] + back_of(e, unit_rows, inverse, gain[...])
        grad_resid[at(j)] = rows
        own[at(j)] = rows.astype(LOW)
        gather.start(j)
        sums[0:1] += jnp.sum(e * unit_rows, axis=0, keepdims=True)
        sums[1:2] += jnp.sum(e, axis=0, keepdims=True)
        sums[2:3] += jnp.sum(rows, axis=0, keepdims=True)
        sums[3:4] += jnp.sum(grad[at(j)], axis=0, keepdims=True)

    fill_mask(mask, infos, True)
    first.spread(lines // 2, lines)
    gather.relay()
    gather.finish()
    other.start()
    other.spread()
    mixed = whole[...].reshape(-1, whole.shape[3])
    grad_att[...] = dot(mixed, o_whole[...], NN).astype(LOW)
    steps = iter(((1, 2), (2, 3), (3, 4)) if lines == 4 else ((1, lines),))

    def between():
        span = next(steps, None)
        if span:
            second.spread(*span)

    attend_back(queries, keys, values, grad_att, mask, grad_qkv, between)
    sums[4:5, : grad_qkv.shape[1]] = jnp.sum(grad_qkv[...].astype(F32), axis=0, keepdims=True)
    other.turn()

    @pl.loop(0, resid.shape[1] // 256)
    def _(n):
        columns = whole[:, :, :, block(n)].reshape(-1, 256)
        grad_out[:, block(n)] = dot(attended[...], columns, TN).astype(LOW)

    first.finish(store_rows(down_done))

    @pl.loop(0, NC)
    def _(j):
        output[at(j)] = resid[at(j)] + other.result(j) + down_bias[...]

    scatter.finish()
    other.finish()
    second.finish(store_columns(up_done))


def tail_kernel(
    dp_total, x, gain, grad_resid, early, out, whole, grad_qkv, qkv_whole,
    grad_inputs, sums, out_done, query_done, key_done, value_done,
    qkv, parts, *scratch,
):
    me = Place(dp_total)
    at, cut = pieces(x.shape[0]), Cut(scratch)
    scatter = Scatter(me, parts, *cut.take(8))
    first, second = WeightScatter(me, out, *cut.take(8)), WeightScatter(me, qkv, *cut.take(8))
    vectors = SumAll(me, *cut.take(4))
    block = column_blocks_of(x.shape[1])
    me.greet()
    first.start()

    @pl.loop(0, qkv.shape[0] // 256)
    def _(n):
        qkv[pl.ds(pl.multiple_of(n * 256, 256), 256)] = dot(whole[:, block(n)], grad_qkv[...], TN).astype(LOW)

    second.start()

    @pl.loop(0, x.shape[1] // 256)
    def _(n):
        total = dot(grad_qkv[...], qkv_whole[pl.ds(pl.multiple_of(n * 256, 256), 256)], NT)
        parts[:, :, :, block(n)] = total.astype(LOW).reshape(*parts.shape[:3], 256)

    scatter.start()
    scatter.spread()
    first.spread(1, me.lines)
    scatter.turn()
    vectors.held[0] = early[...]

    @pl.loop(0, NC)
    def _(j):
        unit_rows, inverse = unit_of(x[at(j)])
        e = scatter.result(j)
        grad_inputs[at(j)] = grad_resid[at(j)] + back_of(e, unit_rows, inverse, gain[...])
        vectors.held[0, 0:1] += jnp.sum(e * unit_rows, axis=0, keepdims=True)
        vectors.held[0, 1:2] += jnp.sum(e, axis=0, keepdims=True)

    second.spread(1, me.lines)
    sums[...] = vectors.run(6)
    scatter.finish()
    first.finish(store_rows(out_done))
    second.finish(store_columns(query_done, key_done, value_done))


VMEM = pl.BlockSpec(memory_space=pltpu.VMEM)
ANY = pl.BlockSpec(memory_space=pl.ANY)


def call(kernel, number, ins, in_specs, outs, out_specs, scratch, aliases=None):
    return pl.pallas_call(
        functools.partial(kernel, lax.axis_size("dp")),
        out_shape=outs,
        in_specs=in_specs,
        out_specs=out_specs,
        scratch_shapes=scratch,
        input_output_aliases=aliases or {},
        compiler_params=pltpu.CompilerParams(
            collective_id=number, has_side_effects=True, vmem_limit_bytes=60 << 20
        ),
        cost_estimate=pl.CostEstimate(flops=0, bytes_accessed=100_000_000, transcendentals=0),
    )(*ins)


def like(*shape, dtype=F32):
    return jax.ShapeDtypeStruct(shape, dtype)


def local(
    inputs,
    grad_output,
    seg_ids,
    positions,
    norm1_gain,
    norm1_bias,
    query_weight,
    query_bias,
    key_weight,
    value_weight,
    value_bias,
    out_weight,
    out_bias,
    norm2_gain,
    norm2_bias,
    up_weight,
    up_bias,
    down_weight,
    down_bias,
):
    dp_total = lax.axis_size("dp")
    tensor_total = lax.axis_size("tensor")
    lines = dp_total // 2
    place = lax.axis_index("dp")
    side = (place >> 1) & 1

    def own_half(vector):
        return lax.dynamic_slice_in_dim(vector, side * (vector.shape[0] // 2), vector.shape[0] // 2, 0)

    def mm(left, right):
        return jnp.dot(left, right, preferred_element_type=F32)

    def mm_nt(left, right):
        return jnp.einsum("td,fd->tf", left, right, preferred_element_type=F32)

    def mm_tn(left, right):
        return jnp.einsum("ta,tb->ab", left, right, preferred_element_type=F32)

    rows, width = inputs.shape
    row = lambda vector: vector.reshape(1, -1)
    group = like(2, tensor_total, rows, width, dtype=LOW)
    own = pltpu.VMEM((rows, width), LOW)
    token_scratch = Scatter.scratch(rows, width)

    slab = lambda *shape: pltpu.VMEM(shape, LOW)
    head_width, hidden = query_weight.shape[1] // 2, up_weight.shape[1] // 2
    high, wide = up_weight.shape[0], down_weight.shape[1]
    tokens = 2 * tensor_total * rows

    def side_by_side(whole):
        return whole if whole.ndim == 2 else whole.transpose(1, 0, 2).reshape(whole.shape[1], -1)

    def column_blocks(partial):
        return partial.reshape(-1, dp_total, wide).transpose(1, 0, 2) if wide % 128 else partial

    info = jnp.pad(jnp.stack([seg_ids, positions]), ((0, 6), (0, 0)))
    heads = like(tokens, head_width, dtype=LOW)

    whole1, grad_whole, qkv_full, o_full, up_part, parts, queries, keys, values, attended, infos = call(
        head_kernel, 1,
        (
            inputs, row(norm1_gain), row(norm1_bias), grad_output, query_weight, key_weight, value_weight, out_weight,
            up_weight, row(own_half(query_bias)), row(own_half(value_bias)), info,
        ),
        [VMEM] * 12,
        (
            group, group, like(width, 3 * head_width, dtype=LOW), like(width, head_width, dtype=LOW),
            like(width, hidden, dtype=LOW), group, heads, heads, heads, heads, like(2, *info.shape, dtype=jnp.int32),
        ),
        (ANY,) * 5 + (VMEM,) * 6,
        [
            own, own, slab(*group.shape), slab(2, high, 3 * head_width), slab(2, wide, head_width),
            slab(2, high, hidden), slab(width, 3 * head_width), slab(width, head_width), slab(2, GROUP, GROUP),
        ]
        + Gather.SEMS * 2 + WeightGather.sems(lines) * 3 + [grid_of(5)],
    )
    resid, whole2, up_full, down_full = call(
        middle_kernel, 2,
        (parts, inputs, row(out_bias), row(norm2_gain), row(norm2_bias), up_weight, down_weight, up_part),
        [ANY] + [VMEM] * 6 + [ANY],
        (
            like(rows, width), group, like(width, hidden, dtype=LOW),
            like(*((dp_total, hidden, wide) if wide % 128 else (hidden, width)), dtype=LOW),
        ),
        (VMEM, ANY, ANY, ANY),
        [own, slab(2, high, hidden), slab(2, hidden, wide)]
        + token_scratch + Gather.SEMS + WeightGather.sems(lines) * 2,
        {7: 2},
    )
    grad_whole = grad_whole.reshape(-1, width)
    whole2, down_full = whole2.reshape(-1, width), side_by_side(down_full)
    pre_act = mm(whole2, up_full) + own_half(up_bias)
    cumulative, slope = gelu_parts(pre_act)
    activated = (pre_act * cumulative).astype(LOW)
    grad_down = column_blocks(mm_tn(activated, grad_whole).astype(LOW))
    lowered = mm(activated, down_full).astype(LOW).reshape(group.shape)
    grad_pre = (mm_nt(grad_whole, down_full) * slope).astype(LOW)
    grad_parts = mm_nt(grad_pre, up_full).astype(LOW).reshape(group.shape)

    grad_resid, layer_output, sums2, down_done, up_done, grad_qkv, grad_out = call(
        turn_kernel, 3,
        (
            grad_parts, lowered, resid, grad_output, row(norm2_gain), row(down_bias), grad_down, whole2, grad_pre, o_full,
            queries, keys, values, attended, infos,
        ),
        [ANY] * 2 + [VMEM] * 4 + [ANY] + [VMEM] * 8,
        (
            like(rows, width), like(rows, width), like(8, width), like(*down_weight.shape), like(*up_weight.shape),
            like(tokens, 3 * head_width, dtype=LOW), like(head_width, width, dtype=LOW),
        ),
        (VMEM,) * 7,
        [own, slab(*group.shape), slab(2, GROUP, GROUP), slab(tokens, head_width), slab(width, hidden)]
        + token_scratch * 2 + Gather.SEMS
        + WeightScatter.scratch(lines, hidden, wide) + WeightScatter.scratch(lines, high, hidden),
    )

    def spread(half):
        return jnp.where(side == jnp.arange(2)[:, None], half, 0.0).reshape(-1)

    def padded(vector):
        return row(jnp.pad(vector, (0, width - vector.shape[0])))

    biases = [spread(sums2[4, n * head_width : (n + 1) * head_width]) for n in (0, 2)]
    early = jnp.concatenate(
        [
            jnp.zeros((2, width), F32),
            sums2[:4],
            padded(spread(jnp.sum(grad_pre.astype(F32), axis=0))),
            padded(jnp.concatenate(biases)),
        ]
    )
    grad_inputs, sums, out_done, query_done, key_done, value_done = call(
        tail_kernel, 4,
        (
            inputs, row(norm1_gain), grad_resid, early, column_blocks(grad_out), whole1.reshape(-1, width), grad_qkv,
            qkv_full,
        ),
        [VMEM] * 4 + [ANY] + [VMEM] * 3,
        (like(rows, width), like(8, width), like(*out_weight.shape), *[like(*query_weight.shape)] * 3),
        (VMEM,) * 6,
        [slab(width, 3 * head_width), slab(*group.shape)]
        + token_scratch
        + WeightScatter.scratch(lines, head_width, wide) + WeightScatter.scratch(lines, high, 3 * head_width)
        + SumAll.scratch(dp_total, width),
    )
    return (
        layer_output,
        grad_inputs,
        sums[0],
        sums[1],
        query_done,
        sums[7, : 2 * head_width],
        key_done,
        value_done,
        sums[7, 2 * head_width : 4 * head_width],
        out_done,
        sums[4],
        sums[2],
        sums[3],
        up_done,
        sums[6, : up_bias.shape[0]],
        down_done,
        sums[5],
    )


def solution(mesh):
    tokens, weight, weight_t = P(("dp", "tensor"), None), P("dp", "tensor"), P("tensor", "dp")
    whole, part = P(), P("tensor")
    return jax.shard_map(
        local,
        mesh=mesh,
        in_specs=(
            tokens, tokens, P("dp"), P("dp"), whole, whole, weight, part, weight, weight, part,
            weight_t, whole, whole, whole, weight, part, weight_t, whole,
        ),
        out_specs=(
            tokens, tokens, whole, whole, weight, part, weight, weight, part, weight_t, whole,
            whole, whole, weight, part, weight_t, whole,
        ),
        check_vma=False,
    )
```

```python
import functools

import jax
import jax.numpy as jnp
from jax import lax
from jax.experimental import pallas as pl
from jax.experimental.pallas import tpu as pltpu
from jax.sharding import PartitionSpec as P

HEAD_DIM = 128
GROUP = 512
EPSILON = 1e-05
NEGATIVE = -1e30
LOW = jnp.bfloat16
F32 = jnp.float32


def gelu_parts(pre_act):
    cumulative = 0.5 * (1.0 + lax.erf(pre_act * 0.7071067811865476))
    density = jnp.exp(-0.5 * pre_act * pre_act) * 0.3989422804014327
    return cumulative, cumulative + pre_act * density


NC = 4
NW = 2
NF = 4
MESH = pl.DeviceIdType.MESH


def remote(src, dst, send, recv, peer):
    return pltpu.make_async_remote_copy(
        src_ref=src, dst_ref=dst, send_sem=send, recv_sem=recv, device_id=peer, device_id_type=MESH
    )


def grid_of(*shape):
    return pltpu.SemaphoreType.DMA(shape)


class Place:
    def __init__(self, dp_total):
        self.lines = dp_total // 2
        self.d = lax.axis_index("dp")
        self.t = lax.axis_index("tensor")
        self.lane, self.line = lax.rem(self.d, 2), lax.div(self.d, 2)
        self.side = lax.rem(self.line, 2)
        self.t_core = self.t + 1 - 2 * lax.rem(self.t, 2)
        self.t_x = lax.rem(self.t + 2, 4)
        self.t_far = lax.rem(self.t_core + 2, 4)
        self.core = (self.d, self.t_core)
        self.x = (self.d, self.t_x)
        self.y = (self.d + 1 - 2 * self.lane, self.t)
        self.z = (self.d + 2 - 4 * self.side, self.t)

    def ahead(self, k):
        return lax.rem(self.line + k, self.lines)

    def behind(self, k):
        return lax.rem(self.line + self.lines - k, self.lines)

    def mate(self, line):
        return (2 * line + self.lane, self.t)

    def greet(self):
        barrier = pltpu.get_barrier_semaphore()
        for peer in (self.core, self.x, self.y):
            pl.semaphore_signal(barrier, inc=1, device_id=peer, device_id_type=MESH)

        @pl.loop(1, self.lines)
        def _(k):
            pl.semaphore_signal(barrier, inc=1, device_id=self.mate(self.ahead(k)), device_id_type=MESH)

        pl.semaphore_wait(barrier, 2 + self.lines)


class Gather:
    SEMS = [grid_of(7, NC), grid_of(7, NC), grid_of(NC)]

    def __init__(self, me, own, whole, send, recv, keep):
        self.me, self.own, self.whole = me, own, whole
        self.send, self.recv, self.keep = send, recv, keep
        self.rows = own.shape[0] // NC

    def at(self, side, t, j):
        return self.whole.at[side, t, pl.ds(j * self.rows, self.rows)]

    def piece(self, j):
        return self.own.at[pl.ds(j * self.rows, self.rows)]

    def copy(self, kind, j, src, dst, peer):
        return remote(src, dst, self.send.at[kind, j], self.recv.at[kind, j], peer)

    def local(self, j):
        return pltpu.make_async_copy(self.piece(j), self.at(0, self.me.t, j), self.keep.at[j])

    def start(self, j):
        me = self.me
        self.copy(2, j, self.piece(j), self.at(1, me.t, j), me.z).start()
        self.copy(1, j, self.piece(j), self.at(0, me.t, j), me.x).start()
        self.copy(0, j, self.piece(j), self.at(0, me.t, j), me.core).start()
        self.local(j).start()

    def wait_recv(self, kind, j, side, t):
        slot = self.at(side, t, j)
        self.copy(kind, j, slot, slot, self.me.core).wait_recv()

    def share(self, kind, j, side, t):
        self.wait_recv(kind, j, side, t)
        slot = self.at(side, t, j)
        self.copy(kind + 3, j, slot, slot, self.me.core).start()

    def relay(self):
        me = self.me

        @pl.loop(0, NC)
        def _(j):
            self.share(2, j, 1, me.t)
            slot = self.at(1, me.t, j)
            self.copy(3, j, slot, slot, me.x).start()
            self.share(1, j, 0, me.t_x)

    def finish(self):
        me = self.me

        @pl.loop(0, NC)
        def _(j):
            self.share(3, j, 1, me.t_x)

        @pl.loop(0, NC)
        def _(j):
            self.wait_recv(0, j, 0, me.t_core)
            self.wait_recv(4, j, 0, me.t_far)
            self.wait_recv(5, j, 1, me.t_core)
            self.wait_recv(6, j, 1, me.t_far)
            self.local(j).wait()
            for kind in range(7):
                self.copy(kind, j, self.piece(j), self.piece(j), me.core).wait_send()


class Scatter:
    SEMS = [grid_of(4, NC), grid_of(4, NC), grid_of(4, NC), grid_of(3, NC), grid_of(3, NC)]

    @staticmethod
    def scratch(rows, width, loaded=True):
        if loaded:
            return [pltpu.VMEM((n, rows, width), LOW) for n in (4, 4, 3)] + Scatter.SEMS
        return [pltpu.VMEM((n, rows, width), LOW) for n in (4, 3)] + Scatter.SEMS[1:]

    def __init__(self, me, parts, *scratch):
        self.me, self.parts = me, parts
        self.held, self.load = None, None
        if len(scratch) == 8:
            self.held, self.came, self.hops, self.load, *scratch = scratch
        else:
            self.came, self.hops, *scratch = scratch
        self.send, self.recv, self.hop_send, self.hop_recv = scratch
        self.rows = self.came.shape[1] // NC
        self.pairs = [
            (0, me.t, me.t_core),
            (0, me.t_x, me.t_far),
            (1, me.t, me.t_core),
            (1, me.t_x, me.t_far),
        ]

    def span(self, j):
        return pl.ds(j * self.rows, self.rows)

    def core_copy(self, i, j):
        side, _, theirs = self.pairs[i]
        return remote(
            self.parts.at[side, theirs, self.span(j)],
            self.came.at[i, self.span(j)],
            self.send.at[i, j],
            self.recv.at[i, j],
            self.me.core,
        )

    def slot(self, i, j):
        side, mine, _ = self.pairs[i]
        return self.parts.at[side, mine, self.span(j)] if self.held is None else self.held.at[i, self.span(j)]

    def load_copy(self, i, j):
        side, mine, _ = self.pairs[i]
        return pltpu.make_async_copy(
            self.parts.at[side, mine, self.span(j)], self.held.at[i, self.span(j)], self.load.at[i, j]
        )

    def hop(self, kind, j, src, peer):
        return remote(
            src, self.hops.at[kind, self.span(j)], self.hop_send.at[kind, j], self.hop_recv.at[kind, j], peer
        )

    def start(self):
        for i in (3, 1, 2, 0):

            @pl.loop(0, NC)
            def _(j):
                self.core_copy(i, j).start()
                if self.load is not None:
                    self.load_copy(i, j).start()

    def joined(self, i, j):
        if self.load is not None:
            self.load_copy(i, j).wait()
        self.core_copy(i, j).wait_recv()
        return self.slot(i, j)[...].astype(F32) + self.came[i, self.span(j)].astype(F32)

    def arrived(self, kind, j):
        self.hop(kind, j, self.hops.at[kind, self.span(j)], self.me.x).wait_recv()
        return self.hops[kind, self.span(j)].astype(F32)

    def spread(self):
        for kind, i in ((0, 3), (1, 1)):

            @pl.loop(0, NC)
            def _(j):
                self.slot(i, j)[...] = self.joined(i, j).astype(LOW)
                self.hop(kind, j, self.slot(i, j), self.me.x).start()

    def turn(self):
        @pl.loop(0, NC)
        def _(j):
            total = self.joined(2, j) + self.arrived(0, j)
            self.slot(2, j)[...] = total.astype(LOW)
            self.hop(2, j, self.slot(2, j), self.me.z).start()

    def result(self, j):
        return self.joined(0, j) + self.arrived(1, j) + self.arrived(2, j)

    def finish(self):
        @pl.loop(0, NC)
        def _(j):
            for i in range(4):
                self.core_copy(i, j).wait_send()
            for kind in range(3):
                self.hop(kind, j, self.hops.at[kind, self.span(j)], self.me.x).wait_send()


def block_at(ref, owner, rows, width, first=0, count=None):
    count = rows if count is None else count
    if len(ref.shape) == 3:
        return ref.at[owner, pl.ds(first, count)]
    if ref.shape[0] == rows:
        return ref.at[pl.ds(first, count), pl.ds(pl.multiple_of(owner * width, width), width)]
    return ref.at[pl.ds(pl.multiple_of(owner * rows + first, count), count)]


class WeightGather:
    @staticmethod
    def sems(lines, parts):
        return [grid_of(lines, parts)] * 4 + [grid_of(parts)]

    def __init__(self, me, halves, whole, z_send, z_recv, y_send, y_recv, keep):
        self.me, self.halves, self.whole = me, halves, whole
        self.z_send, self.z_recv, self.y_send, self.y_recv, self.keep = z_send, z_recv, y_send, y_recv, keep
        _, self.rows, self.width = halves.shape
        self.parts = keep.shape[0]
        self.count = self.rows // self.parts

    def at(self, owner, p):
        return block_at(self.whole, owner, self.rows, self.width, p * self.count, self.count)

    def piece(self, half, p):
        return self.halves.at[half, pl.ds(p * self.count, self.count)]

    def z_copy(self, k, p, src, dst, peer):
        return remote(src, dst, self.z_send.at[k, p], self.z_recv.at[k, p], peer)

    def y_copy(self, k, p, src, dst):
        return remote(src, dst, self.y_send.at[k, p], self.y_recv.at[k, p], self.me.y)

    def local(self, p):
        return pltpu.make_async_copy(self.piece(self.me.side, p), self.at(self.me.d, p), self.keep.at[p])

    def start(self, p):
        me = self.me

        @pl.loop(1, me.lines)
        def _(k):
            line = me.ahead(k)
            self.z_copy(k, p, self.piece(lax.rem(line, 2), p), self.at(me.d, p), me.mate(line)).start()

        self.y_copy(0, p, self.piece(me.side, p), self.at(me.d, p)).start()
        self.local(p).start()

    def forward(self, p):
        me = self.me

        @pl.loop(1, me.lines)
        def _(k):
            slot = self.at(2 * me.behind(k) + me.lane, p)
            self.z_copy(k, p, slot, slot, me.y).wait_recv()
            self.y_copy(k, p, slot, slot).start()

    def finish(self):
        me = self.me
        for p in range(self.parts):

            @pl.loop(0, me.lines)
            def _(k):
                slot = self.at(2 * me.behind(k) + 1 - me.lane, p)
                self.y_copy(k, p, slot, slot).wait()

            @pl.loop(1, me.lines)
            def _(k):
                slot = self.at(me.d, p)
                self.z_copy(k, p, slot, slot, me.y).wait_send()

            self.local(p).wait()


class WeightScatter:
    @staticmethod
    def scratch(lines, rows, width):
        return [pltpu.VMEM((lines, rows, width), LOW)] * 3 + [grid_of(lines)] * 5

    def __init__(self, me, parts, held, came, hops, load, y_send, y_recv, z_send, z_recv):
        self.me, self.parts, self.held, self.came, self.hops = me, parts, held, came, hops
        self.load, self.y_send, self.y_recv, self.z_send, self.z_recv = load, y_send, y_recv, z_send, z_recv
        _, self.rows, self.width = held.shape
        self.step = 32

    def y_copy(self, k):
        src = block_at(self.parts, 2 * self.me.ahead(k) + 1 - self.me.lane, self.rows, self.width)
        return remote(src, self.came.at[k], self.y_send.at[k], self.y_recv.at[k], self.me.y)

    def load_copy(self, k):
        src = block_at(self.parts, 2 * self.me.ahead(k) + self.me.lane, self.rows, self.width)
        return pltpu.make_async_copy(src, self.held.at[k], self.load.at[k])

    def z_copy(self, k, peer):
        return remote(self.held.at[k], self.hops.at[k], self.z_send.at[k], self.z_recv.at[k], peer)

    def start(self):
        @pl.loop(1, self.me.lines + 1)
        def _(n):
            k = lax.rem(n, self.me.lines)
            self.y_copy(k).start()
            self.load_copy(k).start()

    def joined(self, k, at):
        return self.held[k, at].astype(F32) + self.came[k, at].astype(F32)

    def spread(self, first, last):
        @pl.loop(first, last)
        def _(k):
            self.load_copy(k).wait()
            self.y_copy(k).wait_recv()

            @pl.loop(0, self.rows, step=self.step)
            def _(row):
                at = pl.ds(row, self.step)
                self.held[k, at] = self.joined(k, at).astype(LOW)

            self.z_copy(k, self.me.mate(self.me.ahead(k))).start()

    def finish(self, store):
        me = self.me
        self.load_copy(0).wait()
        self.y_copy(0).wait_recv()

        @pl.loop(1, me.lines)
        def _(k):
            self.z_copy(k, me.y).wait_recv()

        @pl.loop(0, self.rows, step=self.step)
        def _(row):
            at = pl.ds(row, self.step)
            same, other = self.joined(0, at), self.hops[1, at].astype(F32)
            for k in range(2, me.lines):
                if k % 2:
                    other = other + self.hops[k, at].astype(F32)
                else:
                    same = same + self.hops[k, at].astype(F32)
            store(me.side, at, same)
            store(1 - me.side, at, other)

        @pl.loop(0, me.lines)
        def _(k):
            self.y_copy(k).wait_send()

        @pl.loop(1, me.lines)
        def _(k):
            self.z_copy(k, me.y).wait_send()


def store_columns(*outs):
    def store(half, at, value):
        width = outs[0].shape[1] // 2
        for n, out in enumerate(outs):
            out[at, pl.ds(pl.multiple_of(half * width, width), width)] = value[:, n * width : (n + 1) * width]

    return store


def store_rows(out):
    def store(half, at, value):
        out[pl.ds(pl.multiple_of(half * (out.shape[0] // 2) + at.start, at.size), at.size)] = value

    return store


class SumAll:
    @staticmethod
    def scratch(dp_total, width):
        steps = dp_total.bit_length() + 1
        return [pltpu.VMEM((steps + 1, 8, width), F32), pltpu.VMEM((steps, 8, width), F32), grid_of(steps), grid_of(steps)]

    def __init__(self, me, held, came, send, recv):
        self.me, self.held, self.came, self.send, self.recv = me, held, came, send, recv

    def run(self, shared):
        me, peers, mask = self.me, [], 1
        while mask < 2 * me.lines:
            peers.append((me.d + mask - 2 * mask * lax.rem(lax.div(me.d, mask), 2), me.t))
            mask *= 2
        dp_steps = len(peers)
        for n, peer in enumerate(peers + [me.core, me.x]):
            copy = remote(self.held.at[n], self.came.at[n], self.send.at[n], self.recv.at[n], peer)
            copy.start()
            copy.wait()
            total = self.held[n] + self.came[n]
            if n >= dp_steps:
                row = lax.broadcasted_iota(jnp.int32, total.shape, 0)
                total = jnp.where(row < shared, total, self.held[n])
            self.held[n + 1] = total
        return self.held[dp_steps + 2]


def unit_of(rows):
    centred = rows - jnp.mean(rows, axis=1, keepdims=True)
    inverse = lax.rsqrt(jnp.mean(centred * centred, axis=1, keepdims=True) + EPSILON)
    return centred * inverse, inverse


def back_of(grad_rows, unit_rows, inverse, gain):
    scaled = grad_rows * gain
    return inverse * (
        scaled
        - jnp.mean(scaled, axis=1, keepdims=True)
        - unit_rows * jnp.mean(scaled * unit_rows, axis=1, keepdims=True)
    )


def pieces(rows):
    size = rows // NC
    return lambda j: pl.ds(j * size, size)


class Cut:
    def __init__(self, refs):
        self.refs = list(refs)

    def take(self, count):
        taken, self.refs = self.refs[:count], self.refs[count:]
        return taken


NN, NT, TN = ((1,), (0,)), ((1,), (1,)), ((0,), (0,))


def dot(left, right, dims):
    return lax.dot_general(left, right, (dims, ((), ())), preferred_element_type=F32)


def column_halves(halves, *weights):
    width = weights[0].shape[1] // 2
    for n, weight in enumerate(weights):
        for half in range(2):
            halves[half, :, n * width : (n + 1) * width] = weight[:, half * width : (half + 1) * width].astype(LOW)


def row_halves(halves, weight):
    rows = weight.shape[0] // 2
    for half in range(2):
        halves[half] = weight[half * rows : (half + 1) * rows].astype(LOW)


def turned_halves(halves, weight):
    rows = weight.shape[0] // 2
    for half in range(2):
        halves[half] = weight[half * rows : (half + 1) * rows].T.astype(LOW)


def fill_mask(mask, infos, turned):
    @pl.loop(0, 2)
    def _(side):
        across = infos[side].astype(F32)
        down = across.T
        seg_row, pos_row, seg_col, pos_col = down[:, 0:1], down[:, 1:2], across[0:1], across[1:2]
        if turned:
            seg_q, pos_q, seg_k, pos_k = seg_col, pos_col, seg_row, pos_row
        else:
            seg_q, pos_q, seg_k, pos_k = seg_row, pos_row, seg_col, pos_col
        allowed = (pos_k <= pos_q) & ((seg_k == seg_q) | (seg_k == 0.0))
        mask[side] = jnp.where(allowed, 0.0, NEGATIVE).astype(LOW)


def heads_of(width):
    return [slice(n * HEAD_DIM, (n + 1) * HEAD_DIM) for n in range(width // HEAD_DIM)]


def attend(queries, keys, values, mask, attended, between):
    group = mask.shape[1]
    part = group // 2
    for side in range(2):
        for head in heads_of(queries.shape[1]):
            all_rows = pl.ds(side * group, group)

            @pl.loop(0, 2)
            def _(r):
                at = pl.ds(side * group + r * part, part)
                scores = dot(queries[at, head], keys[all_rows, head], NT) * (HEAD_DIM**-0.5)
                scores = scores + mask[side, pl.ds(r * part, part)].astype(F32)
                terms = jnp.exp(scores - jnp.max(scores, axis=1, keepdims=True))
                probs = (terms / jnp.sum(terms, axis=1, keepdims=True)).astype(LOW)
                attended[at, head] = dot(probs, values[all_rows, head], NN).astype(LOW)

            between()


def attend_back(queries, keys, values, grads, mask, grad_qkv, between):
    group, width = mask.shape[1], queries.shape[1]
    part = group // 2
    scale = HEAD_DIM**-0.5
    for side in range(2):
        for n, head in enumerate(heads_of(width)):
            rows = pl.ds(side * group, group)
            grad_key, grad_value = 0.0, 0.0
            for r in range(2):
                at = pl.ds(side * group + r * part, part)
                scores = dot(keys[rows, head], queries[at, head], NT) * scale
                scores = scores + mask[side, :, r * part : (r + 1) * part].astype(F32)
                terms = jnp.exp(scores - jnp.max(scores, axis=0, keepdims=True))
                probs = terms / jnp.sum(terms, axis=0, keepdims=True)
                grad_probs = dot(values[rows, head], grads[at, head], NT)
                delta = jnp.sum(probs * grad_probs, axis=0, keepdims=True)
                grad_scores = (probs * (grad_probs - delta)).astype(LOW)
                grad_value = grad_value + dot(probs.astype(LOW), grads[at, head], NN)
                grad_key = grad_key + dot(grad_scores, queries[at, head], NN)
                grad_query = dot(grad_scores, keys[rows, head], TN)
                grad_qkv[at, n * HEAD_DIM : (n + 1) * HEAD_DIM] = (grad_query * scale).astype(LOW)
            for m, value in ((1, grad_key * scale), (2, grad_value)):
                grad_qkv[rows, m * width + n * HEAD_DIM : m * width + (n + 1) * HEAD_DIM] = value.astype(LOW)
            between()


def column_blocks_of(width, size=256):
    return lambda n: pl.ds(pl.multiple_of(n * size, size), size)


def half_of(ref, side):
    width = ref.shape[1] // 2
    return ref[:, pl.ds(pl.multiple_of(side * width, width), width)]


def front_kernel(
    dp_total, x, gain1, shift1, grad, query, key, value, out, up, down, query_bias, value_bias, seg, pos,
    out_bias, gain2, shift2, up_bias,
    whole1_out, whole2_out, grad_out, qkv_out, o_out, up_out, down_whole, active_out, slope_out, grad_down_out,
    queries, keys, values, attended, infos, resid,
    own1, own2, own_grad, whole1, whole2, whole_grad, qkv_half, out_half, up_half, down_half,
    qkv_whole, o_whole, up_whole, mask, parts, active, slope, grad_down, *scratch,
):
    me = Place(dp_total)
    at, cut, block = pieces(x.shape[0]), Cut(scratch), column_blocks_of(x.shape[1])
    gather1, gather2 = Gather(me, own1, whole1, *cut.take(3)), Gather(me, own2, whole2, *cut.take(3))
    gather_grad = Gather(me, own_grad, whole_grad, *cut.take(3))
    first, second = WeightGather(me, qkv_half, qkv_whole, *cut.take(5)), WeightGather(me, out_half, o_whole, *cut.take(5))
    third, fourth = WeightGather(me, up_half, up_whole, *cut.take(5)), WeightGather(me, down_half, down_whole, *cut.take(5))
    scatter = Scatter(me, parts, *cut.take(6))
    (save,) = cut.take(1)
    saved = []

    def store(source, target):
        saved.append(pltpu.make_async_copy(source, target, save.at[2 + len(saved)]))
        saved[-1].start()

    infos[0] = jnp.zeros(infos.shape[1:], jnp.int32)
    infos[0, 0:1], infos[0, 1:2] = seg[...], pos[...]
    me.greet()
    info_copy = remote(infos.at[0], infos.at[1], save.at[0], save.at[1], me.z)
    info_copy.start()

    @pl.loop(0, NC)
    def _(j):
        unit_rows, _ = unit_of(x[at(j)])
        own1[at(j)] = (unit_rows * gain1[...] + shift1[...]).astype(LOW)
        gather1.start(j)

    column_halves(qkv_half, query, key, value)
    for p in range(NW):
        first.start(p)
    turned_halves(out_half, out)
    for p in range(NW):
        second.start(p)
    column_halves(up_half, up)
    third.start(0)
    third.start(1)
    row_halves(down_half, down)

    @pl.loop(0, NC)
    def _(j):
        own_grad[at(j)] = grad[at(j)].astype(LOW)

    info_copy.wait()
    fill_mask(mask, infos, False)
    gather1.relay()
    first.forward(0)

    @pl.loop(0, NC)
    def _(j):
        gather_grad.start(j)

    gather1.finish()
    store(whole1, whole1_out)
    first.forward(1)
    first.finish()
    store(qkv_whole, qkv_out)
    group = mask.shape[1]
    width = queries.shape[1]

    @pl.loop(0, 2)
    def _(side):
        rows = pl.ds(pl.multiple_of(side * group, group), group)
        tokens = whole1[side].reshape(group, -1)
        for n, (result, bias) in enumerate(((queries, query_bias), (keys, None), (values, value_bias))):
            total = dot(tokens, qkv_whole[:, n * width : (n + 1) * width], NN)
            result[rows] = (total if bias is None else total + half_of(bias, me.side)).astype(LOW)

    for p in range(NW):
        second.forward(p)
    steps = iter((None, None, lambda: third.forward(0), lambda: third.start(2)))

    def between():
        step = next(steps, None)
        if step:
            step()

    attend(queries, keys, values, mask, attended, between)
    second.finish()
    store(o_whole, o_out)

    @pl.loop(0, x.shape[1] // 256)
    def _(n):
        total = dot(attended[...], o_whole[pl.ds(pl.multiple_of(n * 256, 256), 256)], NT)
        parts[:, :, :, block(n)] = total.astype(LOW).reshape(*parts.shape[:3], 256)

    scatter.start()
    third.forward(1)
    scatter.spread()
    scatter.turn()
    third.start(3)
    third.forward(2)

    @pl.loop(0, NC)
    def _(j):
        rows = x[at(j)] + scatter.result(j) + out_bias[...]
        resid[at(j)] = rows
        unit_rows, _ = unit_of(rows)
        own2[at(j)] = (unit_rows * gain2[...] + shift2[...]).astype(LOW)
        gather2.start(j)

    fourth.start(0)
    fourth.start(1)
    third.forward(3)
    gather2.relay()
    fourth.start(2)
    fourth.start(3)
    gather_grad.relay()
    fourth.forward(0)
    gather2.finish()
    store(whole2, whole2_out)
    third.finish()
    store(up_whole, up_out)

    def activate(first_block, last_block):
        @pl.loop(first_block, last_block)
        def _(n):
            bias = up_bias[:, pl.ds(pl.multiple_of(me.side * active.shape[1] + n * 256, 256), 256)]

            @pl.loop(0, 2)
            def _(side):
                rows = pl.ds(pl.multiple_of(side * group, group), group)
                pre_act = dot(whole2[side].reshape(group, -1), up_whole[:, block(n)], NN) + bias
                cumulative, rise = gelu_parts(pre_act)
                active[rows, block(n)] = (pre_act * cumulative).astype(LOW)
                slope[rows, block(n)] = rise.astype(LOW)

    hidden_blocks = active.shape[1] // 256
    activate(0, hidden_blocks // 2)
    fourth.forward(1)
    activate(hidden_blocks // 2, hidden_blocks)
    store(active, active_out)
    store(slope, slope_out)
    gather_grad.finish()
    store(whole_grad, grad_out)

    def product(first_block, last_block):
        @pl.loop(first_block, last_block)
        def _(n):
            total = dot(active[:, block(n)], whole_grad[...].reshape(active.shape[0], -1), TN)
            grad_down[pl.ds(pl.multiple_of(n * 256, 256), 256)] = total.astype(LOW)

    product(0, hidden_blocks // 2)
    fourth.forward(2)
    product(hidden_blocks // 2, hidden_blocks)
    store(grad_down, grad_down_out)
    fourth.forward(3)
    scatter.finish()
    fourth.finish()
    for copy in saved:
        copy.wait()


def turn_kernel(
    dp_total, parts, lowered, resid, grad, gain, down_bias, down, whole2, grad_pre, o_whole,
    queries, keys, values, attended, infos,
    grad_resid, output, sums, down_done, up_done, grad_qkv, grad_out,
    own, whole, mask, grad_att, grad_up, *scratch,
):
    me = Place(dp_total)
    at, cut = pieces(resid.shape[0]), Cut(scratch)
    scatter, other = Scatter(me, parts, *cut.take(8)), Scatter(me, lowered, *cut.take(8))
    gather = Gather(me, own, whole, *cut.take(3))
    first, second = WeightScatter(me, down, *cut.take(8)), WeightScatter(me, grad_up, *cut.take(8))
    lines = me.lines
    block = column_blocks_of(resid.shape[1])
    me.greet()
    scatter.start()
    first.start()
    scatter.spread()
    scatter.turn()

    @pl.loop(0, grad_up.shape[0] // 256)
    def _(n):
        grad_up[pl.ds(pl.multiple_of(n * 256, 256), 256)] = dot(whole2[:, block(n)], grad_pre[...], TN).astype(LOW)

    second.start()
    first.spread(1, lines // 2)
    sums[...] = jnp.zeros_like(sums)

    @pl.loop(0, NC)
    def _(j):
        unit_rows, inverse = unit_of(resid[at(j)])
        e = scatter.result(j)
        rows = grad[at(j)] + back_of(e, unit_rows, inverse, gain[...])
        grad_resid[at(j)] = rows
        own[at(j)] = rows.astype(LOW)
        gather.start(j)
        sums[0:1] += jnp.sum(e * unit_rows, axis=0, keepdims=True)
        sums[1:2] += jnp.sum(e, axis=0, keepdims=True)
        sums[2:3] += jnp.sum(rows, axis=0, keepdims=True)
        sums[3:4] += jnp.sum(grad[at(j)], axis=0, keepdims=True)

    fill_mask(mask, infos, True)
    first.spread(lines // 2, lines)
    gather.relay()
    gather.finish()
    other.start()
    other.spread()
    mixed = whole[...].reshape(-1, whole.shape[3])
    grad_att[...] = dot(mixed, o_whole[...], NN).astype(LOW)
    steps = iter(((1, 2), (2, 3), (3, 4)) if lines == 4 else ((1, lines),))

    def between():
        span = next(steps, None)
        if span:
            second.spread(*span)

    attend_back(queries, keys, values, grad_att, mask, grad_qkv, between)
    sums[4:5, : grad_qkv.shape[1]] = jnp.sum(grad_qkv[...].astype(F32), axis=0, keepdims=True)
    other.turn()

    @pl.loop(0, resid.shape[1] // 256)
    def _(n):
        columns = whole[:, :, :, block(n)].reshape(-1, 256)
        grad_out[:, block(n)] = dot(attended[...], columns, TN).astype(LOW)

    first.finish(store_rows(down_done))

    @pl.loop(0, NC)
    def _(j):
        output[at(j)] = resid[at(j)] + other.result(j) + down_bias[...]

    scatter.finish()
    other.finish()
    second.finish(store_columns(up_done))


def tail_kernel(
    dp_total, x, gain, grad_resid, early, out, whole, grad_qkv, qkv_whole,
    grad_inputs, sums, out_done, query_done, key_done, value_done,
    qkv, parts, *scratch,
):
    me = Place(dp_total)
    at, cut = pieces(x.shape[0]), Cut(scratch)
    scatter = Scatter(me, parts, *cut.take(8))
    first, second = WeightScatter(me, out, *cut.take(8)), WeightScatter(me, qkv, *cut.take(8))
    vectors = SumAll(me, *cut.take(4))
    block = column_blocks_of(x.shape[1])
    me.greet()
    first.start()

    @pl.loop(0, qkv.shape[0] // 256)
    def _(n):
        qkv[pl.ds(pl.multiple_of(n * 256, 256), 256)] = dot(whole[:, block(n)], grad_qkv[...], TN).astype(LOW)

    second.start()

    @pl.loop(0, x.shape[1] // 256)
    def _(n):
        total = dot(grad_qkv[...], qkv_whole[pl.ds(pl.multiple_of(n * 256, 256), 256)], NT)
        parts[:, :, :, block(n)] = total.astype(LOW).reshape(*parts.shape[:3], 256)

    scatter.start()
    scatter.spread()
    first.spread(1, me.lines)
    scatter.turn()
    vectors.held[0] = early[...]

    @pl.loop(0, NC)
    def _(j):
        unit_rows, inverse = unit_of(x[at(j)])
        e = scatter.result(j)
        grad_inputs[at(j)] = grad_resid[at(j)] + back_of(e, unit_rows, inverse, gain[...])
        vectors.held[0, 0:1] += jnp.sum(e * unit_rows, axis=0, keepdims=True)
        vectors.held[0, 1:2] += jnp.sum(e, axis=0, keepdims=True)

    second.spread(1, me.lines)
    sums[...] = vectors.run(6)
    scatter.finish()
    first.finish(store_rows(out_done))
    second.finish(store_columns(query_done, key_done, value_done))


VMEM = pl.BlockSpec(memory_space=pltpu.VMEM)
ANY = pl.BlockSpec(memory_space=pl.ANY)


def call(kernel, number, ins, in_specs, outs, out_specs, scratch, aliases=None):
    return pl.pallas_call(
        functools.partial(kernel, lax.axis_size("dp")),
        out_shape=outs,
        in_specs=in_specs,
        out_specs=out_specs,
        scratch_shapes=scratch,
        input_output_aliases=aliases or {},
        compiler_params=pltpu.CompilerParams(
            collective_id=number, has_side_effects=True, vmem_limit_bytes=60 << 20
        ),
        cost_estimate=pl.CostEstimate(flops=0, bytes_accessed=100_000_000, transcendentals=0),
    )(*ins)


def like(*shape, dtype=F32):
    return jax.ShapeDtypeStruct(shape, dtype)


def local(
    inputs,
    grad_output,
    seg_ids,
    positions,
    norm1_gain,
    norm1_bias,
    query_weight,
    query_bias,
    key_weight,
    value_weight,
    value_bias,
    out_weight,
    out_bias,
    norm2_gain,
    norm2_bias,
    up_weight,
    up_bias,
    down_weight,
    down_bias,
):
    dp_total = lax.axis_size("dp")
    tensor_total = lax.axis_size("tensor")
    lines = dp_total // 2
    place = lax.axis_index("dp")
    side = (place >> 1) & 1

    def mm(left, right):
        return jnp.dot(left, right, preferred_element_type=F32)

    def mm_nt(left, right):
        return jnp.einsum("td,fd->tf", left, right, preferred_element_type=F32)

    rows, width = inputs.shape
    row = lambda vector: vector.reshape(1, -1)
    group = like(2, tensor_total, rows, width, dtype=LOW)
    own = pltpu.VMEM((rows, width), LOW)
    token_scratch = Scatter.scratch(rows, width)

    slab = lambda *shape: pltpu.VMEM(shape, LOW)
    head_width, hidden = query_weight.shape[1] // 2, up_weight.shape[1] // 2
    high, wide = up_weight.shape[0], down_weight.shape[1]
    tokens = 2 * tensor_total * rows

    def side_by_side(whole):
        return whole if whole.ndim == 2 else whole.transpose(1, 0, 2).reshape(whole.shape[1], -1)

    def column_blocks(partial):
        return partial.reshape(-1, dp_total, wide).transpose(1, 0, 2) if wide % 128 else partial

    heads = like(tokens, head_width, dtype=LOW)
    units = like(tokens, hidden, dtype=LOW)

    (
        whole1, whole2, grad_whole, qkv_full, o_full, up_full, down_full, activated, slope, grad_down,
        queries, keys, values, attended, infos, resid,
    ) = call(
        front_kernel, 1,
        (
            inputs, row(norm1_gain), row(norm1_bias), grad_output, query_weight, key_weight, value_weight, out_weight,
            up_weight, down_weight, row(query_bias), row(value_bias), row(seg_ids), row(positions),
            row(out_bias), row(norm2_gain), row(norm2_bias), row(up_bias),
        ),
        [VMEM] * 18,
        (
            group, group, group, like(width, 3 * head_width, dtype=LOW), like(width, head_width, dtype=LOW),
            like(width, hidden, dtype=LOW), like(*((dp_total, hidden, wide) if wide % 128 else (hidden, width)), dtype=LOW),
            units, units, like(hidden, width, dtype=LOW),
            heads, heads, heads, heads, like(2, 8, GROUP, dtype=jnp.int32), like(rows, width),
        ),
        (ANY,) * 10 + (VMEM,) * 6,
        [
            own, own, own, *[slab(*group.shape)] * 3,
            slab(2, high, 3 * head_width), slab(2, wide, head_width), slab(2, high, hidden), slab(2, hidden, wide),
            slab(width, 3 * head_width), slab(width, head_width), slab(width, hidden), slab(2, GROUP, GROUP),
            slab(*group.shape), slab(tokens, hidden), slab(tokens, hidden), slab(hidden, width),
        ]
        + Gather.SEMS * 3
        + WeightGather.sems(lines, NW) * 2 + WeightGather.sems(lines, NF) * 2
        + Scatter.scratch(rows, width, False) + [grid_of(12)],
    )
    grad_whole, whole2 = grad_whole.reshape(-1, width), whole2.reshape(-1, width)
    down_full, grad_down = side_by_side(down_full), column_blocks(grad_down)
    grad_pre = (mm_nt(grad_whole, down_full) * slope.astype(F32)).astype(LOW)
    grad_parts = mm_nt(grad_pre, up_full).astype(LOW).reshape(group.shape)
    lowered = mm(activated, down_full).astype(LOW).reshape(group.shape)

    grad_resid, layer_output, sums2, down_done, up_done, grad_qkv, grad_out = call(
        turn_kernel, 3,
        (
            grad_parts, lowered, resid, grad_output, row(norm2_gain), row(down_bias), grad_down, whole2, grad_pre, o_full,
            queries, keys, values, attended, infos,
        ),
        [ANY] * 2 + [VMEM] * 4 + [ANY] + [VMEM] * 8,
        (
            like(rows, width), like(rows, width), like(8, width), like(*down_weight.shape), like(*up_weight.shape),
            like(tokens, 3 * head_width, dtype=LOW), like(head_width, width, dtype=LOW),
        ),
        (VMEM,) * 7,
        [own, slab(*group.shape), slab(2, GROUP, GROUP), slab(tokens, head_width), slab(width, hidden)]
        + token_scratch * 2 + Gather.SEMS
        + WeightScatter.scratch(lines, hidden, wide) + WeightScatter.scratch(lines, high, hidden),
    )

    def spread(half):
        return jnp.where(side == jnp.arange(2)[:, None], half, 0.0).reshape(-1)

    def padded(vector):
        return row(jnp.pad(vector, (0, width - vector.shape[0])))

    biases = [spread(sums2[4, n * head_width : (n + 1) * head_width]) for n in (0, 2)]
    early = jnp.concatenate(
        [
            jnp.zeros((2, width), F32),
            sums2[:4],
            padded(spread(jnp.sum(grad_pre.astype(F32), axis=0))),
            padded(jnp.concatenate(biases)),
        ]
    )
    grad_inputs, sums, out_done, query_done, key_done, value_done = call(
        tail_kernel, 4,
        (
            inputs, row(norm1_gain), grad_resid, early, column_blocks(grad_out), whole1.reshape(-1, width), grad_qkv,
            qkv_full,
        ),
        [VMEM] * 4 + [ANY] + [VMEM] * 3,
        (like(rows, width), like(8, width), like(*out_weight.shape), *[like(*query_weight.shape)] * 3),
        (VMEM,) * 6,
        [slab(width, 3 * head_width), slab(*group.shape)]
        + token_scratch
        + WeightScatter.scratch(lines, head_width, wide) + WeightScatter.scratch(lines, high, 3 * head_width)
        + SumAll.scratch(dp_total, width),
    )
    return (
        layer_output,
        grad_inputs,
        sums[0],
        sums[1],
        query_done,
        sums[7, : 2 * head_width],
        key_done,
        value_done,
        sums[7, 2 * head_width : 4 * head_width],
        out_done,
        sums[4],
        sums[2],
        sums[3],
        up_done,
        sums[6, : up_bias.shape[0]],
        down_done,
        sums[5],
    )


def solution(mesh):
    tokens, weight, weight_t = P(("dp", "tensor"), None), P("dp", "tensor"), P("tensor", "dp")
    whole, part = P(), P("tensor")
    return jax.shard_map(
        local,
        mesh=mesh,
        in_specs=(
            tokens, tokens, P("dp"), P("dp"), whole, whole, weight, part, weight, weight, part,
            weight_t, whole, whole, whole, weight, part, weight_t, whole,
        ),
        out_specs=(
            tokens, tokens, whole, whole, weight, part, weight, weight, part, weight_t, whole,
            whole, whole, weight, part, weight_t, whole,
        ),
        check_vma=False,
    )
```

```python
import functools

import jax
import jax.numpy as jnp
from jax import lax
from jax.experimental import pallas as pl
from jax.experimental.pallas import tpu as pltpu
from jax.sharding import PartitionSpec as P

HEAD_DIM = 128
GROUP = 512
EPSILON = 1e-05
NEGATIVE = -1e30
LOW = jnp.bfloat16
F32 = jnp.float32


def gelu_parts(pre_act):
    cumulative = 0.5 * (1.0 + lax.erf(pre_act * 0.7071067811865476))
    density = jnp.exp(-0.5 * pre_act * pre_act) * 0.3989422804014327
    return cumulative, cumulative + pre_act * density


NC = 4
NW = 2
NF = 4
MESH = pl.DeviceIdType.MESH


def remote(src, dst, send, recv, peer):
    return pltpu.make_async_remote_copy(
        src_ref=src, dst_ref=dst, send_sem=send, recv_sem=recv, device_id=peer, device_id_type=MESH
    )


def grid_of(*shape):
    return pltpu.SemaphoreType.DMA(shape)


class Place:
    def __init__(self, dp_total):
        self.lines = dp_total // 2
        self.d = lax.axis_index("dp")
        self.t = lax.axis_index("tensor")
        self.lane, self.line = lax.rem(self.d, 2), lax.div(self.d, 2)
        self.side = lax.rem(self.line, 2)
        self.t_core = self.t + 1 - 2 * lax.rem(self.t, 2)
        self.t_x = lax.rem(self.t + 2, 4)
        self.t_far = lax.rem(self.t_core + 2, 4)
        self.core = (self.d, self.t_core)
        self.x = (self.d, self.t_x)
        self.y = (self.d + 1 - 2 * self.lane, self.t)
        self.z = (self.d + 2 - 4 * self.side, self.t)

    def ahead(self, k):
        return lax.rem(self.line + k, self.lines)

    def behind(self, k):
        return lax.rem(self.line + self.lines - k, self.lines)

    def mate(self, line):
        return (2 * line + self.lane, self.t)

    def greet(self):
        barrier = pltpu.get_barrier_semaphore()
        for peer in (self.core, self.x, self.y):
            pl.semaphore_signal(barrier, inc=1, device_id=peer, device_id_type=MESH)

        @pl.loop(1, self.lines)
        def _(k):
            pl.semaphore_signal(barrier, inc=1, device_id=self.mate(self.ahead(k)), device_id_type=MESH)

        pl.semaphore_wait(barrier, 2 + self.lines)


class Gather:
    SEMS = [grid_of(7, NC), grid_of(7, NC), grid_of(NC)]

    def __init__(self, me, own, whole, send, recv, keep):
        self.me, self.own, self.whole = me, own, whole
        self.send, self.recv, self.keep = send, recv, keep
        self.rows = own.shape[0] // NC

    def at(self, side, t, j):
        return self.whole.at[side, t, pl.ds(j * self.rows, self.rows)]

    def piece(self, j):
        return self.own.at[pl.ds(j * self.rows, self.rows)]

    def copy(self, kind, j, src, dst, peer):
        return remote(src, dst, self.send.at[kind, j], self.recv.at[kind, j], peer)

    def local(self, j):
        return pltpu.make_async_copy(self.piece(j), self.at(0, self.me.t, j), self.keep.at[j])

    def start(self, j):
        me = self.me
        self.copy(2, j, self.piece(j), self.at(1, me.t, j), me.z).start()
        self.copy(1, j, self.piece(j), self.at(0, me.t, j), me.x).start()
        self.copy(0, j, self.piece(j), self.at(0, me.t, j), me.core).start()
        self.local(j).start()

    def wait_recv(self, kind, j, side, t):
        slot = self.at(side, t, j)
        self.copy(kind, j, slot, slot, self.me.core).wait_recv()

    def share(self, kind, j, side, t):
        self.wait_recv(kind, j, side, t)
        slot = self.at(side, t, j)
        self.copy(kind + 3, j, slot, slot, self.me.core).start()

    def relay(self):
        me = self.me

        @pl.loop(0, NC)
        def _(j):
            self.share(2, j, 1, me.t)
            slot = self.at(1, me.t, j)
            self.copy(3, j, slot, slot, me.x).start()
            self.share(1, j, 0, me.t_x)

    def finish(self):
        me = self.me

        @pl.loop(0, NC)
        def _(j):
            self.share(3, j, 1, me.t_x)

        @pl.loop(0, NC)
        def _(j):
            self.wait_recv(0, j, 0, me.t_core)
            self.wait_recv(4, j, 0, me.t_far)
            self.wait_recv(5, j, 1, me.t_core)
            self.wait_recv(6, j, 1, me.t_far)
            self.local(j).wait()
            for kind in range(7):
                self.copy(kind, j, self.piece(j), self.piece(j), me.core).wait_send()


class Scatter:
    SEMS = [grid_of(4, NC), grid_of(4, NC), grid_of(4, NC), grid_of(3, NC), grid_of(3, NC)]

    @staticmethod
    def scratch(rows, width, loaded=True):
        if loaded:
            return [pltpu.VMEM((n, rows, width), LOW) for n in (4, 4, 3)] + Scatter.SEMS
        return [pltpu.VMEM((n, rows, width), LOW) for n in (4, 3)] + Scatter.SEMS[1:]

    def __init__(self, me, parts, *scratch):
        self.me, self.parts = me, parts
        self.held, self.load = None, None
        if len(scratch) == 8:
            self.held, self.came, self.hops, self.load, *scratch = scratch
        else:
            self.came, self.hops, *scratch = scratch
        self.send, self.recv, self.hop_send, self.hop_recv = scratch
        self.rows = self.came.shape[1] // NC
        self.pairs = [
            (0, me.t, me.t_core),
            (0, me.t_x, me.t_far),
            (1, me.t, me.t_core),
            (1, me.t_x, me.t_far),
        ]

    def span(self, j):
        return pl.ds(j * self.rows, self.rows)

    def core_copy(self, i, j):
        side, _, theirs = self.pairs[i]
        return remote(
            self.parts.at[side, theirs, self.span(j)],
            self.came.at[i, self.span(j)],
            self.send.at[i, j],
            self.recv.at[i, j],
            self.me.core,
        )

    def slot(self, i, j):
        side, mine, _ = self.pairs[i]
        return self.parts.at[side, mine, self.span(j)] if self.held is None else self.held.at[i, self.span(j)]

    def load_copy(self, i, j):
        side, mine, _ = self.pairs[i]
        return pltpu.make_async_copy(
            self.parts.at[side, mine, self.span(j)], self.held.at[i, self.span(j)], self.load.at[i, j]
        )

    def hop(self, kind, j, src, peer):
        return remote(
            src, self.hops.at[kind, self.span(j)], self.hop_send.at[kind, j], self.hop_recv.at[kind, j], peer
        )

    def start(self):
        for i in (3, 1, 2, 0):

            @pl.loop(0, NC)
            def _(j):
                self.core_copy(i, j).start()
                if self.load is not None:
                    self.load_copy(i, j).start()

    def joined(self, i, j):
        if self.load is not None:
            self.load_copy(i, j).wait()
        self.core_copy(i, j).wait_recv()
        return self.slot(i, j)[...].astype(F32) + self.came[i, self.span(j)].astype(F32)

    def arrived(self, kind, j):
        self.hop(kind, j, self.hops.at[kind, self.span(j)], self.me.x).wait_recv()
        return self.hops[kind, self.span(j)].astype(F32)

    def spread(self):
        for kind, i in ((0, 3), (1, 1)):

            @pl.loop(0, NC)
            def _(j):
                self.slot(i, j)[...] = self.joined(i, j).astype(LOW)
                self.hop(kind, j, self.slot(i, j), self.me.x).start()

    def turn(self):
        @pl.loop(0, NC)
        def _(j):
            total = self.joined(2, j) + self.arrived(0, j)
            self.slot(2, j)[...] = total.astype(LOW)
            self.hop(2, j, self.slot(2, j), self.me.z).start()

    def result(self, j):
        return self.joined(0, j) + self.arrived(1, j) + self.arrived(2, j)

    def finish(self):
        @pl.loop(0, NC)
        def _(j):
            for i in range(4):
                self.core_copy(i, j).wait_send()
            for kind in range(3):
                self.hop(kind, j, self.hops.at[kind, self.span(j)], self.me.x).wait_send()


def block_at(ref, owner, rows, width, first=0, count=None):
    count = rows if count is None else count
    if len(ref.shape) == 3:
        return ref.at[owner, pl.ds(first, count)]
    if ref.shape[0] == rows:
        return ref.at[pl.ds(first, count), pl.ds(pl.multiple_of(owner * width, width), width)]
    return ref.at[pl.ds(pl.multiple_of(owner * rows + first, count), count)]


class WeightGather:
    @staticmethod
    def sems(lines, parts):
        return [grid_of(lines, parts)] * 4 + [grid_of(parts)]

    def __init__(self, me, halves, whole, z_send, z_recv, y_send, y_recv, keep):
        self.me, self.halves, self.whole = me, halves, whole
        self.z_send, self.z_recv, self.y_send, self.y_recv, self.keep = z_send, z_recv, y_send, y_recv, keep
        _, self.rows, self.width = halves.shape
        self.parts = keep.shape[0]
        self.count = self.rows // self.parts

    def at(self, owner, p):
        return block_at(self.whole, owner, self.rows, self.width, p * self.count, self.count)

    def piece(self, half, p):
        return self.halves.at[half, pl.ds(p * self.count, self.count)]

    def z_copy(self, k, p, src, dst, peer):
        return remote(src, dst, self.z_send.at[k, p], self.z_recv.at[k, p], peer)

    def y_copy(self, k, p, src, dst):
        return remote(src, dst, self.y_send.at[k, p], self.y_recv.at[k, p], self.me.y)

    def local(self, p):
        return pltpu.make_async_copy(self.piece(self.me.side, p), self.at(self.me.d, p), self.keep.at[p])

    def start(self, p):
        me = self.me

        @pl.loop(1, me.lines)
        def _(k):
            line = me.ahead(k)
            self.z_copy(k, p, self.piece(lax.rem(line, 2), p), self.at(me.d, p), me.mate(line)).start()

        self.y_copy(0, p, self.piece(me.side, p), self.at(me.d, p)).start()
        self.local(p).start()

    def forward(self, p):
        me = self.me

        @pl.loop(1, me.lines)
        def _(k):
            slot = self.at(2 * me.behind(k) + me.lane, p)
            self.z_copy(k, p, slot, slot, me.y).wait_recv()
            self.y_copy(k, p, slot, slot).start()

    def finish(self):
        me = self.me
        for p in range(self.parts):

            @pl.loop(0, me.lines)
            def _(k):
                slot = self.at(2 * me.behind(k) + 1 - me.lane, p)
                self.y_copy(k, p, slot, slot).wait()

            @pl.loop(1, me.lines)
            def _(k):
                slot = self.at(me.d, p)
                self.z_copy(k, p, slot, slot, me.y).wait_send()

            self.local(p).wait()


class WeightScatter:
    @staticmethod
    def scratch(lines, rows, width, loaded=False):
        blocks = [pltpu.VMEM((lines, rows, width), LOW)] * (2 if loaded else 1)
        return blocks + [grid_of(lines)] * (5 if loaded else 4) + [grid_of(1)]

    def __init__(self, me, parts, hops, *scratch):
        self.me, self.parts, self.hops = me, parts, hops
        self.held, self.load = None, None
        if len(scratch) == 8:
            self.held, self.came, self.load, *scratch = scratch
        else:
            self.came, *scratch = scratch
        self.y_send, self.y_recv, self.z_send, self.z_recv, self.keep = scratch
        _, self.rows, self.width = self.came.shape
        self.step = 32

    def theirs(self, k):
        return block_at(self.parts, 2 * self.me.ahead(k) + 1 - self.me.lane, self.rows, self.width)

    def mine(self, k):
        return block_at(self.parts, 2 * self.me.ahead(k) + self.me.lane, self.rows, self.width)

    def slot(self, k):
        return self.mine(k) if self.held is None else self.held.at[k]

    def y_copy(self, k):
        return remote(self.theirs(k), self.came.at[k], self.y_send.at[k], self.y_recv.at[k], self.me.y)

    def load_copy(self, k):
        return pltpu.make_async_copy(self.mine(k), self.held.at[k], self.load.at[k])

    def z_copy(self, k, peer):
        return remote(self.slot(k), self.hops.at[k], self.z_send.at[k], self.z_recv.at[k], peer)

    def keep_copy(self):
        return pltpu.make_async_copy(self.slot(0), self.hops.at[0], self.keep.at[0])

    def start(self):
        @pl.loop(1, self.me.lines + 1)
        def _(n):
            k = lax.rem(n, self.me.lines)
            self.y_copy(k).start()
            if self.load is not None:
                self.load_copy(k).start()

    def join(self, k):
        if self.load is not None:
            self.load_copy(k).wait()
        self.y_copy(k).wait_recv()
        slot = self.slot(k)

        @pl.loop(0, self.rows, step=self.step)
        def _(row):
            at = pl.ds(pl.multiple_of(row, self.step), self.step)
            slot[at] = (slot[at].astype(F32) + self.came[k, at].astype(F32)).astype(LOW)

    def spread(self, first, last):
        @pl.loop(first, last)
        def _(k):
            self.join(k)
            self.z_copy(k, self.me.mate(self.me.ahead(k))).start()

    def own(self):
        self.join(0)
        self.keep_copy().start()

    def finish(self):
        me = self.me

        @pl.loop(1, me.lines)
        def _(k):
            self.z_copy(k, me.y).wait()

        @pl.loop(0, me.lines)
        def _(k):
            self.y_copy(k).wait_send()

        self.keep_copy().wait()


class SumAll:
    @staticmethod
    def scratch(dp_total, width):
        steps = dp_total.bit_length() + 1
        return [pltpu.VMEM((steps + 1, 8, width), F32), pltpu.VMEM((steps, 8, width), F32), grid_of(steps), grid_of(steps)]

    def __init__(self, me, held, came, send, recv):
        self.me, self.held, self.came, self.send, self.recv = me, held, came, send, recv

    def run(self, first, last, shared):
        me, mask = self.me, 1
        peers = [me.core, me.x]
        while mask < 2 * me.lines:
            peers.append((me.d + mask - 2 * mask * lax.rem(lax.div(me.d, mask), 2), me.t))
            mask *= 2
        for n in range(len(peers))[first:last]:
            copy = remote(self.held.at[n], self.came.at[n], self.send.at[n], self.recv.at[n], peers[n])
            copy.start()
            copy.wait()
            total = self.held[n] + self.came[n]
            if n < 2:
                row = lax.broadcasted_iota(jnp.int32, total.shape, 0)
                total = jnp.where(row < shared, total, self.held[n])
            self.held[n + 1] = total
        return self.held[len(peers)]


def unit_of(rows):
    centred = rows - jnp.mean(rows, axis=1, keepdims=True)
    inverse = lax.rsqrt(jnp.mean(centred * centred, axis=1, keepdims=True) + EPSILON)
    return centred * inverse, inverse


def back_of(grad_rows, unit_rows, inverse, gain):
    scaled = grad_rows * gain
    return inverse * (
        scaled
        - jnp.mean(scaled, axis=1, keepdims=True)
        - unit_rows * jnp.mean(scaled * unit_rows, axis=1, keepdims=True)
    )


def pieces(rows):
    size = rows // NC
    return lambda j: pl.ds(j * size, size)


class Cut:
    def __init__(self, refs):
        self.refs = list(refs)

    def take(self, count):
        taken, self.refs = self.refs[:count], self.refs[count:]
        return taken


NN, NT, TN = ((1,), (0,)), ((1,), (1,)), ((0,), (0,))


def dot(left, right, dims):
    return lax.dot_general(left, right, (dims, ((), ())), preferred_element_type=F32)


def column_halves(halves, *weights):
    width = weights[0].shape[1] // 2
    for n, weight in enumerate(weights):
        for half in range(2):
            halves[half, :, n * width : (n + 1) * width] = weight[:, half * width : (half + 1) * width].astype(LOW)


def row_halves(halves, weight):
    rows = weight.shape[0] // 2
    for half in range(2):
        halves[half] = weight[half * rows : (half + 1) * rows].astype(LOW)


def turned_halves(halves, weight):
    rows = weight.shape[0] // 2
    for half in range(2):
        halves[half] = weight[half * rows : (half + 1) * rows].T.astype(LOW)


def fill_mask(mask, infos, turned):
    @pl.loop(0, 2)
    def _(side):
        across = infos[side].astype(F32)
        down = across.T
        seg_row, pos_row, seg_col, pos_col = down[:, 0:1], down[:, 1:2], across[0:1], across[1:2]
        if turned:
            seg_q, pos_q, seg_k, pos_k = seg_col, pos_col, seg_row, pos_row
        else:
            seg_q, pos_q, seg_k, pos_k = seg_row, pos_row, seg_col, pos_col
        allowed = (pos_k <= pos_q) & ((seg_k == seg_q) | (seg_k == 0.0))
        mask[side] = jnp.where(allowed, 0.0, NEGATIVE).astype(LOW)


def heads_of(width):
    return [slice(n * HEAD_DIM, (n + 1) * HEAD_DIM) for n in range(width // HEAD_DIM)]


def attend(queries, keys, values, mask, attended, between):
    group = mask.shape[1]
    part = group // 2
    for side in range(2):
        for head in heads_of(queries.shape[1]):
            all_rows = pl.ds(side * group, group)

            @pl.loop(0, 2)
            def _(r):
                at = pl.ds(side * group + r * part, part)
                scores = dot(queries[at, head], keys[all_rows, head], NT) * (HEAD_DIM**-0.5)
                scores = scores + mask[side, pl.ds(r * part, part)].astype(F32)
                terms = jnp.exp(scores - jnp.max(scores, axis=1, keepdims=True))
                probs = (terms / jnp.sum(terms, axis=1, keepdims=True)).astype(LOW)
                attended[at, head] = dot(probs, values[all_rows, head], NN).astype(LOW)

            between()


def attend_back(queries, keys, values, grads, mask, grad_qkv, between):
    group, width = mask.shape[1], queries.shape[1]
    part = group // 2
    scale = HEAD_DIM**-0.5
    for side in range(2):
        for n, head in enumerate(heads_of(width)):
            rows = pl.ds(side * group, group)
            grad_key, grad_value = 0.0, 0.0
            for r in range(2):
                at = pl.ds(side * group + r * part, part)
                scores = dot(keys[rows, head], queries[at, head], NT) * scale
                scores = scores + mask[side, :, r * part : (r + 1) * part].astype(F32)
                terms = jnp.exp(scores - jnp.max(scores, axis=0, keepdims=True))
                probs = terms / jnp.sum(terms, axis=0, keepdims=True)
                grad_probs = dot(values[rows, head], grads[at, head], NT)
                delta = jnp.sum(probs * grad_probs, axis=0, keepdims=True)
                grad_scores = (probs * (grad_probs - delta)).astype(LOW)
                grad_value = grad_value + dot(probs.astype(LOW), grads[at, head], NN)
                grad_key = grad_key + dot(grad_scores, queries[at, head], NN)
                grad_query = dot(grad_scores, keys[rows, head], TN)
                grad_qkv[at, n * HEAD_DIM : (n + 1) * HEAD_DIM] = (grad_query * scale).astype(LOW)
            for m, value in ((1, grad_key * scale), (2, grad_value)):
                grad_qkv[rows, m * width + n * HEAD_DIM : m * width + (n + 1) * HEAD_DIM] = value.astype(LOW)
            between()


def column_blocks_of(width, size=256):
    return lambda n: pl.ds(pl.multiple_of(n * size, size), size)


def half_of(ref, side):
    width = ref.shape[1] // 2
    return ref[:, pl.ds(pl.multiple_of(side * width, width), width)]


def front_kernel(
    dp_total, x, gain1, shift1, grad, query, key, value, out, up, down, query_bias, value_bias, seg, pos,
    out_bias, gain2, shift2, up_bias,
    whole1_out, whole2_out, grad_out, qkv_out, o_out, up_out, down_whole, active_out, slope_out, grad_down_out,
    queries, keys, values, attended, infos, resid,
    own1, own2, own_grad, whole1, whole2, whole_grad, qkv_half, out_half, up_half, down_half,
    qkv_whole, o_whole, up_whole, mask, parts, active, slope, grad_down, *scratch,
):
    me = Place(dp_total)
    at, cut, block = pieces(x.shape[0]), Cut(scratch), column_blocks_of(x.shape[1])
    gather1, gather2 = Gather(me, own1, whole1, *cut.take(3)), Gather(me, own2, whole2, *cut.take(3))
    gather_grad = Gather(me, own_grad, whole_grad, *cut.take(3))
    first, second = WeightGather(me, qkv_half, qkv_whole, *cut.take(5)), WeightGather(me, out_half, o_whole, *cut.take(5))
    third, fourth = WeightGather(me, up_half, up_whole, *cut.take(5)), WeightGather(me, down_half, down_whole, *cut.take(5))
    scatter = Scatter(me, parts, *cut.take(6))
    (save,) = cut.take(1)
    saved = []

    def store(source, target):
        saved.append(pltpu.make_async_copy(source, target, save.at[2 + len(saved)]))
        saved[-1].start()

    infos[0] = jnp.zeros(infos.shape[1:], jnp.int32)
    infos[0, 0:1], infos[0, 1:2] = seg[...], pos[...]
    me.greet()
    info_copy = remote(infos.at[0], infos.at[1], save.at[0], save.at[1], me.z)
    info_copy.start()

    @pl.loop(0, NC)
    def _(j):
        unit_rows, _ = unit_of(x[at(j)])
        own1[at(j)] = (unit_rows * gain1[...] + shift1[...]).astype(LOW)
        gather1.start(j)

    column_halves(qkv_half, query, key, value)
    for p in range(NW):
        first.start(p)
    turned_halves(out_half, out)
    for p in range(NW):
        second.start(p)
    column_halves(up_half, up)
    third.start(0)
    third.start(1)
    row_halves(down_half, down)

    @pl.loop(0, NC)
    def _(j):
        own_grad[at(j)] = grad[at(j)].astype(LOW)

    info_copy.wait()
    fill_mask(mask, infos, False)
    gather1.relay()
    first.forward(0)

    @pl.loop(0, NC)
    def _(j):
        gather_grad.start(j)

    gather1.finish()
    store(whole1, whole1_out)
    first.forward(1)
    first.finish()
    store(qkv_whole, qkv_out)
    group = mask.shape[1]
    width = queries.shape[1]

    @pl.loop(0, 2)
    def _(side):
        rows = pl.ds(pl.multiple_of(side * group, group), group)
        tokens = whole1[side].reshape(group, -1)
        for n, (result, bias) in enumerate(((queries, query_bias), (keys, None), (values, value_bias))):
            total = dot(tokens, qkv_whole[:, n * width : (n + 1) * width], NN)
            result[rows] = (total if bias is None else total + half_of(bias, me.side)).astype(LOW)

    for p in range(NW):
        second.forward(p)
    steps = iter((None, None, lambda: third.forward(0), lambda: third.start(2)))

    def between():
        step = next(steps, None)
        if step:
            step()

    attend(queries, keys, values, mask, attended, between)
    second.finish()
    store(o_whole, o_out)

    @pl.loop(0, x.shape[1] // 256)
    def _(n):
        total = dot(attended[...], o_whole[pl.ds(pl.multiple_of(n * 256, 256), 256)], NT)
        parts[:, :, :, block(n)] = total.astype(LOW).reshape(*parts.shape[:3], 256)

    scatter.start()
    third.forward(1)
    scatter.spread()
    scatter.turn()
    third.start(3)
    third.forward(2)

    @pl.loop(0, NC)
    def _(j):
        rows = x[at(j)] + scatter.result(j) + out_bias[...]
        resid[at(j)] = rows
        unit_rows, _ = unit_of(rows)
        own2[at(j)] = (unit_rows * gain2[...] + shift2[...]).astype(LOW)
        gather2.start(j)

    fourth.start(0)
    fourth.start(1)
    third.forward(3)
    gather2.relay()
    fourth.start(2)
    fourth.start(3)
    gather_grad.relay()
    fourth.forward(0)
    gather2.finish()
    store(whole2, whole2_out)
    third.finish()
    store(up_whole, up_out)

    def activate(first_block, last_block):
        @pl.loop(first_block, last_block)
        def _(n):
            bias = up_bias[:, pl.ds(pl.multiple_of(me.side * active.shape[1] + n * 256, 256), 256)]

            @pl.loop(0, 2)
            def _(side):
                rows = pl.ds(pl.multiple_of(side * group, group), group)
                pre_act = dot(whole2[side].reshape(group, -1), up_whole[:, block(n)], NN) + bias
                cumulative, rise = gelu_parts(pre_act)
                active[rows, block(n)] = (pre_act * cumulative).astype(LOW)
                slope[rows, block(n)] = rise.astype(LOW)

    hidden_blocks = active.shape[1] // 256
    activate(0, hidden_blocks // 2)
    fourth.forward(1)
    activate(hidden_blocks // 2, hidden_blocks)
    store(active, active_out)
    store(slope, slope_out)
    gather_grad.finish()
    store(whole_grad, grad_out)

    def product(first_block, last_block):
        @pl.loop(first_block, last_block)
        def _(n):
            total = dot(active[:, block(n)], whole_grad[...].reshape(active.shape[0], -1), TN)
            grad_down[pl.ds(pl.multiple_of(n * 256, 256), 256)] = total.astype(LOW)

    product(0, hidden_blocks // 2)
    fourth.forward(2)
    product(hidden_blocks // 2, hidden_blocks)
    store(grad_down, grad_down_out)
    fourth.forward(3)
    scatter.finish()
    fourth.finish()
    for copy in saved:
        copy.wait()


def back_kernel(
    dp_total, grad_parts, lowered, down, whole2, whole1, grad_pre_in, resid, grad, gain2, down_bias, o_whole,
    queries, keys, values, attended, infos, x, gain1, qkv_whole,
    down_hops, up_hops, out_hops, qkv_hops, output, grad_inputs, sums,
    own, tokens, whole, mask, grad_att, grad_up, shared, grad_out, qkv, *scratch,
):
    me = Place(dp_total)
    at, cut, block = pieces(x.shape[0]), Cut(scratch), column_blocks_of(x.shape[1])
    scatter, other = Scatter(me, grad_parts, *cut.take(8)), Scatter(me, lowered, *cut.take(8))
    last, gather = Scatter(me, whole, *cut.take(6)), Gather(me, own, whole, *cut.take(3))
    first = WeightScatter(me, down, down_hops, *cut.take(8))
    second = WeightScatter(me, grad_up, up_hops, *cut.take(6))
    third = WeightScatter(me, grad_out, out_hops, *cut.take(6))
    fourth = WeightScatter(me, qkv, qkv_hops, *cut.take(6))
    vectors = SumAll(me, *cut.take(4))
    (load,) = cut.take(1)
    start = vectors.held.at[0]
    lines, hidden, head_width = me.lines, grad_up.shape[1], queries.shape[1]
    grad_pre, grad_qkv = shared.at[:, :hidden], shared.at[:, : 3 * head_width]
    me.greet()
    load2 = pltpu.make_async_copy(whole2, tokens, load.at[0])
    load1 = pltpu.make_async_copy(whole1, tokens, load.at[1])
    load3 = pltpu.make_async_copy(grad_pre_in, grad_pre, load.at[2])
    load2.start()
    load3.start()
    scatter.start()
    first.start()
    scatter.spread()
    load2.wait()
    load3.wait()
    row_blocks = grad_up.shape[0] // 256

    def up_product(first_block, last_block):
        @pl.loop(first_block, last_block)
        def _(n):
            total = dot(tokens[:, block(n)], grad_pre[...], TN)
            grad_up[pl.ds(pl.multiple_of(n * 256, 256), 256)] = total.astype(LOW)

    up_product(0, row_blocks // 2)
    scatter.turn()
    up_product(row_blocks // 2, row_blocks)
    second.start()
    load1.start()
    first.spread(1, lines // 2)
    start[...] = jnp.zeros_like(start)

    @pl.loop(0, hidden // 256)
    def _(n):
        columns = pl.ds(pl.multiple_of(me.side * hidden + n * 256, 256), 256)
        start[6:7, columns] = jnp.sum(grad_pre[:, block(n)].astype(F32), axis=0, keepdims=True)

    @pl.loop(0, NC)
    def _(j):
        unit_rows, inverse = unit_of(resid[at(j)])
        e = scatter.result(j)
        rows = grad[at(j)] + back_of(e, unit_rows, inverse, gain2[...])
        grad_inputs[at(j)] = rows
        own[at(j)] = rows.astype(LOW)
        gather.start(j)
        start[2:3] += jnp.sum(e * unit_rows, axis=0, keepdims=True)
        start[3:4] += jnp.sum(e, axis=0, keepdims=True)
        start[4:5] += jnp.sum(rows, axis=0, keepdims=True)
        start[5:6] += jnp.sum(grad[at(j)], axis=0, keepdims=True)

    fill_mask(mask, infos, True)
    first.spread(lines // 2, lines)
    gather.relay()
    gather.finish()
    other.start()
    other.spread()
    mixed = whole[...].reshape(-1, whole.shape[3])
    grad_att[...] = dot(mixed, o_whole[...], NN).astype(LOW)
    steps = iter((None, lambda: second.spread(1, lines // 2), None, lambda: first.own()))

    def between():
        step = next(steps, None)
        if step:
            step()

    attend_back(queries, keys, values, grad_att, mask, grad_qkv, between)

    for n in (0, 2):
        total = jnp.sum(grad_qkv[:, n * head_width : (n + 1) * head_width].astype(F32), axis=0, keepdims=True)
        start[7:8, pl.ds(pl.multiple_of((n + me.side) * head_width, head_width), head_width)] = total

    wide = third.width

    @pl.loop(0, x.shape[1] // 256)
    def _(n):
        columns = whole[:, :, :, block(n)].reshape(-1, 256)
        total = dot(attended[...], columns, TN).astype(LOW)
        if wide % 128:
            for i in range(256 // wide):
                grad_out[n * (256 // wide) + i] = total[:, i * wide : (i + 1) * wide]
        else:
            grad_out[:, block(n)] = total

    second.spread(lines // 2, lines - 1)
    third.start()
    load1.wait()

    @pl.loop(0, qkv.shape[0] // 256)
    def _(n):
        qkv[pl.ds(pl.multiple_of(n * 256, 256), 256)] = dot(tokens[:, block(n)], grad_qkv[...], TN).astype(LOW)

    fourth.start()
    other.turn()

    @pl.loop(0, x.shape[1] // 256)
    def _(n):
        total = dot(grad_qkv[...], qkv_whole[pl.ds(pl.multiple_of(n * 256, 256), 256)], NT)
        whole[:, :, :, block(n)] = total.astype(LOW).reshape(*whole.shape[:3], 256)

    last.start()
    second.spread(lines - 1, lines)
    last.spread()
    last.turn()
    second.own()

    @pl.loop(0, NC)
    def _(j):
        output[at(j)] = resid[at(j)] + other.result(j) + down_bias[...]

    third.spread(1, lines)
    third.own()

    @pl.loop(0, NC)
    def _(j):
        unit_rows, inverse = unit_of(x[at(j)])
        e = last.result(j)
        grad_inputs[at(j)] += back_of(e, unit_rows, inverse, gain1[...])
        start[0:1] += jnp.sum(e * unit_rows, axis=0, keepdims=True)
        start[1:2] += jnp.sum(e, axis=0, keepdims=True)

    vectors.run(0, 2, 6)
    fourth.spread(1, lines)
    fourth.own()
    sums[...] = vectors.run(2, None, 6)
    for part in (scatter, other, last, first, second, third, fourth):
        part.finish()


def final_kernel(
    lines, down_hops, up_hops, out_hops, qkv_hops, rows_in, grads_in, sums,
    output, grad_inputs, down, up, out, query, key, value, *vectors,
):
    side = lax.rem(lax.div(lax.axis_index("dp"), 2), 2)

    def half_sums(hops):
        same, opposite = hops[0].astype(F32), hops[1].astype(F32)
        for k in range(2, lines):
            if k % 2:
                opposite = opposite + hops[k].astype(F32)
            else:
                same = same + hops[k].astype(F32)
        return (side, same), (1 - side, opposite)

    for half, total in half_sums(down_hops):
        down[half] = total
    for half, total in half_sums(out_hops):
        out[half] = total
    for half, total in half_sums(up_hops):
        width = total.shape[1]
        up[:, pl.ds(pl.multiple_of(half * width, width), width)] = total
    for half, total in half_sums(qkv_hops):
        width = total.shape[1] // 3
        for n, ref in enumerate((query, key, value)):
            ref[:, pl.ds(pl.multiple_of(half * width, width), width)] = total[:, n * width : (n + 1) * width]
    output[...], grad_inputs[...] = rows_in[...], grads_in[...]
    first = 0
    for n, ref in enumerate(vectors):
        if n < 7:
            ref[...] = sums[n : n + 1, : ref.shape[1]]
        else:
            ref[...] = sums[7:8, first : first + ref.shape[1]]
            first += ref.shape[1]


VMEM = pl.BlockSpec(memory_space=pltpu.VMEM)
ANY = pl.BlockSpec(memory_space=pl.ANY)


def call(kernel, number, ins, in_specs, outs, out_specs, scratch, limit=60):
    return pl.pallas_call(
        functools.partial(kernel, lax.axis_size("dp")),
        out_shape=outs,
        in_specs=in_specs,
        out_specs=out_specs,
        scratch_shapes=scratch,
        compiler_params=pltpu.CompilerParams(
            collective_id=number, has_side_effects=True, vmem_limit_bytes=limit << 20
        ),
        cost_estimate=pl.CostEstimate(flops=0, bytes_accessed=100_000_000, transcendentals=0),
    )(*ins)


def like(*shape, dtype=F32):
    return jax.ShapeDtypeStruct(shape, dtype)


def local(
    inputs,
    grad_output,
    seg_ids,
    positions,
    norm1_gain,
    norm1_bias,
    query_weight,
    query_bias,
    key_weight,
    value_weight,
    value_bias,
    out_weight,
    out_bias,
    norm2_gain,
    norm2_bias,
    up_weight,
    up_bias,
    down_weight,
    down_bias,
):
    dp_total = lax.axis_size("dp")
    tensor_total = lax.axis_size("tensor")
    lines = dp_total // 2
    place = lax.axis_index("dp")
    side = (place >> 1) & 1

    def mm(left, right):
        return jnp.dot(left, right, preferred_element_type=F32)

    def mm_nt(left, right):
        return jnp.einsum("td,fd->tf", left, right, preferred_element_type=F32)

    rows, width = inputs.shape
    row = lambda vector: vector.reshape(1, -1)
    group = like(2, tensor_total, rows, width, dtype=LOW)
    own = pltpu.VMEM((rows, width), LOW)
    token_scratch = Scatter.scratch(rows, width)

    slab = lambda *shape: pltpu.VMEM(shape, LOW)
    head_width, hidden = query_weight.shape[1] // 2, up_weight.shape[1] // 2
    high, wide = up_weight.shape[0], down_weight.shape[1]
    tokens = 2 * tensor_total * rows

    def side_by_side(whole):
        return whole if whole.ndim == 2 else whole.transpose(1, 0, 2).reshape(whole.shape[1], -1)

    def column_blocks(partial):
        return partial.reshape(-1, dp_total, wide).transpose(1, 0, 2) if wide % 128 else partial

    heads = like(tokens, head_width, dtype=LOW)
    units = like(tokens, hidden, dtype=LOW)

    (
        whole1, whole2, grad_whole, qkv_full, o_full, up_full, down_full, activated, slope, grad_down,
        queries, keys, values, attended, infos, resid,
    ) = call(
        front_kernel, 1,
        (
            inputs, row(norm1_gain), row(norm1_bias), grad_output, query_weight, key_weight, value_weight, out_weight,
            up_weight, down_weight, row(query_bias), row(value_bias), row(seg_ids), row(positions),
            row(out_bias), row(norm2_gain), row(norm2_bias), row(up_bias),
        ),
        [VMEM] * 18,
        (
            group, group, group, like(width, 3 * head_width, dtype=LOW), like(width, head_width, dtype=LOW),
            like(width, hidden, dtype=LOW), like(*((dp_total, hidden, wide) if wide % 128 else (hidden, width)), dtype=LOW),
            units, units, like(hidden, width, dtype=LOW),
            heads, heads, heads, heads, like(2, 8, GROUP, dtype=jnp.int32), like(rows, width),
        ),
        (ANY,) * 10 + (VMEM,) * 6,
        [
            own, own, own, *[slab(*group.shape)] * 3,
            slab(2, high, 3 * head_width), slab(2, wide, head_width), slab(2, high, hidden), slab(2, hidden, wide),
            slab(width, 3 * head_width), slab(width, head_width), slab(width, hidden), slab(2, GROUP, GROUP),
            slab(*group.shape), slab(tokens, hidden), slab(tokens, hidden), slab(hidden, width),
        ]
        + Gather.SEMS * 3
        + WeightGather.sems(lines, NW) * 2 + WeightGather.sems(lines, NF) * 2
        + Scatter.scratch(rows, width, False) + [grid_of(12)],
    )
    grad_whole, whole2 = grad_whole.reshape(-1, width), whole2.reshape(-1, width)
    down_full, grad_down = side_by_side(down_full), column_blocks(grad_down)
    grad_pre = (mm_nt(grad_whole, down_full) * slope.astype(F32)).astype(LOW)
    grad_parts = mm_nt(grad_pre, up_full).astype(LOW).reshape(group.shape)
    lowered = mm(activated, down_full).astype(LOW).reshape(group.shape)

    hops = [
        like(lines, *shape, dtype=LOW)
        for shape in ((hidden, wide), (high, hidden), (head_width, wide), (high, 3 * head_width))
    ]
    *hops, layer_output, grad_inputs, sums = call(
        back_kernel, 2,
        (
            grad_parts, lowered, grad_down, whole2, whole1.reshape(-1, width), grad_pre, resid, grad_output,
            row(norm2_gain), row(down_bias), o_full, queries, keys, values, attended, infos, inputs, row(norm1_gain), qkv_full,
        ),
        [ANY] * 6 + [VMEM] * 13,
        (*hops, like(rows, width), like(rows, width), like(8, width)),
        (ANY,) * 4 + (VMEM,) * 3,
        [
            own, slab(tokens, width), slab(*group.shape), slab(2, GROUP, GROUP), slab(tokens, head_width),
            slab(width, hidden), slab(tokens, max(hidden, 3 * head_width)),
            slab(*((dp_total, head_width, wide) if wide % 128 else (head_width, width))), slab(width, 3 * head_width),
        ]
        + Scatter.scratch(rows, width) * 2 + Scatter.scratch(rows, width, False) + Gather.SEMS
        + WeightScatter.scratch(lines, hidden, wide, True) + WeightScatter.scratch(lines, high, hidden)
        + WeightScatter.scratch(lines, head_width, wide) + WeightScatter.scratch(lines, high, 3 * head_width)
        + SumAll.scratch(dp_total, width) + [grid_of(3)],
        63,
    )
    cuts = 4

    def cut_at(dim, *shape):
        block = tuple(n // cuts if i == dim else n for i, n in enumerate(shape))
        return pl.BlockSpec(block, lambda g: tuple(g if i == dim else 0 for i in range(len(shape))))

    up_total, bias_total = up_bias.shape[0], query_bias.shape[0]
    lengths = [width] * 6 + [up_total, bias_total, bias_total]
    results = pl.pallas_call(
        functools.partial(final_kernel, lines),
        grid=(cuts,),
        out_shape=(
            like(rows, width), like(rows, width), like(2, hidden, wide), like(high, 2 * hidden), like(2, head_width, wide),
            *[like(high, 2 * head_width)] * 3, *[like(1, n) for n in lengths],
        ),
        in_specs=[
            cut_at(1, lines, hidden, wide), cut_at(1, lines, high, hidden), cut_at(1, lines, head_width, wide),
            cut_at(1, lines, high, 3 * head_width), cut_at(0, rows, width), cut_at(0, rows, width), cut_at(None, 8, width),
        ],
        out_specs=(
            cut_at(0, rows, width), cut_at(0, rows, width), cut_at(1, 2, hidden, wide), cut_at(0, high, 2 * hidden),
            cut_at(1, 2, head_width, wide), *[cut_at(0, high, 2 * head_width)] * 3, *[cut_at(None, 1, n) for n in lengths],
        ),
        compiler_params=pltpu.CompilerParams(vmem_limit_bytes=63 << 20),
    )(*hops, layer_output, grad_inputs, sums)
    layer_output, grad_inputs, down_done, up_done, out_done, query_done, key_done, value_done = results[:8]
    sums = [vector.reshape(-1) for vector in results[8:]]
    return (
        layer_output,
        grad_inputs,
        sums[0],
        sums[1],
        query_done,
        sums[7],
        key_done,
        value_done,
        sums[8],
        out_done.reshape(-1, wide),
        sums[4],
        sums[2],
        sums[3],
        up_done,
        sums[6],
        down_done.reshape(-1, wide),
        sums[5],
    )


def solution(mesh):
    tokens, weight, weight_t = P(("dp", "tensor"), None), P("dp", "tensor"), P("tensor", "dp")
    whole, part = P(), P("tensor")
    return jax.shard_map(
        local,
        mesh=mesh,
        in_specs=(
            tokens, tokens, P("dp"), P("dp"), whole, whole, weight, part, weight, weight, part,
            weight_t, whole, whole, whole, weight, part, weight_t, whole,
        ),
        out_specs=(
            tokens, tokens, whole, whole, weight, part, weight, weight, part, weight_t, whole,
            whole, whole, weight, part, weight_t, whole,
        ),
        check_vma=False,
    )
```

```python
import functools

import jax
import jax.numpy as jnp
from jax import lax
from jax.experimental import pallas as pl
from jax.experimental.pallas import tpu as pltpu
from jax.sharding import PartitionSpec as P

HEAD_DIM = 128
GROUP = 512
EPSILON = 1e-05
NEGATIVE = -1e30
LOW = jnp.bfloat16
F32 = jnp.float32


def gelu_parts(pre_act):
    cumulative = 0.5 * (1.0 + lax.erf(pre_act * 0.7071067811865476))
    density = jnp.exp(-0.5 * pre_act * pre_act) * 0.3989422804014327
    return cumulative, cumulative + pre_act * density


NC = 4
NW = 2
NF = 4
MESH = pl.DeviceIdType.MESH


def remote(src, dst, send, recv, peer):
    return pltpu.make_async_remote_copy(
        src_ref=src, dst_ref=dst, send_sem=send, recv_sem=recv, device_id=peer, device_id_type=MESH
    )


def grid_of(*shape):
    return pltpu.SemaphoreType.DMA(shape)


class Place:
    def __init__(self, dp_total):
        self.lines = dp_total // 2
        self.d = lax.axis_index("dp")
        self.t = lax.axis_index("tensor")
        self.lane, self.line = lax.rem(self.d, 2), lax.div(self.d, 2)
        self.side = lax.rem(self.line, 2)
        self.t_core = self.t + 1 - 2 * lax.rem(self.t, 2)
        self.t_x = lax.rem(self.t + 2, 4)
        self.t_far = lax.rem(self.t_core + 2, 4)
        self.core = (self.d, self.t_core)
        self.x = (self.d, self.t_x)
        self.y = (self.d + 1 - 2 * self.lane, self.t)
        self.z = (self.d + 2 - 4 * self.side, self.t)

    def ahead(self, k):
        return lax.rem(self.line + k, self.lines)

    def behind(self, k):
        return lax.rem(self.line + self.lines - k, self.lines)

    def mate(self, line):
        return (2 * line + self.lane, self.t)

    def greet(self):
        barrier = pltpu.get_barrier_semaphore()
        for peer in (self.core, self.x, self.y):
            pl.semaphore_signal(barrier, inc=1, device_id=peer, device_id_type=MESH)

        @pl.loop(1, self.lines)
        def _(k):
            pl.semaphore_signal(barrier, inc=1, device_id=self.mate(self.ahead(k)), device_id_type=MESH)

        pl.semaphore_wait(barrier, 2 + self.lines)


class Gather:
    SEMS = [grid_of(7, NC), grid_of(7, NC), grid_of(NC)]

    def __init__(self, me, own, whole, send, recv, keep):
        self.me, self.own, self.whole = me, own, whole
        self.send, self.recv, self.keep = send, recv, keep
        self.rows = own.shape[0] // NC

    def at(self, side, t, j):
        return self.whole.at[side, t, pl.ds(j * self.rows, self.rows)]

    def piece(self, j):
        return self.own.at[pl.ds(j * self.rows, self.rows)]

    def copy(self, kind, j, src, dst, peer):
        return remote(src, dst, self.send.at[kind, j], self.recv.at[kind, j], peer)

    def local(self, j):
        return pltpu.make_async_copy(self.piece(j), self.at(0, self.me.t, j), self.keep.at[j])

    def start(self, j):
        me = self.me
        self.copy(2, j, self.piece(j), self.at(1, me.t, j), me.z).start()
        self.copy(1, j, self.piece(j), self.at(0, me.t, j), me.x).start()
        self.copy(0, j, self.piece(j), self.at(0, me.t, j), me.core).start()
        self.local(j).start()

    def wait_recv(self, kind, j, side, t):
        slot = self.at(side, t, j)
        self.copy(kind, j, slot, slot, self.me.core).wait_recv()

    def share(self, kind, j, side, t):
        self.wait_recv(kind, j, side, t)
        slot = self.at(side, t, j)
        self.copy(kind + 3, j, slot, slot, self.me.core).start()

    def relay(self):
        me = self.me

        @pl.loop(0, NC)
        def _(j):
            self.share(2, j, 1, me.t)
            slot = self.at(1, me.t, j)
            self.copy(3, j, slot, slot, me.x).start()
            self.share(1, j, 0, me.t_x)

    def finish(self):
        me = self.me

        @pl.loop(0, NC)
        def _(j):
            self.share(3, j, 1, me.t_x)

        @pl.loop(0, NC)
        def _(j):
            self.wait_recv(0, j, 0, me.t_core)
            self.wait_recv(4, j, 0, me.t_far)
            self.wait_recv(5, j, 1, me.t_core)
            self.wait_recv(6, j, 1, me.t_far)
            self.local(j).wait()
            for kind in range(7):
                self.copy(kind, j, self.piece(j), self.piece(j), me.core).wait_send()


class Scatter:
    SEMS = [grid_of(4, NC), grid_of(4, NC), grid_of(4, NC), grid_of(3, NC), grid_of(3, NC)]

    @staticmethod
    def scratch(rows, width, loaded=True):
        if loaded:
            return [pltpu.VMEM((n, rows, width), LOW) for n in (4, 4, 3)] + Scatter.SEMS
        return [pltpu.VMEM((n, rows, width), LOW) for n in (4, 3)] + Scatter.SEMS[1:]

    def __init__(self, me, parts, *scratch):
        self.me, self.parts = me, parts
        self.held, self.load = None, None
        if len(scratch) == 8:
            self.held, self.came, self.hops, self.load, *scratch = scratch
        else:
            self.came, self.hops, *scratch = scratch
        self.send, self.recv, self.hop_send, self.hop_recv = scratch
        self.rows = self.came.shape[1] // NC
        self.pairs = [
            (0, me.t, me.t_core),
            (0, me.t_x, me.t_far),
            (1, me.t, me.t_core),
            (1, me.t_x, me.t_far),
        ]

    def span(self, j):
        return pl.ds(j * self.rows, self.rows)

    def part(self, side, t, j):
        if len(self.parts.shape) == 4:
            return self.parts.at[side, t, self.span(j)]
        return self.parts.at[pl.ds(pl.multiple_of(((4 * side + t) * NC + j) * self.rows, self.rows), self.rows)]

    def pair_rows(self, i):
        side, mine, _ = self.pairs[i]
        count = 2 * NC * self.rows
        return pl.ds(pl.multiple_of((2 * side + lax.div(mine, 2)) * count, count), count)

    def core_copy(self, i, j):
        side, _, theirs = self.pairs[i]
        return remote(
            self.part(side, theirs, j),
            self.came.at[i, self.span(j)],
            self.send.at[i, j],
            self.recv.at[i, j],
            self.me.core,
        )

    def slot(self, i, j):
        side, mine, _ = self.pairs[i]
        return self.part(side, mine, j) if self.held is None else self.held.at[i, self.span(j)]

    def load_copy(self, i, j):
        side, mine, _ = self.pairs[i]
        return pltpu.make_async_copy(
            self.part(side, mine, j), self.held.at[i, self.span(j)], self.load.at[i, j]
        )

    def hop(self, kind, j, src, peer):
        return remote(
            src, self.hops.at[kind, self.span(j)], self.hop_send.at[kind, j], self.hop_recv.at[kind, j], peer
        )

    def start(self, blocks=(3, 1, 2, 0)):
        for i in blocks:

            @pl.loop(0, NC)
            def _(j):
                self.core_copy(i, j).start()
                if self.load is not None:
                    self.load_copy(i, j).start()

    def joined(self, i, j):
        if self.load is not None:
            self.load_copy(i, j).wait()
        self.core_copy(i, j).wait_recv()
        return self.slot(i, j)[...].astype(F32) + self.came[i, self.span(j)].astype(F32)

    def arrived(self, kind, j):
        self.hop(kind, j, self.hops.at[kind, self.span(j)], self.me.x).wait_recv()
        return self.hops[kind, self.span(j)].astype(F32)

    def spread(self, hops=((0, 3), (1, 1))):
        for kind, i in hops:

            @pl.loop(0, NC)
            def _(j):
                self.slot(i, j)[...] = self.joined(i, j).astype(LOW)
                self.hop(kind, j, self.slot(i, j), self.me.x).start()

    def turn(self):
        @pl.loop(0, NC)
        def _(j):
            total = self.joined(2, j) + self.arrived(0, j)
            self.slot(2, j)[...] = total.astype(LOW)
            self.hop(2, j, self.slot(2, j), self.me.z).start()

    def result(self, j):
        return self.joined(0, j) + self.arrived(1, j) + self.arrived(2, j)

    def finish(self):
        @pl.loop(0, NC)
        def _(j):
            for i in range(4):
                self.core_copy(i, j).wait_send()
            for kind in range(3):
                self.hop(kind, j, self.hops.at[kind, self.span(j)], self.me.x).wait_send()


def block_at(ref, owner, rows, width, first=0, count=None):
    count = rows if count is None else count
    if len(ref.shape) == 3:
        return ref.at[owner, pl.ds(first, count)]
    if ref.shape[0] == rows:
        return ref.at[pl.ds(first, count), pl.ds(pl.multiple_of(owner * width, width), width)]
    return ref.at[pl.ds(pl.multiple_of(owner * rows + first, count), count)]


class WeightGather:
    @staticmethod
    def sems(lines, parts):
        return [grid_of(lines, parts)] * 4 + [grid_of(parts)]

    def __init__(self, me, halves, whole, z_send, z_recv, y_send, y_recv, keep):
        self.me, self.halves, self.whole = me, halves, whole
        self.z_send, self.z_recv, self.y_send, self.y_recv, self.keep = z_send, z_recv, y_send, y_recv, keep
        _, self.rows, self.width = halves.shape
        self.parts = keep.shape[0]
        self.count = self.rows // self.parts

    def at(self, owner, p):
        return block_at(self.whole, owner, self.rows, self.width, p * self.count, self.count)

    def piece(self, half, p):
        return self.halves.at[half, pl.ds(p * self.count, self.count)]

    def z_copy(self, k, p, src, dst, peer):
        return remote(src, dst, self.z_send.at[k, p], self.z_recv.at[k, p], peer)

    def y_copy(self, k, p, src, dst):
        return remote(src, dst, self.y_send.at[k, p], self.y_recv.at[k, p], self.me.y)

    def local(self, p):
        return pltpu.make_async_copy(self.piece(self.me.side, p), self.at(self.me.d, p), self.keep.at[p])

    def start(self, p):
        me = self.me

        @pl.loop(1, me.lines)
        def _(k):
            line = me.ahead(k)
            self.z_copy(k, p, self.piece(lax.rem(line, 2), p), self.at(me.d, p), me.mate(line)).start()

        self.y_copy(0, p, self.piece(me.side, p), self.at(me.d, p)).start()
        self.local(p).start()

    def forward(self, p):
        me = self.me

        @pl.loop(1, me.lines)
        def _(k):
            slot = self.at(2 * me.behind(k) + me.lane, p)
            self.z_copy(k, p, slot, slot, me.y).wait_recv()
            self.y_copy(k, p, slot, slot).start()

    def arrive(self, p):
        me = self.me

        @pl.loop(0, me.lines)
        def _(k):
            slot = self.at(2 * me.behind(k) + 1 - me.lane, p)
            self.y_copy(k, p, slot, slot).wait()

        @pl.loop(1, me.lines)
        def _(k):
            slot = self.at(me.d, p)
            self.z_copy(k, p, slot, slot, me.y).wait_send()

        self.local(p).wait()

    def finish(self):
        for p in range(self.parts):
            self.arrive(p)


class WeightScatter:
    @staticmethod
    def scratch(lines, rows, width, loaded=False):
        blocks = [pltpu.VMEM((lines, rows, width), LOW)] * (2 if loaded else 1)
        return blocks + [grid_of(lines)] * (5 if loaded else 4) + [grid_of(1)]

    def __init__(self, me, parts, hops, *scratch):
        self.me, self.parts, self.hops = me, parts, hops
        self.held, self.load = None, None
        if len(scratch) == 8:
            self.held, self.came, self.load, *scratch = scratch
        else:
            self.came, *scratch = scratch
        self.y_send, self.y_recv, self.z_send, self.z_recv, self.keep = scratch
        _, self.rows, self.width = self.came.shape
        self.step = 32

    def theirs(self, k):
        return block_at(self.parts, 2 * self.me.ahead(k) + 1 - self.me.lane, self.rows, self.width)

    def mine(self, k):
        return block_at(self.parts, 2 * self.me.ahead(k) + self.me.lane, self.rows, self.width)

    def slot(self, k):
        return self.mine(k) if self.held is None else self.held.at[k]

    def y_copy(self, k):
        return remote(self.theirs(k), self.came.at[k], self.y_send.at[k], self.y_recv.at[k], self.me.y)

    def load_copy(self, k):
        return pltpu.make_async_copy(self.mine(k), self.held.at[k], self.load.at[k])

    def z_copy(self, k, peer):
        return remote(self.slot(k), self.hops.at[k], self.z_send.at[k], self.z_recv.at[k], peer)

    def keep_copy(self):
        return pltpu.make_async_copy(self.slot(0), self.hops.at[0], self.keep.at[0])

    def start(self):
        @pl.loop(1, self.me.lines + 1)
        def _(n):
            k = lax.rem(n, self.me.lines)
            self.y_copy(k).start()
            if self.load is not None:
                self.load_copy(k).start()

    def join(self, k):
        if self.load is not None:
            self.load_copy(k).wait()
        self.y_copy(k).wait_recv()
        slot = self.slot(k)

        @pl.loop(0, self.rows, step=self.step)
        def _(row):
            at = pl.ds(pl.multiple_of(row, self.step), self.step)
            slot[at] = (slot[at].astype(F32) + self.came[k, at].astype(F32)).astype(LOW)

    def spread(self, first, last):
        @pl.loop(first, last)
        def _(k):
            self.join(k)
            self.z_copy(k, self.me.mate(self.me.ahead(k))).start()

    def own(self):
        self.join(0)
        self.keep_copy().start()

    def finish(self):
        me = self.me

        @pl.loop(1, me.lines)
        def _(k):
            self.z_copy(k, me.y).wait()

        @pl.loop(0, me.lines)
        def _(k):
            self.y_copy(k).wait_send()

        self.keep_copy().wait()


class SumAll:
    @staticmethod
    def scratch(dp_total, width):
        steps = dp_total.bit_length() + 1
        return [pltpu.VMEM((steps + 1, 8, width), F32), pltpu.VMEM((steps, 8, width), F32), grid_of(steps), grid_of(steps)]

    def __init__(self, me, held, came, send, recv):
        self.me, self.held, self.came, self.send, self.recv = me, held, came, send, recv

    def run(self, first, last, shared):
        me, mask = self.me, 1
        peers = [me.core, me.x]
        while mask < 2 * me.lines:
            peers.append((me.d + mask - 2 * mask * lax.rem(lax.div(me.d, mask), 2), me.t))
            mask *= 2
        for n in range(len(peers))[first:last]:
            copy = remote(self.held.at[n], self.came.at[n], self.send.at[n], self.recv.at[n], peers[n])
            copy.start()
            copy.wait()
            total = self.held[n] + self.came[n]
            if n < 2:
                row = lax.broadcasted_iota(jnp.int32, total.shape, 0)
                total = jnp.where(row < shared, total, self.held[n])
            self.held[n + 1] = total
        return self.held[len(peers)]


def unit_of(rows):
    centred = rows - jnp.mean(rows, axis=1, keepdims=True)
    inverse = lax.rsqrt(jnp.mean(centred * centred, axis=1, keepdims=True) + EPSILON)
    return centred * inverse, inverse


def back_of(grad_rows, unit_rows, inverse, gain):
    scaled = grad_rows * gain
    return inverse * (
        scaled
        - jnp.mean(scaled, axis=1, keepdims=True)
        - unit_rows * jnp.mean(scaled * unit_rows, axis=1, keepdims=True)
    )


def pieces(rows):
    size = rows // NC
    return lambda j: pl.ds(j * size, size)


class Cut:
    def __init__(self, refs):
        self.refs = list(refs)

    def take(self, count):
        taken, self.refs = self.refs[:count], self.refs[count:]
        return taken


NN, NT, TN = ((1,), (0,)), ((1,), (1,)), ((0,), (0,))


def dot(left, right, dims):
    return lax.dot_general(left, right, (dims, ((), ())), preferred_element_type=F32)


def column_halves(halves, *weights):
    width = weights[0].shape[1] // 2
    for n, weight in enumerate(weights):
        for half in range(2):
            halves[half, :, n * width : (n + 1) * width] = weight[:, half * width : (half + 1) * width].astype(LOW)


def row_halves(halves, weight):
    rows = weight.shape[0] // 2
    for half in range(2):
        halves[half] = weight[half * rows : (half + 1) * rows].astype(LOW)


def turned_halves(halves, weight):
    rows = weight.shape[0] // 2
    for half in range(2):
        halves[half] = weight[half * rows : (half + 1) * rows].T.astype(LOW)


def fill_mask(mask, infos, turned):
    @pl.loop(0, 2)
    def _(side):
        across = infos[side].astype(F32)
        down = across.T
        seg_row, pos_row, seg_col, pos_col = down[:, 0:1], down[:, 1:2], across[0:1], across[1:2]
        if turned:
            seg_q, pos_q, seg_k, pos_k = seg_col, pos_col, seg_row, pos_row
        else:
            seg_q, pos_q, seg_k, pos_k = seg_row, pos_row, seg_col, pos_col
        allowed = (pos_k <= pos_q) & ((seg_k == seg_q) | (seg_k == 0.0))
        mask[side] = jnp.where(allowed, 0.0, NEGATIVE).astype(LOW)


def heads_of(width):
    return [slice(n * HEAD_DIM, (n + 1) * HEAD_DIM) for n in range(width // HEAD_DIM)]


def attend(queries, keys, values, mask, attended, between):
    group = mask.shape[1]
    part = group // 2
    for side in range(2):
        for head in heads_of(queries.shape[1]):
            all_rows = pl.ds(side * group, group)

            @pl.loop(0, 2)
            def _(r):
                at = pl.ds(side * group + r * part, part)
                scores = dot(queries[at, head], keys[all_rows, head], NT) * (HEAD_DIM**-0.5)
                scores = scores + mask[side, pl.ds(r * part, part)].astype(F32)
                terms = jnp.exp(scores - jnp.max(scores, axis=1, keepdims=True))
                probs = (terms / jnp.sum(terms, axis=1, keepdims=True)).astype(LOW)
                attended[at, head] = dot(probs, values[all_rows, head], NN).astype(LOW)

            between()


def attend_back(queries, keys, values, grads, mask, grad_qkv, between):
    group, width = mask.shape[1], queries.shape[1]
    part = group // 2
    scale = HEAD_DIM**-0.5
    for side in range(2):
        for n, head in enumerate(heads_of(width)):
            rows = pl.ds(side * group, group)
            grad_key, grad_value = 0.0, 0.0
            for r in range(2):
                at = pl.ds(side * group + r * part, part)
                scores = dot(keys[rows, head], queries[at, head], NT) * scale
                scores = scores + mask[side, :, r * part : (r + 1) * part].astype(F32)
                terms = jnp.exp(scores - jnp.max(scores, axis=0, keepdims=True))
                probs = terms / jnp.sum(terms, axis=0, keepdims=True)
                grad_probs = dot(values[rows, head], grads[at, head], NT)
                delta = jnp.sum(probs * grad_probs, axis=0, keepdims=True)
                grad_scores = (probs * (grad_probs - delta)).astype(LOW)
                grad_value = grad_value + dot(probs.astype(LOW), grads[at, head], NN)
                grad_key = grad_key + dot(grad_scores, queries[at, head], NN)
                grad_query = dot(grad_scores, keys[rows, head], TN)
                grad_qkv[at, n * HEAD_DIM : (n + 1) * HEAD_DIM] = (grad_query * scale).astype(LOW)
            for m, value in ((1, grad_key * scale), (2, grad_value)):
                grad_qkv[rows, m * width + n * HEAD_DIM : m * width + (n + 1) * HEAD_DIM] = value.astype(LOW)
            between()


def column_blocks_of(width, size=256):
    return lambda n: pl.ds(pl.multiple_of(n * size, size), size)


def half_of(ref, side):
    width = ref.shape[1] // 2
    return ref[:, pl.ds(pl.multiple_of(side * width, width), width)]


def front_kernel(
    dp_total, x, gain1, shift1, grad, query, key, value, out, up, down, query_bias, value_bias, seg, pos,
    out_bias, gain2, shift2, up_bias,
    whole1_out, whole2_out, qkv_out, o_out, up_out, down_out, active_out, grad_pre_out, grad_down_out,
    queries, keys, values, attended, infos, resid,
    own1, own2, own_grad, whole1, whole2, whole_grad, qkv_half, out_half, up_half, down_half,
    qkv_whole, o_whole, up_whole, down_whole, mask, parts, active, slope, grad_down, *scratch,
):
    me = Place(dp_total)
    at, cut, block = pieces(x.shape[0]), Cut(scratch), column_blocks_of(x.shape[1])
    gather1, gather2 = Gather(me, own1, whole1, *cut.take(3)), Gather(me, own2, whole2, *cut.take(3))
    gather_grad = Gather(me, own_grad, whole_grad, *cut.take(3))
    first, second = WeightGather(me, qkv_half, qkv_whole, *cut.take(5)), WeightGather(me, out_half, o_whole, *cut.take(5))
    third, fourth = WeightGather(me, up_half, up_whole, *cut.take(5)), WeightGather(me, down_half, down_whole, *cut.take(5))
    scatter = Scatter(me, parts, *cut.take(6))
    (save,) = cut.take(1)
    saved = []

    def store(source, target):
        saved.append(pltpu.make_async_copy(source, target, save.at[2 + len(saved)]))
        saved[-1].start()

    infos[0] = jnp.zeros(infos.shape[1:], jnp.int32)
    infos[0, 0:1], infos[0, 1:2] = seg[...], pos[...]
    me.greet()
    info_copy = remote(infos.at[0], infos.at[1], save.at[0], save.at[1], me.z)
    info_copy.start()

    @pl.loop(0, NC)
    def _(j):
        unit_rows, _ = unit_of(x[at(j)])
        own1[at(j)] = (unit_rows * gain1[...] + shift1[...]).astype(LOW)
        gather1.start(j)

    column_halves(qkv_half, query, key, value)
    for p in range(NW):
        first.start(p)
    turned_halves(out_half, out)
    for p in range(NW):
        second.start(p)
    column_halves(up_half, up)
    third.start(0)
    third.start(1)
    row_halves(down_half, down)

    @pl.loop(0, NC)
    def _(j):
        own_grad[at(j)] = grad[at(j)].astype(LOW)

    info_copy.wait()
    fill_mask(mask, infos, False)
    gather1.relay()
    first.forward(0)

    @pl.loop(0, NC)
    def _(j):
        gather_grad.start(j)

    gather1.finish()
    store(whole1, whole1_out)
    first.forward(1)
    first.finish()
    store(qkv_whole, qkv_out)
    group = mask.shape[1]
    width = queries.shape[1]

    @pl.loop(0, 2)
    def _(side):
        rows = pl.ds(pl.multiple_of(side * group, group), group)
        tokens = whole1[side].reshape(group, -1)
        for n, (result, bias) in enumerate(((queries, query_bias), (keys, None), (values, value_bias))):
            total = dot(tokens, qkv_whole[:, n * width : (n + 1) * width], NN)
            result[rows] = (total if bias is None else total + half_of(bias, me.side)).astype(LOW)

    for p in range(NW):
        second.forward(p)
    steps = iter((None, None, lambda: third.forward(0), lambda: third.start(2)))

    def between():
        step = next(steps, None)
        if step:
            step()

    attend(queries, keys, values, mask, attended, between)
    second.finish()
    store(o_whole, o_out)

    @pl.loop(0, x.shape[1] // 256)
    def _(n):
        total = dot(attended[...], o_whole[pl.ds(pl.multiple_of(n * 256, 256), 256)], NT)
        parts[:, :, :, block(n)] = total.astype(LOW).reshape(*parts.shape[:3], 256)

    scatter.start()
    third.forward(1)
    scatter.spread()
    scatter.turn()
    third.start(3)
    third.forward(2)

    @pl.loop(0, NC)
    def _(j):
        rows = x[at(j)] + scatter.result(j) + out_bias[...]
        resid[at(j)] = rows
        unit_rows, _ = unit_of(rows)
        own2[at(j)] = (unit_rows * gain2[...] + shift2[...]).astype(LOW)
        gather2.start(j)

    fourth.start(0)
    fourth.start(1)
    third.forward(3)
    gather2.relay()
    fourth.start(2)
    fourth.start(3)
    gather_grad.relay()
    fourth.forward(0)
    gather2.finish()
    store(whole2, whole2_out)
    third.finish()
    store(up_whole, up_out)

    def activate(first_block, last_block):
        @pl.loop(first_block, last_block)
        def _(n):
            bias = up_bias[:, pl.ds(pl.multiple_of(me.side * active.shape[1] + n * 256, 256), 256)]

            @pl.loop(0, 2)
            def _(side):
                rows = pl.ds(pl.multiple_of(side * group, group), group)
                pre_act = dot(whole2[side].reshape(group, -1), up_whole[:, block(n)], NN) + bias
                cumulative, rise = gelu_parts(pre_act)
                active[rows, block(n)] = (pre_act * cumulative).astype(LOW)
                slope[rows, block(n)] = rise.astype(LOW)

    hidden_blocks = active.shape[1] // 256
    activate(0, hidden_blocks // 2)
    fourth.forward(1)
    activate(hidden_blocks // 2, hidden_blocks)
    store(active, active_out)
    gather_grad.finish()
    fourth.forward(2)

    @pl.loop(0, hidden_blocks)
    def _(n):
        total = dot(active[:, block(n)], whole_grad[...].reshape(active.shape[0], -1), TN)
        grad_down[pl.ds(pl.multiple_of(n * 256, 256), 256)] = total.astype(LOW)

    store(grad_down, grad_down_out)

    def lower(p):
        fourth.arrive(p)
        units = pl.ds(p * fourth.count, fourth.count)
        if len(down_whole.shape) == 2:
            store(down_whole.at[units], down_out.at[units])
            total = dot(whole_grad[...].reshape(slope.shape[0], -1), down_whole[units], NT)
        else:
            store(down_whole.at[:, units], down_out.at[:, units])
            owners = 128 // fourth.width

            def add(n, total):
                columns = pl.ds(pl.multiple_of(n * 128, 128), 128)
                weights = jnp.concatenate([down_whole[n * owners + i, units] for i in range(owners)], axis=1)
                return total + dot(whole_grad[:, :, :, columns].reshape(slope.shape[0], -1), weights, NT)

            total = lax.fori_loop(
                0, down_whole.shape[0] // owners, add, jnp.zeros((slope.shape[0], fourth.count), F32)
            )
        slope[:, units] = (total * slope[:, units].astype(F32)).astype(LOW)
        store(slope.at[:, units], grad_pre_out.at[:, units])

    lower(0)
    lower(1)
    fourth.forward(3)
    lower(2)
    lower(3)
    scatter.finish()
    for copy in saved:
        copy.wait()


def back_kernel(
    dp_total, down, whole2, whole1, grad_pre_in, active, up_whole, down_whole, resid, grad, gain2, down_bias, o_whole,
    queries, keys, values, attended, infos, x, gain1, qkv_whole,
    down_hops, up_hops, out_hops, qkv_hops, lowered, output, grad_inputs, sums,
    own, tokens, whole, mask, grad_att, grad_up, shared, grad_out, qkv, *scratch,
):
    me = Place(dp_total)
    at, cut, block = pieces(x.shape[0]), Cut(scratch), column_blocks_of(x.shape[1])
    scatter, other = Scatter(me, tokens, *cut.take(6)), Scatter(me, lowered, *cut.take(8))
    last, gather = Scatter(me, whole, *cut.take(6)), Gather(me, own, whole, *cut.take(3))
    first = WeightScatter(me, down, down_hops, *cut.take(8))
    second = WeightScatter(me, grad_up, up_hops, *cut.take(6))
    third = WeightScatter(me, grad_out, out_hops, *cut.take(6))
    fourth = WeightScatter(me, qkv, qkv_hops, *cut.take(6))
    vectors = SumAll(me, *cut.take(4))
    load, tiles = cut.take(2)
    start = vectors.held.at[0]
    lines, hidden, head_width = me.lines, grad_up.shape[1], queries.shape[1]
    grad_pre, grad_qkv = shared.at[:, :hidden], shared.at[:, : 3 * head_width]
    load1, load2, load3, load4 = (
        pltpu.make_async_copy(source, target, load.at[n])
        for n, (source, target) in enumerate(
            ((whole1, tokens), (whole2, tokens), (grad_pre_in, grad_pre), (up_whole, grad_up))
        )
    )
    load3.start()
    load4.start()
    me.greet()
    first.start()
    load3.wait()
    load4.wait()

    def norm_parts(i):
        rows = scatter.pair_rows(i)

        @pl.loop(0, x.shape[1] // 256)
        def _(n):
            weights = grad_up[pl.ds(pl.multiple_of(n * 256, 256), 256)]
            tokens[rows, block(n)] = dot(grad_pre[rows], weights, NT).astype(LOW)

        scatter.start((i,))

    norm_parts(3)
    norm_parts(1)
    scatter.spread(((0, 3),))
    norm_parts(2)
    scatter.spread(((1, 1),))
    norm_parts(0)

    scatter.turn()
    first.spread(1, lines // 2)
    start[...] = jnp.zeros_like(start)

    @pl.loop(0, hidden // 256)
    def _(n):
        columns = pl.ds(pl.multiple_of(me.side * hidden + n * 256, 256), 256)
        start[6:7, columns] = jnp.sum(grad_pre[:, block(n)].astype(F32), axis=0, keepdims=True)

    @pl.loop(0, NC)
    def _(j):
        unit_rows, inverse = unit_of(resid[at(j)])
        e = scatter.result(j)
        rows = grad[at(j)] + back_of(e, unit_rows, inverse, gain2[...])
        grad_inputs[at(j)] = rows
        own[at(j)] = rows.astype(LOW)
        gather.start(j)
        start[2:3] += jnp.sum(e * unit_rows, axis=0, keepdims=True)
        start[3:4] += jnp.sum(e, axis=0, keepdims=True)
        start[4:5] += jnp.sum(rows, axis=0, keepdims=True)
        start[5:6] += jnp.sum(grad[at(j)], axis=0, keepdims=True)

    scatter.finish()
    load2.start()
    fill_mask(mask, infos, True)
    first.spread(lines // 2, lines - 1)
    load2.wait()

    @pl.loop(0, grad_up.shape[0] // 256)
    def _(n):
        total = dot(tokens[:, block(n)], grad_pre[...], TN)
        grad_up[pl.ds(pl.multiple_of(n * 256, 256), 256)] = total.astype(LOW)

    second.start()
    load1.start()
    first.spread(lines - 1, lines)
    gather.relay()
    gather.finish()
    mixed = whole[...].reshape(-1, whole.shape[3])
    grad_att[...] = dot(mixed, o_whole[...], NN).astype(LOW)
    steps = iter((None, lambda: second.spread(1, lines // 2), None, lambda: first.own()))

    def between():
        step = next(steps, None)
        if step:
            step()

    attend_back(queries, keys, values, grad_att, mask, grad_qkv, between)

    for n in (0, 2):
        total = jnp.sum(grad_qkv[:, n * head_width : (n + 1) * head_width].astype(F32), axis=0, keepdims=True)
        start[7:8, pl.ds(pl.multiple_of((n + me.side) * head_width, head_width), head_width)] = total

    load1.wait()

    @pl.loop(0, qkv.shape[0] // 256)
    def _(n):
        qkv[pl.ds(pl.multiple_of(n * 256, 256), 256)] = dot(tokens[:, block(n)], grad_qkv[...], TN).astype(LOW)

    fourth.start()
    second.spread(lines // 2, lines - 1)
    wide = third.width

    @pl.loop(0, x.shape[1] // 256)
    def _(n):
        columns = whole[:, :, :, block(n)].reshape(-1, 256)
        total = dot(attended[...], columns, TN).astype(LOW)
        if wide % 128:
            for i in range(256 // wide):
                grad_out[n * (256 // wide) + i] = total[:, i * wide : (i + 1) * wide]
        else:
            grad_out[:, block(n)] = total

    third.start()

    @pl.loop(0, x.shape[1] // 256)
    def _(n):
        total = dot(grad_qkv[...], qkv_whole[pl.ds(pl.multiple_of(n * 256, 256), 256)], NT)
        whole[:, :, :, block(n)] = total.astype(LOW).reshape(*whole.shape[:3], 256)

    last.start()
    second.spread(lines - 1, lines)
    last.spread()

    held = tokens.at[:, :hidden]
    load_active = pltpu.make_async_copy(active, held, tiles.at[0])
    load_active.start()

    def tile_at(b):
        return tokens.at[:hidden, hidden + b * 256 : hidden + (b + 1) * 256]

    def result_at(b):
        return tokens.at[:, hidden + (2 + b) * 256 : hidden + (3 + b) * 256]

    def load_tile(n, b):
        return pltpu.make_async_copy(down_whole.at[:, block(n)], tile_at(b), tiles.at[1 + b])

    def save_tile(n, b):
        return pltpu.make_async_copy(result_at(b), lowered.at[:, block(n)], tiles.at[3 + b])

    load_tile(0, 0).start()
    load_tile(1, 1).start()
    load_active.wait()
    tile_total = x.shape[1] // 256

    @pl.loop(0, tile_total // 2)
    def _(m):
        for b in range(2):
            n = 2 * m + b
            load_tile(n, b).wait()

            @pl.when(m > 0)
            def _():
                save_tile(n, b).wait()

            result_at(b)[...] = dot(held[...], tile_at(b)[...], NN).astype(LOW)
            save_tile(n, b).start()

            @pl.when(m < tile_total // 2 - 1)
            def _():
                load_tile(n + 2, b).start()

    for b in range(2):
        save_tile(tile_total - 2 + b, b).wait()
    other.start()
    last.turn()
    second.own()
    other.spread()
    fourth.spread(1, lines // 2)
    other.turn()
    fourth.spread(lines // 2, lines - 1)

    @pl.loop(0, NC)
    def _(j):
        unit_rows, inverse = unit_of(x[at(j)])
        e = last.result(j)
        grad_inputs[at(j)] += back_of(e, unit_rows, inverse, gain1[...])
        start[0:1] += jnp.sum(e * unit_rows, axis=0, keepdims=True)
        start[1:2] += jnp.sum(e, axis=0, keepdims=True)

    vectors.run(0, 2, 6)
    fourth.spread(lines - 1, lines)
    fourth.own()
    third.spread(1, lines)
    third.own()

    @pl.loop(0, NC)
    def _(j):
        output[at(j)] = resid[at(j)] + other.result(j) + down_bias[...]

    sums[...] = vectors.run(2, None, 6)
    for part in (other, last, first, second, third, fourth):
        part.finish()


def final_kernel(
    lines, down_hops, up_hops, out_hops, qkv_hops, rows_in, grads_in, sums,
    output, grad_inputs, down, up, out, query, key, value, *vectors,
):
    side = lax.rem(lax.div(lax.axis_index("dp"), 2), 2)

    def half_sums(hops):
        same, opposite = hops[0].astype(F32), hops[1].astype(F32)
        for k in range(2, lines):
            if k % 2:
                opposite = opposite + hops[k].astype(F32)
            else:
                same = same + hops[k].astype(F32)
        return (side, same), (1 - side, opposite)

    for half, total in half_sums(down_hops):
        down[half] = total
    for half, total in half_sums(out_hops):
        out[half] = total
    for half, total in half_sums(up_hops):
        width = total.shape[1]
        up[:, pl.ds(pl.multiple_of(half * width, width), width)] = total
    for half, total in half_sums(qkv_hops):
        width = total.shape[1] // 3
        for n, ref in enumerate((query, key, value)):
            ref[:, pl.ds(pl.multiple_of(half * width, width), width)] = total[:, n * width : (n + 1) * width]
    output[...], grad_inputs[...] = rows_in[...], grads_in[...]
    first = 0
    for n, ref in enumerate(vectors):
        if n < 7:
            ref[...] = sums[n : n + 1, : ref.shape[1]]
        else:
            ref[...] = sums[7:8, first : first + ref.shape[1]]
            first += ref.shape[1]


VMEM = pl.BlockSpec(memory_space=pltpu.VMEM)
ANY = pl.BlockSpec(memory_space=pl.ANY)


def call(kernel, number, ins, in_specs, outs, out_specs, scratch, limit=60):
    return pl.pallas_call(
        functools.partial(kernel, lax.axis_size("dp")),
        out_shape=outs,
        in_specs=in_specs,
        out_specs=out_specs,
        scratch_shapes=scratch,
        compiler_params=pltpu.CompilerParams(
            collective_id=number, has_side_effects=True, vmem_limit_bytes=limit << 20
        ),
        cost_estimate=pl.CostEstimate(flops=0, bytes_accessed=100_000_000, transcendentals=0),
    )(*ins)


def like(*shape, dtype=F32):
    return jax.ShapeDtypeStruct(shape, dtype)


def local(
    inputs,
    grad_output,
    seg_ids,
    positions,
    norm1_gain,
    norm1_bias,
    query_weight,
    query_bias,
    key_weight,
    value_weight,
    value_bias,
    out_weight,
    out_bias,
    norm2_gain,
    norm2_bias,
    up_weight,
    up_bias,
    down_weight,
    down_bias,
):
    dp_total = lax.axis_size("dp")
    tensor_total = lax.axis_size("tensor")
    lines = dp_total // 2
    place = lax.axis_index("dp")
    side = (place >> 1) & 1

    rows, width = inputs.shape
    row = lambda vector: vector.reshape(1, -1)
    group = like(2, tensor_total, rows, width, dtype=LOW)
    own = pltpu.VMEM((rows, width), LOW)
    token_scratch = Scatter.scratch(rows, width)

    slab = lambda *shape: pltpu.VMEM(shape, LOW)
    head_width, hidden = query_weight.shape[1] // 2, up_weight.shape[1] // 2
    high, wide = up_weight.shape[0], down_weight.shape[1]
    tokens = 2 * tensor_total * rows

    def side_by_side(whole):
        return whole if whole.ndim == 2 else whole.transpose(1, 0, 2).reshape(whole.shape[1], -1)

    def column_blocks(partial):
        return partial.reshape(-1, dp_total, wide).transpose(1, 0, 2) if wide % 128 else partial

    down_shape = (dp_total, hidden, wide) if wide % 128 else (hidden, width)
    heads = like(tokens, head_width, dtype=LOW)
    units = like(tokens, hidden, dtype=LOW)

    (
        whole1, whole2, qkv_full, o_full, up_full, down_full, activated, grad_pre, grad_down,
        queries, keys, values, attended, infos, resid,
    ) = call(
        front_kernel, 1,
        (
            inputs, row(norm1_gain), row(norm1_bias), grad_output, query_weight, key_weight, value_weight, out_weight,
            up_weight, down_weight, row(query_bias), row(value_bias), row(seg_ids), row(positions),
            row(out_bias), row(norm2_gain), row(norm2_bias), row(up_bias),
        ),
        [VMEM] * 18,
        (
            group, group, like(width, 3 * head_width, dtype=LOW), like(width, head_width, dtype=LOW),
            like(width, hidden, dtype=LOW), like(*down_shape, dtype=LOW),
            units, units, like(hidden, width, dtype=LOW),
            heads, heads, heads, heads, like(2, 8, GROUP, dtype=jnp.int32), like(rows, width),
        ),
        (ANY,) * 9 + (VMEM,) * 6,
        [
            own, own, own, *[slab(*group.shape)] * 3,
            slab(2, high, 3 * head_width), slab(2, wide, head_width), slab(2, high, hidden), slab(2, hidden, wide),
            slab(width, 3 * head_width), slab(width, head_width), slab(width, hidden), slab(*down_shape),
            slab(2, GROUP, GROUP), slab(*group.shape), slab(tokens, hidden), slab(tokens, hidden), slab(hidden, width),
        ]
        + Gather.SEMS * 3
        + WeightGather.sems(lines, NW) * 2 + WeightGather.sems(lines, NF) * 2
        + Scatter.scratch(rows, width, False) + [grid_of(9 + 2 * NF)],
        63,
    )
    down_full, grad_down = side_by_side(down_full), column_blocks(grad_down)
    hops = [
        like(lines, *shape, dtype=LOW)
        for shape in ((hidden, wide), (high, hidden), (head_width, wide), (high, 3 * head_width))
    ]
    *hops, _, layer_output, grad_inputs, sums = call(
        back_kernel, 2,
        (
            grad_down, whole2.reshape(-1, width), whole1.reshape(-1, width), grad_pre, activated, up_full, down_full,
            resid, grad_output, row(norm2_gain), row(down_bias), o_full, queries, keys, values, attended, infos, inputs, row(norm1_gain), qkv_full,
        ),
        [ANY] * 7 + [VMEM] * 13,
        (*hops, like(tokens, width, dtype=LOW), like(rows, width), like(rows, width), like(8, width)),
        (ANY,) * 5 + (VMEM,) * 3,
        [
            own, slab(tokens, width), slab(*group.shape), slab(2, GROUP, GROUP), slab(tokens, head_width),
            slab(width, hidden), slab(tokens, max(hidden, 3 * head_width)),
            slab(*((dp_total, head_width, wide) if wide % 128 else (head_width, width))), slab(width, 3 * head_width),
        ]
        + Scatter.scratch(rows, width, False) + Scatter.scratch(rows, width) + Scatter.scratch(rows, width, False)
        + Gather.SEMS
        + WeightScatter.scratch(lines, hidden, wide, True) + WeightScatter.scratch(lines, high, hidden)
        + WeightScatter.scratch(lines, head_width, wide) + WeightScatter.scratch(lines, high, 3 * head_width)
        + SumAll.scratch(dp_total, width) + [grid_of(4), grid_of(5)],
        63,
    )
    cuts = 4

    def cut_at(dim, *shape):
        block = tuple(n // cuts if i == dim else n for i, n in enumerate(shape))
        return pl.BlockSpec(block, lambda g: tuple(g if i == dim else 0 for i in range(len(shape))))

    up_total, bias_total = up_bias.shape[0], query_bias.shape[0]
    lengths = [width] * 6 + [up_total, bias_total, bias_total]
    results = pl.pallas_call(
        functools.partial(final_kernel, lines),
        grid=(cuts,),
        out_shape=(
            like(rows, width), like(rows, width), like(2, hidden, wide), like(high, 2 * hidden), like(2, head_width, wide),
            *[like(high, 2 * head_width)] * 3, *[like(1, n) for n in lengths],
        ),
        in_specs=[
            cut_at(1, lines, hidden, wide), cut_at(1, lines, high, hidden), cut_at(1, lines, head_width, wide),
            cut_at(1, lines, high, 3 * head_width), cut_at(0, rows, width), cut_at(0, rows, width), cut_at(None, 8, width),
        ],
        out_specs=(
            cut_at(0, rows, width), cut_at(0, rows, width), cut_at(1, 2, hidden, wide), cut_at(0, high, 2 * hidden),
            cut_at(1, 2, head_width, wide), *[cut_at(0, high, 2 * head_width)] * 3, *[cut_at(None, 1, n) for n in lengths],
        ),
        compiler_params=pltpu.CompilerParams(vmem_limit_bytes=63 << 20),
    )(*hops, layer_output, grad_inputs, sums)
    layer_output, grad_inputs, down_done, up_done, out_done, query_done, key_done, value_done = results[:8]
    sums = [vector.reshape(-1) for vector in results[8:]]
    return (
        layer_output,
        grad_inputs,
        sums[0],
        sums[1],
        query_done,
        sums[7],
        key_done,
        value_done,
        sums[8],
        out_done.reshape(-1, wide),
        sums[4],
        sums[2],
        sums[3],
        up_done,
        sums[6],
        down_done.reshape(-1, wide),
        sums[5],
    )


def solution(mesh):
    tokens, weight, weight_t = P(("dp", "tensor"), None), P("dp", "tensor"), P("tensor", "dp")
    whole, part = P(), P("tensor")
    return jax.shard_map(
        local,
        mesh=mesh,
        in_specs=(
            tokens, tokens, P("dp"), P("dp"), whole, whole, weight, part, weight, weight, part,
            weight_t, whole, whole, whole, weight, part, weight_t, whole,
        ),
        out_specs=(
            tokens, tokens, whole, whole, weight, part, weight, weight, part, weight_t, whole,
            whole, whole, weight, part, weight_t, whole,
        ),
        check_vma=False,
    )
```

```python
import functools

import jax
import jax.numpy as jnp
from jax import lax
from jax.experimental import pallas as pl
from jax.experimental.pallas import tpu as pltpu
from jax.sharding import PartitionSpec as P

HEAD_DIM = 128
GROUP = 512
EPSILON = 1e-05
NEGATIVE = -1e30
LOW = jnp.bfloat16
F32 = jnp.float32


def gelu_parts(pre_act):
    cumulative = 0.5 * (1.0 + lax.erf(pre_act * 0.7071067811865476))
    density = jnp.exp(-0.5 * pre_act * pre_act) * 0.3989422804014327
    return cumulative, cumulative + pre_act * density


NC = 4
NW = 2
NF = 4
MESH = pl.DeviceIdType.MESH


def remote(src, dst, send, recv, peer):
    return pltpu.make_async_remote_copy(
        src_ref=src, dst_ref=dst, send_sem=send, recv_sem=recv, device_id=peer, device_id_type=MESH
    )


def grid_of(*shape):
    return pltpu.SemaphoreType.DMA(shape)


class Place:
    def __init__(self, dp_total):
        self.lines = dp_total // 2
        self.d = lax.axis_index("dp")
        self.t = lax.axis_index("tensor")
        self.lane, self.line = lax.rem(self.d, 2), lax.div(self.d, 2)
        self.side = lax.rem(self.line, 2)
        self.t_core = self.t + 1 - 2 * lax.rem(self.t, 2)
        self.t_x = lax.rem(self.t + 2, 4)
        self.t_far = lax.rem(self.t_core + 2, 4)
        self.core = (self.d, self.t_core)
        self.x = (self.d, self.t_x)
        self.y = (self.d + 1 - 2 * self.lane, self.t)
        self.z = (self.d + 2 - 4 * self.side, self.t)

    def ahead(self, k):
        return lax.rem(self.line + k, self.lines)

    def behind(self, k):
        return lax.rem(self.line + self.lines - k, self.lines)

    def mate(self, line):
        return (2 * line + self.lane, self.t)

    def greet(self):
        barrier = pltpu.get_barrier_semaphore()
        for peer in (self.core, self.x, self.y):
            pl.semaphore_signal(barrier, inc=1, device_id=peer, device_id_type=MESH)

        @pl.loop(1, self.lines)
        def _(k):
            pl.semaphore_signal(barrier, inc=1, device_id=self.mate(self.ahead(k)), device_id_type=MESH)

        pl.semaphore_wait(barrier, 2 + self.lines)


class Gather:
    SEMS = [grid_of(7, NC), grid_of(7, NC), grid_of(NC)]

    def __init__(self, me, own, whole, send, recv, keep):
        self.me, self.own, self.whole = me, own, whole
        self.send, self.recv, self.keep = send, recv, keep
        self.rows = own.shape[0] // NC

    def at(self, side, t, j):
        return self.whole.at[side, t, pl.ds(j * self.rows, self.rows)]

    def piece(self, j):
        return self.own.at[pl.ds(j * self.rows, self.rows)]

    def copy(self, kind, j, src, dst, peer):
        return remote(src, dst, self.send.at[kind, j], self.recv.at[kind, j], peer)

    def local(self, j):
        return pltpu.make_async_copy(self.piece(j), self.at(0, self.me.t, j), self.keep.at[j])

    def start(self, j):
        me = self.me
        self.copy(2, j, self.piece(j), self.at(1, me.t, j), me.z).start()
        self.copy(1, j, self.piece(j), self.at(0, me.t, j), me.x).start()
        self.copy(0, j, self.piece(j), self.at(0, me.t, j), me.core).start()
        self.local(j).start()

    def wait_recv(self, kind, j, side, t):
        slot = self.at(side, t, j)
        self.copy(kind, j, slot, slot, self.me.core).wait_recv()

    def share(self, kind, j, side, t):
        self.wait_recv(kind, j, side, t)
        slot = self.at(side, t, j)
        self.copy(kind + 3, j, slot, slot, self.me.core).start()

    def relay(self):
        me = self.me

        @pl.loop(0, NC)
        def _(j):
            self.share(2, j, 1, me.t)
            slot = self.at(1, me.t, j)
            self.copy(3, j, slot, slot, me.x).start()
            self.share(1, j, 0, me.t_x)

    def finish(self):
        me = self.me

        @pl.loop(0, NC)
        def _(j):
            self.share(3, j, 1, me.t_x)

        @pl.loop(0, NC)
        def _(j):
            self.wait_recv(0, j, 0, me.t_core)
            self.wait_recv(4, j, 0, me.t_far)
            self.wait_recv(5, j, 1, me.t_core)
            self.wait_recv(6, j, 1, me.t_far)
            self.local(j).wait()
            for kind in range(7):
                self.copy(kind, j, self.piece(j), self.piece(j), me.core).wait_send()


class Scatter:
    SEMS = [grid_of(4, NC), grid_of(4, NC), grid_of(4, NC), grid_of(3, NC), grid_of(3, NC)]

    @staticmethod
    def scratch(rows, width, loaded=True):
        if loaded:
            return [pltpu.VMEM((n, rows, width), LOW) for n in (4, 4, 3)] + Scatter.SEMS
        return [pltpu.VMEM((n, rows, width), LOW) for n in (4, 3)] + Scatter.SEMS[1:]

    def __init__(self, me, parts, *scratch):
        self.me, self.parts = me, parts
        self.held, self.load = None, None
        if len(scratch) == 8:
            self.held, self.came, self.hops, self.load, *scratch = scratch
        else:
            self.came, self.hops, *scratch = scratch
        self.send, self.recv, self.hop_send, self.hop_recv = scratch
        self.rows = self.came.shape[1] // NC
        self.pairs = [
            (0, me.t, me.t_core),
            (0, me.t_x, me.t_far),
            (1, me.t, me.t_core),
            (1, me.t_x, me.t_far),
        ]

    def span(self, j):
        return pl.ds(j * self.rows, self.rows)

    def part(self, side, t, j):
        if len(self.parts.shape) == 4:
            return self.parts.at[side, t, self.span(j)]
        return self.parts.at[pl.ds(pl.multiple_of(((4 * side + t) * NC + j) * self.rows, self.rows), self.rows)]

    def pair_rows(self, i):
        side, mine, _ = self.pairs[i]
        count = 2 * NC * self.rows
        return pl.ds(pl.multiple_of((2 * side + lax.div(mine, 2)) * count, count), count)

    def core_copy(self, i, j):
        side, _, theirs = self.pairs[i]
        return remote(
            self.part(side, theirs, j),
            self.came.at[i, self.span(j)],
            self.send.at[i, j],
            self.recv.at[i, j],
            self.me.core,
        )

    def slot(self, i, j):
        side, mine, _ = self.pairs[i]
        return self.part(side, mine, j) if self.held is None else self.held.at[i, self.span(j)]

    def load_copy(self, i, j):
        side, mine, _ = self.pairs[i]
        return pltpu.make_async_copy(
            self.part(side, mine, j), self.held.at[i, self.span(j)], self.load.at[i, j]
        )

    def hop(self, kind, j, src, peer):
        return remote(
            src, self.hops.at[kind, self.span(j)], self.hop_send.at[kind, j], self.hop_recv.at[kind, j], peer
        )

    def start(self, blocks=(3, 1, 2, 0)):
        for i in blocks:

            @pl.loop(0, NC)
            def _(j):
                self.core_copy(i, j).start()
                if self.load is not None:
                    self.load_copy(i, j).start()

    def joined(self, i, j):
        if self.load is not None:
            self.load_copy(i, j).wait()
        self.core_copy(i, j).wait_recv()
        return self.slot(i, j)[...].astype(F32) + self.came[i, self.span(j)].astype(F32)

    def arrived(self, kind, j):
        self.hop(kind, j, self.hops.at[kind, self.span(j)], self.me.x).wait_recv()
        return self.hops[kind, self.span(j)].astype(F32)

    def spread(self, hops=((0, 3), (1, 1))):
        for kind, i in hops:

            @pl.loop(0, NC)
            def _(j):
                self.slot(i, j)[...] = self.joined(i, j).astype(LOW)
                self.hop(kind, j, self.slot(i, j), self.me.x).start()

    def turn(self):
        @pl.loop(0, NC)
        def _(j):
            total = self.joined(2, j) + self.arrived(0, j)
            self.slot(2, j)[...] = total.astype(LOW)
            self.hop(2, j, self.slot(2, j), self.me.z).start()

    def result(self, j):
        return self.joined(0, j) + self.arrived(1, j) + self.arrived(2, j)

    def finish(self):
        @pl.loop(0, NC)
        def _(j):
            for i in range(4):
                self.core_copy(i, j).wait_send()
            for kind in range(3):
                self.hop(kind, j, self.hops.at[kind, self.span(j)], self.me.x).wait_send()


def block_at(ref, owner, rows, width, first=0, count=None):
    count = rows if count is None else count
    if len(ref.shape) == 3:
        return ref.at[owner, pl.ds(first, count)]
    if ref.shape[0] == rows:
        return ref.at[pl.ds(first, count), pl.ds(pl.multiple_of(owner * width, width), width)]
    return ref.at[pl.ds(pl.multiple_of(owner * rows + first, count), count)]


class WeightGather:
    @staticmethod
    def sems(lines, parts):
        return [grid_of(lines, parts)] * 4 + [grid_of(parts)]

    def __init__(self, me, halves, whole, z_send, z_recv, y_send, y_recv, keep):
        self.me, self.halves, self.whole = me, halves, whole
        self.z_send, self.z_recv, self.y_send, self.y_recv, self.keep = z_send, z_recv, y_send, y_recv, keep
        _, self.rows, self.width = halves.shape
        self.parts = keep.shape[0]
        self.count = self.rows // self.parts

    def at(self, owner, p):
        return block_at(self.whole, owner, self.rows, self.width, p * self.count, self.count)

    def piece(self, half, p):
        return self.halves.at[half, pl.ds(p * self.count, self.count)]

    def z_copy(self, k, p, src, dst, peer):
        return remote(src, dst, self.z_send.at[k, p], self.z_recv.at[k, p], peer)

    def y_copy(self, k, p, src, dst):
        return remote(src, dst, self.y_send.at[k, p], self.y_recv.at[k, p], self.me.y)

    def local(self, p):
        return pltpu.make_async_copy(self.piece(self.me.side, p), self.at(self.me.d, p), self.keep.at[p])

    def start(self, p):
        me = self.me

        @pl.loop(1, me.lines)
        def _(k):
            line = me.ahead(k)
            self.z_copy(k, p, self.piece(lax.rem(line, 2), p), self.at(me.d, p), me.mate(line)).start()

        self.y_copy(0, p, self.piece(me.side, p), self.at(me.d, p)).start()
        self.local(p).start()

    def forward(self, p):
        me = self.me

        @pl.loop(1, me.lines)
        def _(k):
            slot = self.at(2 * me.behind(k) + me.lane, p)
            self.z_copy(k, p, slot, slot, me.y).wait_recv()
            self.y_copy(k, p, slot, slot).start()

    def arrive(self, p):
        me = self.me

        @pl.loop(0, me.lines)
        def _(k):
            slot = self.at(2 * me.behind(k) + 1 - me.lane, p)
            self.y_copy(k, p, slot, slot).wait()

        @pl.loop(1, me.lines)
        def _(k):
            slot = self.at(me.d, p)
            self.z_copy(k, p, slot, slot, me.y).wait_send()

        self.local(p).wait()

    def finish(self):
        for p in range(self.parts):
            self.arrive(p)


class WeightScatter:
    @staticmethod
    def scratch(lines, rows, width, loaded=False):
        blocks = [pltpu.VMEM((lines, rows, width), LOW)] * (2 if loaded else 1)
        return blocks + [grid_of(lines)] * (5 if loaded else 4) + [grid_of(1)]

    def __init__(self, me, parts, hops, *scratch):
        self.me, self.parts, self.hops = me, parts, hops
        self.held, self.load = None, None
        if len(scratch) == 8:
            self.held, self.came, self.load, *scratch = scratch
        else:
            self.came, *scratch = scratch
        self.y_send, self.y_recv, self.z_send, self.z_recv, self.keep = scratch
        _, self.rows, self.width = self.came.shape
        self.step = 32

    def theirs(self, k):
        return block_at(self.parts, 2 * self.me.ahead(k) + 1 - self.me.lane, self.rows, self.width)

    def mine(self, k):
        return block_at(self.parts, 2 * self.me.ahead(k) + self.me.lane, self.rows, self.width)

    def slot(self, k):
        return self.mine(k) if self.held is None else self.held.at[k]

    def y_copy(self, k):
        return remote(self.theirs(k), self.came.at[k], self.y_send.at[k], self.y_recv.at[k], self.me.y)

    def load_copy(self, k):
        return pltpu.make_async_copy(self.mine(k), self.held.at[k], self.load.at[k])

    def z_copy(self, k, peer):
        return remote(self.slot(k), self.hops.at[k], self.z_send.at[k], self.z_recv.at[k], peer)

    def keep_copy(self):
        return pltpu.make_async_copy(self.slot(0), self.hops.at[0], self.keep.at[0])

    def start(self):
        @pl.loop(1, self.me.lines + 1)
        def _(n):
            k = lax.rem(n, self.me.lines)
            self.y_copy(k).start()
            if self.load is not None:
                self.load_copy(k).start()

    def join(self, k):
        if self.load is not None:
            self.load_copy(k).wait()
        self.y_copy(k).wait_recv()
        slot = self.slot(k)

        @pl.loop(0, self.rows, step=self.step)
        def _(row):
            at = pl.ds(pl.multiple_of(row, self.step), self.step)
            slot[at] = (slot[at].astype(F32) + self.came[k, at].astype(F32)).astype(LOW)

    def spread(self, first, last):
        @pl.loop(first, last)
        def _(k):
            self.join(k)
            self.z_copy(k, self.me.mate(self.me.ahead(k))).start()

    def own(self):
        self.join(0)
        self.keep_copy().start()

    def finish(self):
        me = self.me

        @pl.loop(1, me.lines)
        def _(k):
            self.z_copy(k, me.y).wait()

        @pl.loop(0, me.lines)
        def _(k):
            self.y_copy(k).wait_send()

        self.keep_copy().wait()


class SumAll:
    @staticmethod
    def scratch(dp_total, width):
        steps = dp_total.bit_length() + 1
        return [pltpu.VMEM((steps + 1, 8, width), F32), pltpu.VMEM((steps, 8, width), F32), grid_of(steps), grid_of(steps)]

    def __init__(self, me, held, came, send, recv):
        self.me, self.held, self.came, self.send, self.recv = me, held, came, send, recv

    def run(self, first, last, shared):
        me, mask = self.me, 1
        peers = [me.core, me.x]
        while mask < 2 * me.lines:
            peers.append((me.d + mask - 2 * mask * lax.rem(lax.div(me.d, mask), 2), me.t))
            mask *= 2
        for n in range(len(peers))[first:last]:
            copy = remote(self.held.at[n], self.came.at[n], self.send.at[n], self.recv.at[n], peers[n])
            copy.start()
            copy.wait()
            total = self.held[n] + self.came[n]
            if n < 2:
                row = lax.broadcasted_iota(jnp.int32, total.shape, 0)
                total = jnp.where(row < shared, total, self.held[n])
            self.held[n + 1] = total
        return self.held[len(peers)]


def unit_of(rows):
    centred = rows - jnp.mean(rows, axis=1, keepdims=True)
    inverse = lax.rsqrt(jnp.mean(centred * centred, axis=1, keepdims=True) + EPSILON)
    return centred * inverse, inverse


def back_of(grad_rows, unit_rows, inverse, gain):
    scaled = grad_rows * gain
    return inverse * (
        scaled
        - jnp.mean(scaled, axis=1, keepdims=True)
        - unit_rows * jnp.mean(scaled * unit_rows, axis=1, keepdims=True)
    )


def pieces(rows):
    size = rows // NC
    return lambda j: pl.ds(j * size, size)


class Cut:
    def __init__(self, refs):
        self.refs = list(refs)

    def take(self, count):
        taken, self.refs = self.refs[:count], self.refs[count:]
        return taken


NN, NT, TN = ((1,), (0,)), ((1,), (1,)), ((0,), (0,))


def dot(left, right, dims):
    return lax.dot_general(left, right, (dims, ((), ())), preferred_element_type=F32)


def column_halves(halves, *weights):
    width = weights[0].shape[1] // 2
    for n, weight in enumerate(weights):
        for half in range(2):
            halves[half, :, n * width : (n + 1) * width] = weight[:, half * width : (half + 1) * width].astype(LOW)


def row_halves(halves, weight):
    rows = weight.shape[0] // 2
    for half in range(2):
        halves[half] = weight[half * rows : (half + 1) * rows].astype(LOW)


def turned_halves(halves, weight):
    rows = weight.shape[0] // 2
    for half in range(2):
        halves[half] = weight[half * rows : (half + 1) * rows].T.astype(LOW)


def fill_mask(mask, infos, turned):
    @pl.loop(0, 2)
    def _(side):
        across = infos[side].astype(F32)
        down = across.T
        seg_row, pos_row, seg_col, pos_col = down[:, 0:1], down[:, 1:2], across[0:1], across[1:2]
        if turned:
            seg_q, pos_q, seg_k, pos_k = seg_col, pos_col, seg_row, pos_row
        else:
            seg_q, pos_q, seg_k, pos_k = seg_row, pos_row, seg_col, pos_col
        allowed = (pos_k <= pos_q) & ((seg_k == seg_q) | (seg_k == 0.0))
        mask[side] = jnp.where(allowed, 0.0, NEGATIVE).astype(LOW)


def heads_of(width):
    return [slice(n * HEAD_DIM, (n + 1) * HEAD_DIM) for n in range(width // HEAD_DIM)]


def attend(queries, keys, values, mask, attended, between):
    group = mask.shape[1]
    part = group // 2
    for side in range(2):
        for head in heads_of(queries.shape[1]):
            all_rows = pl.ds(side * group, group)

            @pl.loop(0, 2)
            def _(r):
                at = pl.ds(side * group + r * part, part)
                scores = dot(queries[at, head], keys[all_rows, head], NT) * (HEAD_DIM**-0.5)
                scores = scores + mask[side, pl.ds(r * part, part)].astype(F32)
                terms = jnp.exp(scores - jnp.max(scores, axis=1, keepdims=True))
                probs = (terms / jnp.sum(terms, axis=1, keepdims=True)).astype(LOW)
                attended[at, head] = dot(probs, values[all_rows, head], NN).astype(LOW)

            between()


def attend_back(queries, keys, values, grads, mask, grad_qkv, between):
    group, width = mask.shape[1], queries.shape[1]
    part = group // 2
    scale = HEAD_DIM**-0.5
    for side in range(2):
        for n, head in enumerate(heads_of(width)):
            rows = pl.ds(side * group, group)
            grad_key, grad_value = 0.0, 0.0
            for r in range(2):
                at = pl.ds(side * group + r * part, part)
                scores = dot(keys[rows, head], queries[at, head], NT) * scale
                scores = scores + mask[side, :, r * part : (r + 1) * part].astype(F32)
                terms = jnp.exp(scores - jnp.max(scores, axis=0, keepdims=True))
                probs = terms / jnp.sum(terms, axis=0, keepdims=True)
                grad_probs = dot(values[rows, head], grads[at, head], NT)
                delta = jnp.sum(probs * grad_probs, axis=0, keepdims=True)
                grad_scores = (probs * (grad_probs - delta)).astype(LOW)
                grad_value = grad_value + dot(probs.astype(LOW), grads[at, head], NN)
                grad_key = grad_key + dot(grad_scores, queries[at, head], NN)
                grad_query = dot(grad_scores, keys[rows, head], TN)
                grad_qkv[at, n * HEAD_DIM : (n + 1) * HEAD_DIM] = (grad_query * scale).astype(LOW)
            for m, value in ((1, grad_key * scale), (2, grad_value)):
                grad_qkv[rows, m * width + n * HEAD_DIM : m * width + (n + 1) * HEAD_DIM] = value.astype(LOW)
            between()


def column_blocks_of(width, size=256):
    return lambda n: pl.ds(pl.multiple_of(n * size, size), size)


def half_of(ref, side):
    width = ref.shape[1] // 2
    return ref[:, pl.ds(pl.multiple_of(side * width, width), width)]


def front_kernel(
    dp_total, x, gain1, shift1, grad, query, key, value, out, up, down, query_bias, value_bias, seg, pos,
    out_bias, gain2, shift2, up_bias,
    whole1_out, whole2_out, qkv_out, o_out, up_out, down_out, active_out, grad_pre_out, grad_down_out,
    queries, keys, values, attended, infos, resid,
    own1, own2, own_grad, whole1, whole2, whole_grad, qkv_half, out_half, up_half, down_half,
    qkv_whole, o_whole, up_whole, down_whole, mask, parts, active, slope, grad_down, *scratch,
):
    me = Place(dp_total)
    at, cut, block = pieces(x.shape[0]), Cut(scratch), column_blocks_of(x.shape[1])
    gather1, gather2 = Gather(me, own1, whole1, *cut.take(3)), Gather(me, own2, whole2, *cut.take(3))
    gather_grad = Gather(me, own_grad, whole_grad, *cut.take(3))
    first, second = WeightGather(me, qkv_half, qkv_whole, *cut.take(5)), WeightGather(me, out_half, o_whole, *cut.take(5))
    third, fourth = WeightGather(me, up_half, up_whole, *cut.take(5)), WeightGather(me, down_half, down_whole, *cut.take(5))
    scatter = Scatter(me, parts, *cut.take(6))
    (save,) = cut.take(1)
    saved = []

    def store(source, target):
        saved.append(pltpu.make_async_copy(source, target, save.at[2 + len(saved)]))
        saved[-1].start()

    infos[0] = jnp.zeros(infos.shape[1:], jnp.int32)
    infos[0, 0:1], infos[0, 1:2] = seg[...], pos[...]
    me.greet()
    info_copy = remote(infos.at[0], infos.at[1], save.at[0], save.at[1], me.z)
    info_copy.start()

    @pl.loop(0, NC)
    def _(j):
        unit_rows, _ = unit_of(x[at(j)])
        own1[at(j)] = (unit_rows * gain1[...] + shift1[...]).astype(LOW)
        gather1.start(j)

    column_halves(qkv_half, query, key, value)
    for p in range(NW):
        first.start(p)
    turned_halves(out_half, out)
    for p in range(NW):
        second.start(p)
    column_halves(up_half, up)
    third.start(0)
    third.start(1)
    row_halves(down_half, down)

    @pl.loop(0, NC)
    def _(j):
        own_grad[at(j)] = grad[at(j)].astype(LOW)

    info_copy.wait()
    fill_mask(mask, infos, False)
    gather1.relay()
    first.forward(0)

    @pl.loop(0, NC)
    def _(j):
        gather_grad.start(j)

    gather1.finish()
    store(whole1, whole1_out)
    first.forward(1)
    first.finish()
    store(qkv_whole, qkv_out)
    group = mask.shape[1]
    width = queries.shape[1]

    @pl.loop(0, 2)
    def _(side):
        rows = pl.ds(pl.multiple_of(side * group, group), group)
        tokens = whole1[side].reshape(group, -1)
        for n, (result, bias) in enumerate(((queries, query_bias), (keys, None), (values, value_bias))):
            total = dot(tokens, qkv_whole[:, n * width : (n + 1) * width], NN)
            result[rows] = (total if bias is None else total + half_of(bias, me.side)).astype(LOW)

    for p in range(NW):
        second.forward(p)
    steps = iter((None, None, lambda: third.forward(0), lambda: third.start(2)))

    def between():
        step = next(steps, None)
        if step:
            step()

    attend(queries, keys, values, mask, attended, between)
    second.finish()
    store(o_whole, o_out)

    @pl.loop(0, x.shape[1] // 256)
    def _(n):
        total = dot(attended[...], o_whole[pl.ds(pl.multiple_of(n * 256, 256), 256)], NT)
        parts[:, :, :, block(n)] = total.astype(LOW).reshape(*parts.shape[:3], 256)

    scatter.start()
    third.forward(1)
    scatter.spread()
    scatter.turn()
    third.start(3)
    third.forward(2)

    @pl.loop(0, NC)
    def _(j):
        rows = x[at(j)] + scatter.result(j) + out_bias[...]
        resid[at(j)] = rows
        unit_rows, _ = unit_of(rows)
        own2[at(j)] = (unit_rows * gain2[...] + shift2[...]).astype(LOW)
        gather2.start(j)

    fourth.start(0)
    fourth.start(1)
    fourth.start(2)
    fourth.start(3)
    third.forward(3)
    gather2.relay()
    gather_grad.relay()
    fourth.forward(0)
    gather2.finish()
    store(whole2, whole2_out)
    third.finish()
    store(up_whole, up_out)

    def activate(first_block, last_block):
        @pl.loop(first_block, last_block)
        def _(n):
            bias = up_bias[:, pl.ds(pl.multiple_of(me.side * active.shape[1] + n * 256, 256), 256)]

            @pl.loop(0, 2)
            def _(side):
                rows = pl.ds(pl.multiple_of(side * group, group), group)
                pre_act = dot(whole2[side].reshape(group, -1), up_whole[:, block(n)], NN) + bias
                cumulative, rise = gelu_parts(pre_act)
                active[rows, block(n)] = (pre_act * cumulative).astype(LOW)
                slope[rows, block(n)] = rise.astype(LOW)

    hidden_blocks = active.shape[1] // 256
    activate(0, hidden_blocks // 2)
    fourth.forward(1)
    activate(hidden_blocks // 2, hidden_blocks)
    store(active, active_out)
    gather_grad.finish()
    fourth.forward(2)

    @pl.loop(0, hidden_blocks)
    def _(n):
        total = dot(active[:, block(n)], whole_grad[...].reshape(active.shape[0], -1), TN)
        grad_down[pl.ds(pl.multiple_of(n * 256, 256), 256)] = total.astype(LOW)

    store(grad_down, grad_down_out)

    def lower(p):
        fourth.arrive(p)
        units = pl.ds(p * fourth.count, fourth.count)
        if len(down_whole.shape) == 2:
            store(down_whole.at[units], down_out.at[units])
            total = dot(whole_grad[...].reshape(slope.shape[0], -1), down_whole[units], NT)
        else:
            store(down_whole.at[:, units], down_out.at[:, units])
            owners = 128 // fourth.width

            def add(n, total):
                columns = pl.ds(pl.multiple_of(n * 128, 128), 128)
                weights = jnp.concatenate([down_whole[n * owners + i, units] for i in range(owners)], axis=1)
                return total + dot(whole_grad[:, :, :, columns].reshape(slope.shape[0], -1), weights, NT)

            total = lax.fori_loop(
                0, down_whole.shape[0] // owners, add, jnp.zeros((slope.shape[0], fourth.count), F32)
            )
        slope[:, units] = (total * slope[:, units].astype(F32)).astype(LOW)
        store(slope.at[:, units], grad_pre_out.at[:, units])

    lower(0)
    lower(1)
    fourth.forward(3)
    lower(2)
    lower(3)
    scatter.finish()
    for copy in saved:
        copy.wait()


def back_kernel(
    dp_total, down, whole2, whole1, grad_pre_in, active, up_whole, down_whole, resid, grad, gain2, down_bias, o_whole,
    queries, keys, values, attended, infos, x, gain1, qkv_whole,
    down_hops, up_hops, out_hops, qkv_hops, lowered, output, grad_inputs, sums,
    own, tokens, whole, mask, grad_att, grad_up, shared, grad_out, qkv, *scratch,
):
    me = Place(dp_total)
    at, cut, block = pieces(x.shape[0]), Cut(scratch), column_blocks_of(x.shape[1])
    scatter, other = Scatter(me, tokens, *cut.take(6)), Scatter(me, lowered, *cut.take(8))
    last, gather = Scatter(me, whole, *cut.take(6)), Gather(me, own, whole, *cut.take(3))
    first = WeightScatter(me, down, down_hops, *cut.take(8))
    second = WeightScatter(me, grad_up, up_hops, *cut.take(6))
    third = WeightScatter(me, grad_out, out_hops, *cut.take(6))
    fourth = WeightScatter(me, qkv, qkv_hops, *cut.take(6))
    vectors = SumAll(me, *cut.take(4))
    load, tiles = cut.take(2)
    start = vectors.held.at[0]
    lines, hidden, head_width = me.lines, grad_up.shape[1], queries.shape[1]
    grad_pre, grad_qkv = shared.at[:, :hidden], shared.at[:, : 3 * head_width]
    load1, load2, load3, load4 = (
        pltpu.make_async_copy(source, target, load.at[n])
        for n, (source, target) in enumerate(
            ((whole1, tokens), (whole2, tokens), (grad_pre_in, grad_pre), (up_whole, grad_up))
        )
    )
    load3.start()
    load4.start()
    me.greet()
    first.start()
    load3.wait()
    load4.wait()

    def norm_parts(i):
        rows = scatter.pair_rows(i)

        @pl.loop(0, x.shape[1] // 256)
        def _(n):
            weights = grad_up[pl.ds(pl.multiple_of(n * 256, 256), 256)]
            tokens[rows, block(n)] = dot(grad_pre[rows], weights, NT).astype(LOW)

        scatter.start((i,))

    norm_parts(3)
    norm_parts(1)
    scatter.spread(((0, 3),))
    norm_parts(2)
    scatter.spread(((1, 1),))
    norm_parts(0)

    scatter.turn()
    first.spread(1, lines // 2)
    start[...] = jnp.zeros_like(start)

    @pl.loop(0, hidden // 256)
    def _(n):
        columns = pl.ds(pl.multiple_of(me.side * hidden + n * 256, 256), 256)
        start[6:7, columns] = jnp.sum(grad_pre[:, block(n)].astype(F32), axis=0, keepdims=True)

    @pl.loop(0, NC)
    def _(j):
        unit_rows, inverse = unit_of(resid[at(j)])
        e = scatter.result(j)
        rows = grad[at(j)] + back_of(e, unit_rows, inverse, gain2[...])
        grad_inputs[at(j)] = rows
        own[at(j)] = rows.astype(LOW)
        gather.start(j)
        start[2:3] += jnp.sum(e * unit_rows, axis=0, keepdims=True)
        start[3:4] += jnp.sum(e, axis=0, keepdims=True)
        start[4:5] += jnp.sum(rows, axis=0, keepdims=True)
        start[5:6] += jnp.sum(grad[at(j)], axis=0, keepdims=True)

    scatter.finish()
    load2.start()
    fill_mask(mask, infos, True)
    first.spread(lines // 2, lines - 1)
    load2.wait()

    @pl.loop(0, grad_up.shape[0] // 256)
    def _(n):
        total = dot(tokens[:, block(n)], grad_pre[...], TN)
        grad_up[pl.ds(pl.multiple_of(n * 256, 256), 256)] = total.astype(LOW)

    second.start()
    load1.start()
    first.spread(lines - 1, lines)
    gather.relay()
    gather.finish()
    mixed = whole[...].reshape(-1, whole.shape[3])
    grad_att[...] = dot(mixed, o_whole[...], NN).astype(LOW)
    steps = iter((None, lambda: second.spread(1, lines // 2), None, lambda: first.own()))

    def between():
        step = next(steps, None)
        if step:
            step()

    attend_back(queries, keys, values, grad_att, mask, grad_qkv, between)

    for n in (0, 2):
        total = jnp.sum(grad_qkv[:, n * head_width : (n + 1) * head_width].astype(F32), axis=0, keepdims=True)
        start[7:8, pl.ds(pl.multiple_of((n + me.side) * head_width, head_width), head_width)] = total

    load1.wait()

    @pl.loop(0, qkv.shape[0] // 256)
    def _(n):
        qkv[pl.ds(pl.multiple_of(n * 256, 256), 256)] = dot(tokens[:, block(n)], grad_qkv[...], TN).astype(LOW)

    fourth.start()
    second.spread(lines // 2, lines - 1)
    wide = third.width

    @pl.loop(0, x.shape[1] // 256)
    def _(n):
        columns = whole[:, :, :, block(n)].reshape(-1, 256)
        total = dot(attended[...], columns, TN).astype(LOW)
        if wide % 128:
            for i in range(256 // wide):
                grad_out[n * (256 // wide) + i] = total[:, i * wide : (i + 1) * wide]
        else:
            grad_out[:, block(n)] = total

    third.start()

    @pl.loop(0, x.shape[1] // 256)
    def _(n):
        total = dot(grad_qkv[...], qkv_whole[pl.ds(pl.multiple_of(n * 256, 256), 256)], NT)
        whole[:, :, :, block(n)] = total.astype(LOW).reshape(*whole.shape[:3], 256)

    last.start()
    second.spread(lines - 1, lines)
    last.spread()

    held = tokens.at[:, :hidden]
    load_active = pltpu.make_async_copy(active, held, tiles.at[0])
    load_active.start()

    def tile_at(b):
        return tokens.at[:hidden, hidden + b * 256 : hidden + (b + 1) * 256]

    def result_at(b):
        return tokens.at[:, hidden + (2 + b) * 256 : hidden + (3 + b) * 256]

    def load_tile(n, b):
        return pltpu.make_async_copy(down_whole.at[:, block(n)], tile_at(b), tiles.at[1 + b])

    def save_tile(n, b):
        return pltpu.make_async_copy(result_at(b), lowered.at[:, block(n)], tiles.at[3 + b])

    load_tile(0, 0).start()
    load_tile(1, 1).start()
    load_active.wait()
    tile_total = x.shape[1] // 256

    @pl.loop(0, tile_total // 2)
    def _(m):
        for b in range(2):
            n = 2 * m + b
            load_tile(n, b).wait()

            @pl.when(m > 0)
            def _():
                save_tile(n, b).wait()

            result_at(b)[...] = dot(held[...], tile_at(b)[...], NN).astype(LOW)
            save_tile(n, b).start()

            @pl.when(m < tile_total // 2 - 1)
            def _():
                load_tile(n + 2, b).start()

    for b in range(2):
        save_tile(tile_total - 2 + b, b).wait()
    other.start()
    last.turn()
    second.own()
    other.spread()
    fourth.spread(1, lines // 2)
    fourth.spread(lines // 2, lines - 1)

    @pl.loop(0, NC)
    def _(j):
        unit_rows, inverse = unit_of(x[at(j)])
        e = last.result(j)
        grad_inputs[at(j)] += back_of(e, unit_rows, inverse, gain1[...])
        start[0:1] += jnp.sum(e * unit_rows, axis=0, keepdims=True)
        start[1:2] += jnp.sum(e, axis=0, keepdims=True)

    other.turn()
    vectors.run(0, 2, 6)
    fourth.spread(lines - 1, lines)
    fourth.own()
    third.spread(1, lines)
    third.own()

    @pl.loop(0, NC)
    def _(j):
        output[at(j)] = resid[at(j)] + other.result(j) + down_bias[...]

    sums[...] = vectors.run(2, None, 6)
    for part in (other, last, first, second, third, fourth):
        part.finish()


def final_kernel(
    lines, down_hops, up_hops, out_hops, qkv_hops, rows_in, grads_in, sums,
    output, grad_inputs, down, up, out, query, key, value, *vectors,
):
    side = lax.rem(lax.div(lax.axis_index("dp"), 2), 2)

    def half_sums(hops):
        same, opposite = hops[0].astype(F32), hops[1].astype(F32)
        for k in range(2, lines):
            if k % 2:
                opposite = opposite + hops[k].astype(F32)
            else:
                same = same + hops[k].astype(F32)
        return (side, same), (1 - side, opposite)

    for half, total in half_sums(down_hops):
        down[half] = total
    for half, total in half_sums(out_hops):
        out[half] = total
    for half, total in half_sums(up_hops):
        width = total.shape[1]
        up[:, pl.ds(pl.multiple_of(half * width, width), width)] = total
    for half, total in half_sums(qkv_hops):
        width = total.shape[1] // 3
        for n, ref in enumerate((query, key, value)):
            ref[:, pl.ds(pl.multiple_of(half * width, width), width)] = total[:, n * width : (n + 1) * width]
    output[...], grad_inputs[...] = rows_in[...], grads_in[...]
    first = 0
    for n, ref in enumerate(vectors):
        if n < 7:
            ref[...] = sums[n : n + 1, : ref.shape[1]]
        else:
            ref[...] = sums[7:8, first : first + ref.shape[1]]
            first += ref.shape[1]


VMEM = pl.BlockSpec(memory_space=pltpu.VMEM)
ANY = pl.BlockSpec(memory_space=pl.ANY)


def call(kernel, number, ins, in_specs, outs, out_specs, scratch, limit=60):
    return pl.pallas_call(
        functools.partial(kernel, lax.axis_size("dp")),
        out_shape=outs,
        in_specs=in_specs,
        out_specs=out_specs,
        scratch_shapes=scratch,
        compiler_params=pltpu.CompilerParams(
            collective_id=number, has_side_effects=True, vmem_limit_bytes=limit << 20
        ),
        cost_estimate=pl.CostEstimate(flops=0, bytes_accessed=100_000_000, transcendentals=0),
    )(*ins)


def like(*shape, dtype=F32):
    return jax.ShapeDtypeStruct(shape, dtype)


def local(
    inputs,
    grad_output,
    seg_ids,
    positions,
    norm1_gain,
    norm1_bias,
    query_weight,
    query_bias,
    key_weight,
    value_weight,
    value_bias,
    out_weight,
    out_bias,
    norm2_gain,
    norm2_bias,
    up_weight,
    up_bias,
    down_weight,
    down_bias,
):
    dp_total = lax.axis_size("dp")
    tensor_total = lax.axis_size("tensor")
    lines = dp_total // 2
    place = lax.axis_index("dp")
    side = (place >> 1) & 1

    rows, width = inputs.shape
    row = lambda vector: vector.reshape(1, -1)
    group = like(2, tensor_total, rows, width, dtype=LOW)
    own = pltpu.VMEM((rows, width), LOW)
    token_scratch = Scatter.scratch(rows, width)

    slab = lambda *shape: pltpu.VMEM(shape, LOW)
    head_width, hidden = query_weight.shape[1] // 2, up_weight.shape[1] // 2
    high, wide = up_weight.shape[0], down_weight.shape[1]
    tokens = 2 * tensor_total * rows

    def side_by_side(whole):
        return whole if whole.ndim == 2 else whole.transpose(1, 0, 2).reshape(whole.shape[1], -1)

    def column_blocks(partial):
        return partial.reshape(-1, dp_total, wide).transpose(1, 0, 2) if wide % 128 else partial

    down_shape = (dp_total, hidden, wide) if wide % 128 else (hidden, width)
    heads = like(tokens, head_width, dtype=LOW)
    units = like(tokens, hidden, dtype=LOW)

    (
        whole1, whole2, qkv_full, o_full, up_full, down_full, activated, grad_pre, grad_down,
        queries, keys, values, attended, infos, resid,
    ) = call(
        front_kernel, 1,
        (
            inputs, row(norm1_gain), row(norm1_bias), grad_output, query_weight, key_weight, value_weight, out_weight,
            up_weight, down_weight, row(query_bias), row(value_bias), row(seg_ids), row(positions),
            row(out_bias), row(norm2_gain), row(norm2_bias), row(up_bias),
        ),
        [VMEM] * 18,
        (
            group, group, like(width, 3 * head_width, dtype=LOW), like(width, head_width, dtype=LOW),
            like(width, hidden, dtype=LOW), like(*down_shape, dtype=LOW),
            units, units, like(hidden, width, dtype=LOW),
            heads, heads, heads, heads, like(2, 8, GROUP, dtype=jnp.int32), like(rows, width),
        ),
        (ANY,) * 9 + (VMEM,) * 6,
        [
            own, own, own, *[slab(*group.shape)] * 3,
            slab(2, high, 3 * head_width), slab(2, wide, head_width), slab(2, high, hidden), slab(2, hidden, wide),
            slab(width, 3 * head_width), slab(width, head_width), slab(width, hidden), slab(*down_shape),
            slab(2, GROUP, GROUP), slab(*group.shape), slab(tokens, hidden), slab(tokens, hidden), slab(hidden, width),
        ]
        + Gather.SEMS * 3
        + WeightGather.sems(lines, NW) * 2 + WeightGather.sems(lines, NF) * 2
        + Scatter.scratch(rows, width, False) + [grid_of(9 + 2 * NF)],
        63,
    )
    down_full, grad_down = side_by_side(down_full), column_blocks(grad_down)
    hops = [
        like(lines, *shape, dtype=LOW)
        for shape in ((hidden, wide), (high, hidden), (head_width, wide), (high, 3 * head_width))
    ]
    *hops, _, layer_output, grad_inputs, sums = call(
        back_kernel, 2,
        (
            grad_down, whole2.reshape(-1, width), whole1.reshape(-1, width), grad_pre, activated, up_full, down_full,
            resid, grad_output, row(norm2_gain), row(down_bias), o_full, queries, keys, values, attended, infos, inputs, row(norm1_gain), qkv_full,
        ),
        [ANY] * 7 + [VMEM] * 13,
        (*hops, like(tokens, width, dtype=LOW), like(rows, width), like(rows, width), like(8, width)),
        (ANY,) * 5 + (VMEM,) * 3,
        [
            own, slab(tokens, width), slab(*group.shape), slab(2, GROUP, GROUP), slab(tokens, head_width),
            slab(width, hidden), slab(tokens, max(hidden, 3 * head_width)),
            slab(*((dp_total, head_width, wide) if wide % 128 else (head_width, width))), slab(width, 3 * head_width),
        ]
        + Scatter.scratch(rows, width, False) + Scatter.scratch(rows, width) + Scatter.scratch(rows, width, False)
        + Gather.SEMS
        + WeightScatter.scratch(lines, hidden, wide, True) + WeightScatter.scratch(lines, high, hidden)
        + WeightScatter.scratch(lines, head_width, wide) + WeightScatter.scratch(lines, high, 3 * head_width)
        + SumAll.scratch(dp_total, width) + [grid_of(4), grid_of(5)],
        63,
    )
    cuts = 4

    def cut_at(dim, *shape):
        block = tuple(n // cuts if i == dim else n for i, n in enumerate(shape))
        return pl.BlockSpec(block, lambda g: tuple(g if i == dim else 0 for i in range(len(shape))))

    up_total, bias_total = up_bias.shape[0], query_bias.shape[0]
    lengths = [width] * 6 + [up_total, bias_total, bias_total]
    results = pl.pallas_call(
        functools.partial(final_kernel, lines),
        grid=(cuts,),
        out_shape=(
            like(rows, width), like(rows, width), like(2, hidden, wide), like(high, 2 * hidden), like(2, head_width, wide),
            *[like(high, 2 * head_width)] * 3, *[like(1, n) for n in lengths],
        ),
        in_specs=[
            cut_at(1, lines, hidden, wide), cut_at(1, lines, high, hidden), cut_at(1, lines, head_width, wide),
            cut_at(1, lines, high, 3 * head_width), cut_at(0, rows, width), cut_at(0, rows, width), cut_at(None, 8, width),
        ],
        out_specs=(
            cut_at(0, rows, width), cut_at(0, rows, width), cut_at(1, 2, hidden, wide), cut_at(0, high, 2 * hidden),
            cut_at(1, 2, head_width, wide), *[cut_at(0, high, 2 * head_width)] * 3, *[cut_at(None, 1, n) for n in lengths],
        ),
        compiler_params=pltpu.CompilerParams(vmem_limit_bytes=63 << 20),
    )(*hops, layer_output, grad_inputs, sums)
    layer_output, grad_inputs, down_done, up_done, out_done, query_done, key_done, value_done = results[:8]
    sums = [vector.reshape(-1) for vector in results[8:]]
    return (
        layer_output,
        grad_inputs,
        sums[0],
        sums[1],
        query_done,
        sums[7],
        key_done,
        value_done,
        sums[8],
        out_done.reshape(-1, wide),
        sums[4],
        sums[2],
        sums[3],
        up_done,
        sums[6],
        down_done.reshape(-1, wide),
        sums[5],
    )


def solution(mesh):
    tokens, weight, weight_t = P(("dp", "tensor"), None), P("dp", "tensor"), P("tensor", "dp")
    whole, part = P(), P("tensor")
    return jax.shard_map(
        local,
        mesh=mesh,
        in_specs=(
            tokens, tokens, P("dp"), P("dp"), whole, whole, weight, part, weight, weight, part,
            weight_t, whole, whole, whole, weight, part, weight_t, whole,
        ),
        out_specs=(
            tokens, tokens, whole, whole, weight, part, weight, weight, part, weight_t, whole,
            whole, whole, weight, part, weight_t, whole,
        ),
        check_vma=False,
    )
```
